32 devices in a mesh: dp: 4 (over x, core), fsdp: 8 (over z, y).
Axes of the slice: x: 2, y: 2, z: 4, core: 2. Of those that a mesh axis runs over, the one named last changes fastest.
Arguments:
- tokens: bfloat16 [32, 512, 1024], P(('dp', 'fsdp')), may hold values from -6 to 6
- ln1_gain: bfloat16 [1024], P(('dp', 'fsdp')), may hold values from 0.5 to 1.5
- ln1_bias: bfloat16 [1024], P(('dp', 'fsdp')), may hold values from -1.796875 to 1.796875
- w_qkv: bfloat16 [1024, 3072], P(('dp', 'fsdp')), may hold values from -0.1875 to 0.1875
- bias_q: bfloat16 [1024], P(('dp', 'fsdp')), may hold values from -3 to 3
- bias_v: bfloat16 [1024], P(('dp', 'fsdp')), may hold values from -3 to 3
- w_out: bfloat16 [1024, 1024], P(('dp', 'fsdp')), may hold values from -1 to 1
- bias_out: bfloat16 [1024], P(('dp', 'fsdp')), may hold values from -1.796875 to 1.796875
- ln2_gain: bfloat16 [1024], P(('dp', 'fsdp')), may hold values from 0.5 to 1.5
- ln2_bias: bfloat16 [1024], P(('dp', 'fsdp')), may hold values from -1.796875 to 1.796875
- w_up: bfloat16 [1024, 4096], P(('dp', 'fsdp')), may hold values from -0.1875 to 0.1875
- bias_up: bfloat16 [4096], P(('dp', 'fsdp')), may hold values from -1.796875 to 1.796875
- w_down: bfloat16 [4096, 1024], P(('dp', 'fsdp')), may hold values from -0.09375 to 0.09375
- bias_down: bfloat16 [1024], P(('dp', 'fsdp')), may hold values from -1.796875 to 1.796875
- cot_first: bfloat16 [32, 512, 1024], P(('dp', 'fsdp')), may hold values from -6 to 6
- cot_second: bfloat16 [32, 512, 1024], P(('dp', 'fsdp')), may hold values from -6 to 6
- valid: int32 [32, 512], P(('dp', 'fsdp')), may hold values from 0 to 1, as said below
Outputs:
- out_first: bfloat16 [32, 512, 1024], P(('dp', 'fsdp'))
- out_second: bfloat16 [32, 512, 1024], P(('dp', 'fsdp'))
- grad_tokens: bfloat16 [32, 512, 1024], P(('dp', 'fsdp'))
- grad_ln1_gain: float32 [1024], P(('dp', 'fsdp'))
- grad_ln1_bias: float32 [1024], P(('dp', 'fsdp'))
- grad_w_qkv: float32 [1024, 3072], P(('dp', 'fsdp'))
- grad_bias_q: float32 [1024], P(('dp', 'fsdp'))
- grad_bias_v: float32 [1024], P(('dp', 'fsdp'))
- grad_w_out: float32 [1024, 1024], P(('dp', 'fsdp'))
- grad_bias_out: float32 [1024], P(('dp', 'fsdp'))
- grad_ln2_gain: float32 [1024], P(('dp', 'fsdp'))
- grad_ln2_bias: float32 [1024], P(('dp', 'fsdp'))
- grad_w_up: float32 [1024, 4096], P(('dp', 'fsdp'))
- grad_bias_up: float32 [4096], P(('dp', 'fsdp'))
- grad_w_down: float32 [4096, 1024], P(('dp', 'fsdp'))
- grad_bias_down: float32 [1024], P(('dp', 'fsdp'))
The draws below stay inside these ranges and needn't reach their ends.
Inputs may be any that keep to these rules, and one draw needn't show every extreme that they name: `valid`: the share of present cells differs from sample to sample.
All inputs are finite; a program needn't handle non-finite values.
Results may differ from the reference program's by a relative error of at most 0.02.
Values may be sent and summed in bfloat16 or wider, within the bound.
No kernel may reach another device: no remote copies, remote signals or barrier semaphores. Data moves between devices by JAX's collectives and lax.ppermute only.
A program may use at most 152 MiB of HBM per device.

```python
import jax
import jax.numpy as jnp
from jax import lax

D = 1024
FF = 4096
HEAD_DIM = 64
SEQ = 512
SAMPLES = 32


def draw_valid(key, part):
    key_rate = jax.random.fold_in(key, 11)
    key_roll = jax.random.fold_in(key, 23)
    rate_tenths = jax.random.randint(key_rate, (SAMPLES, 1), 3, 10)
    roll_tenths = jax.random.randint(key_roll, (SAMPLES, SEQ), 0, 10)
    return (roll_tenths < rate_tenths).astype(jnp.int32)


def level_of(rng, dims, shards, smallest, top_value):
    factor_of = 1.0
    for position, blocks in shards:
        steps = jax.random.uniform(jax.random.fold_in(jax.random.fold_in(rng, 6), position), (blocks,), jnp.float32, smallest / len(shards), top_value / len(shards))
        factor_of = factor_of * jnp.repeat(jnp.exp(steps), dims[position] // blocks).reshape((-1,) + (1,) * (len(dims) - 1 - position))
    return factor_of


def gaussian(own_key, shape, scale, bound, shards=(), held_as=jnp.bfloat16):
    level = level_of(own_key, shape, shards, -0.22, 0.18) if shards else 1.0
    result = jax.random.normal(own_key, shape, jnp.float32) * scale * level
    return jnp.minimum(jnp.maximum(result, -bound), bound).astype(held_as)


def setup_inputs(seed: int = 0) -> dict:
    keys = jax.random.split(jax.random.key(seed), 18)
    return {
        "tokens": gaussian(keys[0], (SAMPLES, SEQ, D), 1.0, 6.0, ((0, 32),)),
        "ln1_gain": jnp.clip(1.0 + 0.1 * jax.random.normal(keys[1], (D,), jnp.float32), 0.5, 1.5).astype(jnp.bfloat16),
        "ln1_bias": gaussian(keys[2], (D,), 0.3, 1.796875, ((0, 32),)),
        "w_qkv": gaussian(keys[3], (D, 3 * D), D ** -0.5, 0.1875, ((0, 32),)),
        "bias_q": gaussian(keys[4], (D,), 0.5, 3.0, ((0, 32),)),
        "bias_v": gaussian(keys[5], (D,), 0.5, 3.0, ((0, 32),)),
        "w_out": gaussian(keys[6], (D, D), (max(D // 32, 1)) ** -0.5, 1.0, ((0, 32),)),
        "bias_out": gaussian(keys[7], (D,), 0.3, 1.796875, ((0, 32),)),
        "ln2_gain": jnp.clip(1.0 + 0.1 * jax.random.normal(keys[8], (D,), jnp.float32), 0.5, 1.5).astype(jnp.bfloat16),
        "ln2_bias": gaussian(keys[9], (D,), 0.3, 1.796875, ((0, 32),)),
        "w_up": gaussian(keys[10], (D, FF), D ** -0.5, 0.1875, ((0, 32),)),
        "bias_up": gaussian(keys[11], (FF,), 0.3, 1.796875, ((0, 32),)),
        "w_down": gaussian(keys[12], (FF, D), FF ** -0.5, 0.09375, ((0, 32),)),
        "bias_down": gaussian(keys[13], (D,), 0.3, 1.796875, ((0, 32),)),
        "cot_first": gaussian(keys[14], (SAMPLES, SEQ, D), 1.0, 6.0, ((0, 32),)),
        "cot_second": gaussian(keys[15], (SAMPLES, SEQ, D), 1.0, 6.0, ((0, 32),)),
        "valid": draw_valid(jax.random.fold_in(keys[17], 71), 0),
    }


@jax.custom_vjp
def low(v):
    return lax.optimization_barrier(v.astype(jnp.bfloat16)).astype(jnp.float32)

@jax.custom_vjp
def low_back(v):
    return v

def low_keep(v):
    return (low(v), None)

def low_pass(kept, grad):
    return (grad,)

def back_keep(v):
    return (v, None)

def back_low(kept, grad):
    return (low(grad),)
low.defvjp(low_keep, low_pass)
low_back.defvjp(back_keep, back_low)
EPSILON = 1e-06

def norm_affine(values, gain_vec, shift_vec):
    centre = values - lax.optimization_barrier(jnp.mean(values, axis=-1, keepdims=True))
    spread = lax.optimization_barrier(jnp.mean(centre * centre, axis=-1, keepdims=True))
    return centre * lax.rsqrt(spread + EPSILON) * gain_vec + shift_vec

def matmul_high(left, right):
    return jnp.dot(left, right, precision=lax.Precision.HIGHEST, preferred_element_type=jnp.float32)

def round_both(values):
    return low(low_back(values))

def layer_apply(inputs, params):
    gain_one, shift_one, weight_qkv, query_bias, value_bias, weight_out, out_bias, gain_two, shift_two, weight_up, up_bias, weight_down, down_bias = params
    length = inputs.shape[0]
    model_width = inputs.shape[1]
    head_count = model_width // HEAD_DIM
    normed = low(norm_affine(inputs, gain_one, shift_one))
    projected = matmul_high(normed, weight_qkv)
    queries = round_both(projected[:, :model_width] + query_bias).reshape(length, head_count, HEAD_DIM)
    keys_all = round_both(projected[:, model_width:2 * model_width]).reshape(length, head_count, HEAD_DIM)
    values_all = round_both(projected[:, 2 * model_width:] + value_bias).reshape(length, head_count, HEAD_DIM)
    scores = low_back(jnp.einsum('qhd,khd->hqk', queries, keys_all, precision=lax.Precision.HIGHEST) * 0.125)
    shifted = jnp.exp(scores - lax.optimization_barrier(jnp.max(scores, axis=-1, keepdims=True)))
    attn_probs = low(shifted / lax.optimization_barrier(jnp.sum(shifted, axis=-1, keepdims=True)))
    mixed_heads = jnp.einsum('hqk,khd->qhd', attn_probs, values_all, precision=lax.Precision.HIGHEST)
    mixed_heads = round_both(mixed_heads.reshape(length, model_width))
    middle = inputs + low_back(matmul_high(mixed_heads, weight_out) + out_bias)
    normed_two = low(norm_affine(middle, gain_two, shift_two))
    hidden = low_back(matmul_high(normed_two, weight_up) + up_bias)
    active = low(jax.nn.gelu(hidden, approximate=False))
    return middle + low_back(matmul_high(active, weight_down) + down_bias)

def two_steps(inputs_all, params):
    checked = jax.checkpoint(layer_apply)

    def per_sample(carry, sample):
        first = low(checked(sample, params))
        second = checked(first, params)
        return (carry, (first, second))
    _, (firsts, seconds) = lax.scan(per_sample, jnp.zeros((), jnp.float32), inputs_all)
    return (firsts, seconds)

def reference(tokens, ln1_gain, ln1_bias, w_qkv, bias_q, bias_v, w_out, bias_out, ln2_gain, ln2_bias, w_up, bias_up, w_down, bias_down, cot_first, cot_second, valid):
    params = tuple((tensor.astype(jnp.float32) for tensor in (ln1_gain, ln1_bias, w_qkv, bias_q, bias_v, w_out, bias_out, ln2_gain, ln2_bias, w_up, bias_up, w_down, bias_down)))
    (firsts, seconds), pullback = jax.vjp(two_steps, tokens.astype(jnp.float32), params)
    keep_mask = valid.astype(jnp.float32)[..., None]
    grad_in, grad_params = pullback((cot_first.astype(jnp.float32) * keep_mask, cot_second.astype(jnp.float32) * keep_mask))
    return (firsts.astype(jnp.bfloat16), seconds.astype(jnp.bfloat16), grad_in.astype(jnp.bfloat16), grad_params[0], grad_params[1], grad_params[2], grad_params[3], grad_params[4], grad_params[5], grad_params[6], grad_params[7], grad_params[8], grad_params[9], grad_params[10], grad_params[11], grad_params[12])
```

```python
from functools import partial

import numpy as np

import jax
import jax.numpy as jnp
from jax import lax
from jax.experimental import pallas as pl
from jax.experimental.pallas import tpu as pltpu
from jax.sharding import PartitionSpec as P

HEAD_DIM = 64


EPSILON = 1e-06


def norm_affine(values, gain_vec, shift_vec):
    centre = values - jnp.mean(values, axis=-1, keepdims=True)
    spread = jnp.mean(centre * centre, axis=-1, keepdims=True)
    return centre * lax.rsqrt(spread + EPSILON) * gain_vec + shift_vec


def exact_gelu(values):
    return jax.nn.gelu(values, approximate=False)


def attend_block(query_blk, keys_all, values_all):
    scores = (
        jnp.einsum("qhd,khd->hqk", query_blk, keys_all, preferred_element_type=jnp.float32) * 0.125
    )
    top_score = jnp.max(scores, axis=-1, keepdims=True)
    shifted = jnp.exp(scores - top_score)
    total = jnp.sum(shifted, axis=-1, keepdims=True)
    attn_probs = (shifted / total).astype(jnp.bfloat16)
    mixed_blk = jnp.einsum(
        "hqk,khd->qhd", attn_probs, values_all, preferred_element_type=jnp.float32
    )
    return (mixed_blk, top_score[..., 0] + jnp.log(total[..., 0]))


def attend_back(carry, block, keys_all, values_all):
    grad_keys, grad_values = carry
    query_blk, grad_mixed, log_total = block
    scores = (
        jnp.einsum("qhd,khd->hqk", query_blk, keys_all, preferred_element_type=jnp.float32) * 0.125
    )
    attn_probs = jnp.exp(scores - log_total[..., None])
    grad_probs = jnp.einsum(
        "qhd,khd->hqk", grad_mixed, values_all, preferred_element_type=jnp.float32
    )
    grad_values = grad_values + jnp.einsum(
        "hqk,qhd->khd",
        attn_probs.astype(jnp.bfloat16),
        grad_mixed,
        preferred_element_type=jnp.float32,
    )
    inner_sum = jnp.sum(attn_probs * grad_probs, axis=-1, keepdims=True)
    grad_scores = (attn_probs * (grad_probs - inner_sum)).astype(jnp.bfloat16)
    grad_queries = (
        jnp.einsum("hqk,khd->qhd", grad_scores, keys_all, preferred_element_type=jnp.float32)
        * 0.125
    )
    grad_keys = (
        grad_keys
        + jnp.einsum("hqk,qhd->khd", grad_scores, query_blk, preferred_element_type=jnp.float32)
        * 0.125
    )
    return ((grad_keys, grad_values), grad_queries)


def forward_pass(inputs, weights):
    (
        gain_one,
        shift_one,
        weight_qkv,
        query_bias,
        value_bias,
        weight_out,
        out_bias,
        gain_two,
        shift_two,
        weight_up,
        up_bias,
        weight_down,
        down_bias,
    ) = weights
    length, model_width = inputs.shape
    head_count = model_width // HEAD_DIM
    block_rows = min(512, length)
    block_count = length // block_rows
    normed = norm_affine(
        inputs, gain_one.astype(jnp.float32), shift_one.astype(jnp.float32)
    ).astype(jnp.bfloat16)
    projected = jnp.dot(normed, weight_qkv, preferred_element_type=jnp.float32)
    queries = (projected[:, :model_width] + query_bias.astype(jnp.float32)).astype(jnp.bfloat16)
    keys_all = projected[:, model_width : 2 * model_width].astype(jnp.bfloat16)
    values_all = (projected[:, 2 * model_width :] + value_bias.astype(jnp.float32)).astype(
        jnp.bfloat16
    )
    queries = queries.reshape(length, head_count, HEAD_DIM)
    keys_all = keys_all.reshape(length, head_count, HEAD_DIM)
    values_all = values_all.reshape(length, head_count, HEAD_DIM)
    query_blocks = queries.reshape(block_count, block_rows, head_count, HEAD_DIM)
    mixed_blocks, log_totals = lax.map(
        partial(attend_block, keys_all=keys_all, values_all=values_all), query_blocks
    )
    mixed_heads = mixed_blocks.reshape(length, model_width).astype(jnp.bfloat16)
    middle = (
        inputs
        + jnp.dot(mixed_heads, weight_out, preferred_element_type=jnp.float32)
        + out_bias.astype(jnp.float32)
    )
    normed_two = norm_affine(
        middle, gain_two.astype(jnp.float32), shift_two.astype(jnp.float32)
    ).astype(jnp.bfloat16)
    hidden = jnp.dot(normed_two, weight_up, preferred_element_type=jnp.float32) + up_bias.astype(
        jnp.float32
    )
    active = exact_gelu(hidden).astype(jnp.bfloat16)
    result = (
        middle
        + jnp.dot(active, weight_down, preferred_element_type=jnp.float32)
        + down_bias.astype(jnp.float32)
    )
    saved = (
        inputs,
        normed,
        queries,
        keys_all,
        values_all,
        log_totals,
        mixed_heads,
        middle,
        normed_two,
        hidden,
        active,
    )
    return (result, saved)


def backward_pass(grad_result, saved, weights):
    (
        gain_one,
        shift_one,
        weight_qkv,
        query_bias,
        value_bias,
        weight_out,
        out_bias,
        gain_two,
        shift_two,
        weight_up,
        up_bias,
        weight_down,
        down_bias,
    ) = weights
    (
        inputs,
        normed,
        queries,
        keys_all,
        values_all,
        log_totals,
        mixed_heads,
        middle,
        normed_two,
        hidden,
        active,
    ) = saved
    length, model_width = inputs.shape
    head_count = model_width // HEAD_DIM
    block_rows = min(512, length)
    block_count = length // block_rows
    grad_down_out = grad_result.astype(jnp.bfloat16)
    grad_w_down = jnp.einsum("sf,sd->fd", active, grad_down_out, preferred_element_type=jnp.float32)
    grad_b_down = jnp.sum(grad_down_out.astype(jnp.float32), axis=0)
    grad_active = jnp.einsum(
        "sd,fd->sf", grad_down_out, weight_down, preferred_element_type=jnp.float32
    )
    _, gelu_pullback = jax.vjp(exact_gelu, hidden)
    grad_hidden = gelu_pullback(grad_active)[0].astype(jnp.bfloat16)
    grad_w_up = jnp.einsum("sd,sf->df", normed_two, grad_hidden, preferred_element_type=jnp.float32)
    grad_b_up = jnp.sum(grad_hidden.astype(jnp.float32), axis=0)
    grad_normed_two = jnp.einsum(
        "sf,df->sd", grad_hidden, weight_up, preferred_element_type=jnp.float32
    )
    _, norm_two_pullback = jax.vjp(
        norm_affine, middle, gain_two.astype(jnp.float32), shift_two.astype(jnp.float32)
    )
    grad_mid_norm, grad_gain_two, grad_shift_two = norm_two_pullback(grad_normed_two)
    grad_middle = grad_result + grad_mid_norm
    grad_att = grad_middle.astype(jnp.bfloat16)
    grad_w_out = jnp.einsum("sd,se->de", mixed_heads, grad_att, preferred_element_type=jnp.float32)
    grad_b_out = jnp.sum(grad_att.astype(jnp.float32), axis=0)
    grad_mixed = jnp.einsum("se,de->sd", grad_att, weight_out, preferred_element_type=jnp.float32)
    grad_mixed = grad_mixed.astype(jnp.bfloat16).reshape(
        block_count, block_rows, head_count, HEAD_DIM
    )
    query_blocks = queries.reshape(block_count, block_rows, head_count, HEAD_DIM)
    zeros_kv = jnp.zeros((length, head_count, HEAD_DIM), jnp.float32)
    (grad_keys, grad_values), grad_queries = lax.scan(
        partial(attend_back, keys_all=keys_all, values_all=values_all),
        (zeros_kv, zeros_kv),
        (query_blocks, grad_mixed, log_totals),
    )
    grad_queries = grad_queries.reshape(length, model_width).astype(jnp.bfloat16)
    grad_keys = grad_keys.reshape(length, model_width).astype(jnp.bfloat16)
    grad_values = grad_values.reshape(length, model_width).astype(jnp.bfloat16)
    grad_proj = jnp.concatenate([grad_queries, grad_keys, grad_values], axis=1)
    grad_w_qkv = jnp.einsum("sd,se->de", normed, grad_proj, preferred_element_type=jnp.float32)
    grad_b_query = jnp.sum(grad_queries.astype(jnp.float32), axis=0)
    grad_b_value = jnp.sum(grad_values.astype(jnp.float32), axis=0)
    grad_normed = jnp.einsum("se,de->sd", grad_proj, weight_qkv, preferred_element_type=jnp.float32)
    _, norm_one_pullback = jax.vjp(
        norm_affine, inputs, gain_one.astype(jnp.float32), shift_one.astype(jnp.float32)
    )
    grad_in_norm, grad_gain_one, grad_shift_one = norm_one_pullback(grad_normed)
    grad_inputs = grad_middle + grad_in_norm
    grads = (
        grad_gain_one,
        grad_shift_one,
        grad_w_qkv,
        grad_b_query,
        grad_b_value,
        grad_w_out,
        grad_b_out,
        grad_gain_two,
        grad_shift_two,
        grad_w_up,
        grad_b_up,
        grad_w_down,
        grad_b_down,
    )
    return (grad_inputs, grads)


def bits_of(ndp, nfs):
    core = nfs
    outer = [nfs << i for i in range(1, ndp.bit_length() - 1)]
    inner = [1 << i for i in range(nfs.bit_length() - 1)]
    return core, outer, inner


def stage_orders(ndp, nfs):
    core, outer, inner = bits_of(ndp, nfs)
    first, second = outer[0], inner[0]
    tail = outer[1:] + inner[1:]
    return core, ([first, second] + tail, [second, first] + tail)


def shard_table(ndp, nfs):
    n = ndp * nfs
    core, orders = stage_orders(ndp, nfs)
    table = np.zeros((n, n), np.int32)
    for me in range(n):
        for p in range(n):
            rel = core if p >= n // 2 else 0
            owner = 1 if (me ^ rel) & core else 0
            for i, mask in enumerate(orders[owner]):
                if p & (n >> (i + 2)):
                    rel ^= mask
            table[me, p] = me ^ rel
    return table


def stage_perms(ndp, nfs):
    n = ndp * nfs
    core, orders = stage_orders(ndp, nfs)
    perms = [[(i, i ^ core) for i in range(n)]]
    for a, b in zip(*orders):
        perms.append([(i, i ^ (b if i & core else a)) for i in range(n)])
    return perms


def place_blocks(pieces, table_row, scatter):
    n = pieces[0].shape[0]

    def body(t_ref, *refs):
        ins, outs, sem = refs[: len(pieces)], refs[len(pieces) : -1], refs[-1]
        copies = []
        for src, dst in zip(ins, outs):
            for i in range(n):
                j = t_ref[i]
                s, d = (i, j) if scatter else (j, i)
                copies.append(pltpu.make_async_copy(src.at[s], dst.at[d], sem))
        for c in copies:
            c.start()
        for c in copies:
            c.wait()

    return pl.pallas_call(
        body,
        out_shape=[jax.ShapeDtypeStruct(p.shape, p.dtype) for p in pieces],
        grid_spec=pltpu.PrefetchScalarGridSpec(
            num_scalar_prefetch=1,
            in_specs=[pl.BlockSpec(memory_space=pl.ANY)] * len(pieces),
            out_specs=[pl.BlockSpec(memory_space=pl.ANY)] * len(pieces),
            scratch_shapes=[pltpu.SemaphoreType.DMA],
        ),
        name="place",
    )(table_row, *pieces)


AXES = ("dp", "fsdp")


def gather_relative(shard, perms):
    cur = shard[None]
    for perm in perms[:0:-1]:
        cur = jnp.concatenate([cur, lax.ppermute(cur, AXES, perm)], axis=0)
    return jnp.concatenate([cur, lax.ppermute(cur, AXES, perms[0])], axis=0)


def reduce_relative(rel, perms, wide=jnp.bfloat16):
    cur = rel
    for i, perm in enumerate(perms):
        half = cur.shape[0] // 2
        got = lax.ppermute(cur[half:], AXES, perm)
        total = cur[:half].astype(jnp.float32) + got.astype(jnp.float32)
        cur = total if i == len(perms) - 1 else total.astype(wide)
    return cur[0]


def per_device(ndp, nfs,
    tokens,
    ln1_gain,
    ln1_bias,
    w_qkv,
    bias_q,
    bias_v,
    w_out,
    bias_out,
    ln2_gain,
    ln2_bias,
    w_up,
    bias_up,
    w_down,
    bias_down,
    cot_first,
    cot_second,
    valid,
):
    n = ndp * nfs
    perms = stage_perms(ndp, nfs)
    me = lax.axis_index("dp") * nfs + lax.axis_index("fsdp")
    row = lax.dynamic_slice(jnp.asarray(shard_table(ndp, nfs)), (me, 0), (1, n))[0]
    vectors = (ln1_gain, ln1_bias, bias_q, bias_v, bias_out, ln2_gain, ln2_bias, bias_down, bias_up)
    sizes = [v.shape[0] for v in vectors]
    width = -(-sum(sizes) // 128) * 128
    packed = jnp.pad(jnp.concatenate(vectors), (0, width - sum(sizes)))[None]
    got_small = gather_relative(packed, perms)
    got_qkv = gather_relative(w_qkv, perms)
    got_out = gather_relative(w_out, perms)
    got_up = gather_relative(w_up, perms)
    got_down = gather_relative(w_down, perms)
    full_small = jnp.zeros_like(got_small).at[row].set(got_small)[:, 0]
    parts = []
    offset = 0
    for size in sizes:
        parts.append(full_small[:, offset : offset + size].reshape(-1))
        offset += size
    g1, s1, bq, bv, bo, g2, s2, bd, bu = parts
    (full_qkv,) = place_blocks([got_qkv], row, True)
    (full_out,) = place_blocks([got_out], row, True)
    (full_up,) = place_blocks([got_up], row, True)
    (full_down,) = place_blocks([got_down], row, True)
    flat = lambda w: w.reshape(-1, w.shape[-1])
    gathered = (
        g1,
        s1,
        flat(full_qkv),
        bq,
        bv,
        flat(full_out),
        bo,
        g2,
        s2,
        flat(full_up),
        bu,
        flat(full_down),
        bd,
    )
    start_rows = tokens[0].astype(jnp.float32)
    first_out, saved_first = forward_pass(start_rows, gathered)
    first_low = first_out.astype(jnp.bfloat16)
    second_in = lax.optimization_barrier(first_low).astype(jnp.float32)
    second_out, saved_second = forward_pass(second_in, gathered)
    keep_mask = valid[0].astype(jnp.float32)[:, None]
    grad_second = cot_second[0].astype(jnp.float32) * keep_mask
    grad_between, grads_second = backward_pass(grad_second, saved_second, gathered)
    grad_first = cot_first[0].astype(jnp.float32) * keep_mask + grad_between
    grad_inputs, grads_first = backward_pass(grad_first, saved_first, gathered)
    totals = tuple((left + right for left, right in zip(grads_first, grads_second)))
    (t_g1, t_s1, t_qkv, t_bq, t_bv, t_out, t_bo, t_g2, t_s2, t_up, t_bu, t_down, t_bd) = totals

    def reduce_matrix(total):
        low = total.astype(jnp.bfloat16).reshape(n, total.shape[0] // n, total.shape[1])
        (rel,) = place_blocks([low], row, False)
        return reduce_relative(rel, perms)

    d_down = reduce_matrix(t_down)
    d_up = reduce_matrix(t_up)
    d_out = reduce_matrix(t_out)
    d_qkv = reduce_matrix(t_qkv)
    small = jnp.concatenate(
        [v.reshape(n, -1) for v in (t_g1, t_s1, t_bq, t_bv, t_bo, t_g2, t_s2, t_bd, t_bu)], axis=1
    )
    small = jnp.pad(small, ((0, 0), (0, width - small.shape[1])))[:, None]
    small = reduce_relative(small[row], perms, jnp.float32)[0]
    outs = []
    offset = 0
    for size in sizes:
        outs.append(small[offset : offset + size])
        offset += size
    o_g1, o_s1, o_bq, o_bv, o_bo, o_g2, o_s2, o_bd, o_bu = outs
    return (
        first_low[None],
        second_out.astype(jnp.bfloat16)[None],
        grad_inputs.astype(jnp.bfloat16)[None],
        o_g1,
        o_s1,
        d_qkv,
        o_bq,
        o_bv,
        d_out,
        o_bo,
        o_g2,
        o_s2,
        d_up,
        o_bu,
        d_down,
        o_bd,
    )


def solution(mesh):
    ndp, nfs = mesh.shape["dp"], mesh.shape["fsdp"]
    return jax.shard_map(
        partial(per_device, ndp, nfs),
        mesh=mesh,
        in_specs=(
            P(("dp", "fsdp"), None, None),
            P(("dp", "fsdp")),
            P(("dp", "fsdp")),
            P(("dp", "fsdp"), None),
            P(("dp", "fsdp")),
            P(("dp", "fsdp")),
            P(("dp", "fsdp"), None),
            P(("dp", "fsdp")),
            P(("dp", "fsdp")),
            P(("dp", "fsdp")),
            P(("dp", "fsdp"), None),
            P(("dp", "fsdp")),
            P(("dp", "fsdp"), None),
            P(("dp", "fsdp")),
            P(("dp", "fsdp"), None, None),
            P(("dp", "fsdp"), None, None),
            P(("dp", "fsdp"), None),
        ),
        out_specs=(
            P(("dp", "fsdp"), None, None),
            P(("dp", "fsdp"), None, None),
            P(("dp", "fsdp"), None, None),
            P(("dp", "fsdp")),
            P(("dp", "fsdp")),
            P(("dp", "fsdp"), None),
            P(("dp", "fsdp")),
            P(("dp", "fsdp")),
            P(("dp", "fsdp"), None),
            P(("dp", "fsdp")),
            P(("dp", "fsdp")),
            P(("dp", "fsdp")),
            P(("dp", "fsdp"), None),
            P(("dp", "fsdp")),
            P(("dp", "fsdp"), None),
            P(("dp", "fsdp")),
        ),
        check_vma=False,
    )
```

```python
from functools import partial

import numpy as np

import jax
import jax.numpy as jnp
from jax import lax
from jax.experimental import pallas as pl
from jax.experimental.pallas import tpu as pltpu
from jax.sharding import PartitionSpec as P

HEAD_DIM = 64


EPSILON = 1e-06


def norm_affine(values, gain_vec, shift_vec):
    centre = values - jnp.mean(values, axis=-1, keepdims=True)
    spread = jnp.mean(centre * centre, axis=-1, keepdims=True)
    return centre * lax.rsqrt(spread + EPSILON) * gain_vec + shift_vec


def exact_gelu(values):
    return jax.nn.gelu(values, approximate=False)


def attend_block(query_blk, keys_all, values_all):
    scores = (
        jnp.einsum("qhd,khd->hqk", query_blk, keys_all, preferred_element_type=jnp.float32) * 0.125
    )
    top_score = jnp.max(scores, axis=-1, keepdims=True)
    shifted = jnp.exp(scores - top_score)
    total = jnp.sum(shifted, axis=-1, keepdims=True)
    attn_probs = (shifted / total).astype(jnp.bfloat16)
    mixed_blk = jnp.einsum(
        "hqk,khd->qhd", attn_probs, values_all, preferred_element_type=jnp.float32
    )
    return (mixed_blk, top_score[..., 0] + jnp.log(total[..., 0]))


def attend_back(carry, block, keys_all, values_all):
    grad_keys, grad_values = carry
    query_blk, grad_mixed, log_total = block
    scores = (
        jnp.einsum("qhd,khd->hqk", query_blk, keys_all, preferred_element_type=jnp.float32) * 0.125
    )
    attn_probs = jnp.exp(scores - log_total[..., None])
    grad_probs = jnp.einsum(
        "qhd,khd->hqk", grad_mixed, values_all, preferred_element_type=jnp.float32
    )
    grad_values = grad_values + jnp.einsum(
        "hqk,qhd->khd",
        attn_probs.astype(jnp.bfloat16),
        grad_mixed,
        preferred_element_type=jnp.float32,
    )
    inner_sum = jnp.sum(attn_probs * grad_probs, axis=-1, keepdims=True)
    grad_scores = (attn_probs * (grad_probs - inner_sum)).astype(jnp.bfloat16)
    grad_queries = (
        jnp.einsum("hqk,khd->qhd", grad_scores, keys_all, preferred_element_type=jnp.float32)
        * 0.125
    )
    grad_keys = (
        grad_keys
        + jnp.einsum("hqk,qhd->khd", grad_scores, query_blk, preferred_element_type=jnp.float32)
        * 0.125
    )
    return ((grad_keys, grad_values), grad_queries)


def forward_pass(inputs, weights):
    (
        gain_one,
        shift_one,
        weight_qkv,
        query_bias,
        value_bias,
        weight_out,
        out_bias,
        gain_two,
        shift_two,
        weight_up,
        up_bias,
        weight_down,
        down_bias,
    ) = weights
    length, model_width = inputs.shape
    head_count = model_width // HEAD_DIM
    block_rows = min(512, length)
    block_count = length // block_rows
    normed = norm_affine(
        inputs, gain_one.astype(jnp.float32), shift_one.astype(jnp.float32)
    ).astype(jnp.bfloat16)
    projected = jnp.dot(normed, weight_qkv, preferred_element_type=jnp.float32)
    queries = (projected[:, :model_width] + query_bias.astype(jnp.float32)).astype(jnp.bfloat16)
    keys_all = projected[:, model_width : 2 * model_width].astype(jnp.bfloat16)
    values_all = (projected[:, 2 * model_width :] + value_bias.astype(jnp.float32)).astype(
        jnp.bfloat16
    )
    queries = queries.reshape(length, head_count, HEAD_DIM)
    keys_all = keys_all.reshape(length, head_count, HEAD_DIM)
    values_all = values_all.reshape(length, head_count, HEAD_DIM)
    query_blocks = queries.reshape(block_count, block_rows, head_count, HEAD_DIM)
    mixed_blocks, log_totals = lax.map(
        partial(attend_block, keys_all=keys_all, values_all=values_all), query_blocks
    )
    mixed_heads = mixed_blocks.reshape(length, model_width).astype(jnp.bfloat16)
    middle = (
        inputs
        + jnp.dot(mixed_heads, weight_out, preferred_element_type=jnp.float32)
        + out_bias.astype(jnp.float32)
    )
    normed_two = norm_affine(
        middle, gain_two.astype(jnp.float32), shift_two.astype(jnp.float32)
    ).astype(jnp.bfloat16)
    hidden = jnp.dot(normed_two, weight_up, preferred_element_type=jnp.float32) + up_bias.astype(
        jnp.float32
    )
    active = exact_gelu(hidden).astype(jnp.bfloat16)
    result = (
        middle
        + jnp.dot(active, weight_down, preferred_element_type=jnp.float32)
        + down_bias.astype(jnp.float32)
    )
    saved = (
        inputs,
        normed,
        queries,
        keys_all,
        values_all,
        log_totals,
        mixed_heads,
        middle,
        normed_two,
        hidden,
        active,
    )
    return (result, saved)


def backward_pass(grad_result, saved, weights):
    (
        gain_one,
        shift_one,
        weight_qkv,
        query_bias,
        value_bias,
        weight_out,
        out_bias,
        gain_two,
        shift_two,
        weight_up,
        up_bias,
        weight_down,
        down_bias,
    ) = weights
    (
        inputs,
        normed,
        queries,
        keys_all,
        values_all,
        log_totals,
        mixed_heads,
        middle,
        normed_two,
        hidden,
        active,
    ) = saved
    length, model_width = inputs.shape
    head_count = model_width // HEAD_DIM
    block_rows = min(512, length)
    block_count = length // block_rows
    grad_down_out = grad_result.astype(jnp.bfloat16)
    grad_w_down = jnp.einsum("sf,sd->fd", active, grad_down_out, preferred_element_type=jnp.float32)
    grad_b_down = jnp.sum(grad_down_out.astype(jnp.float32), axis=0)
    grad_active = jnp.einsum(
        "sd,fd->sf", grad_down_out, weight_down, preferred_element_type=jnp.float32
    )
    _, gelu_pullback = jax.vjp(exact_gelu, hidden)
    grad_hidden = gelu_pullback(grad_active)[0].astype(jnp.bfloat16)
    grad_w_up = jnp.einsum("sd,sf->df", normed_two, grad_hidden, preferred_element_type=jnp.float32)
    grad_b_up = jnp.sum(grad_hidden.astype(jnp.float32), axis=0)
    grad_normed_two = jnp.einsum(
        "sf,df->sd", grad_hidden, weight_up, preferred_element_type=jnp.float32
    )
    _, norm_two_pullback = jax.vjp(
        norm_affine, middle, gain_two.astype(jnp.float32), shift_two.astype(jnp.float32)
    )
    grad_mid_norm, grad_gain_two, grad_shift_two = norm_two_pullback(grad_normed_two)
    grad_middle = grad_result + grad_mid_norm
    grad_att = grad_middle.astype(jnp.bfloat16)
    grad_w_out = jnp.einsum("sd,se->de", mixed_heads, grad_att, preferred_element_type=jnp.float32)
    grad_b_out = jnp.sum(grad_att.astype(jnp.float32), axis=0)
    grad_mixed = jnp.einsum("se,de->sd", grad_att, weight_out, preferred_element_type=jnp.float32)
    grad_mixed = grad_mixed.astype(jnp.bfloat16).reshape(
        block_count, block_rows, head_count, HEAD_DIM
    )
    query_blocks = queries.reshape(block_count, block_rows, head_count, HEAD_DIM)
    zeros_kv = jnp.zeros((length, head_count, HEAD_DIM), jnp.float32)
    (grad_keys, grad_values), grad_queries = lax.scan(
        partial(attend_back, keys_all=keys_all, values_all=values_all),
        (zeros_kv, zeros_kv),
        (query_blocks, grad_mixed, log_totals),
    )
    grad_queries = grad_queries.reshape(length, model_width).astype(jnp.bfloat16)
    grad_keys = grad_keys.reshape(length, model_width).astype(jnp.bfloat16)
    grad_values = grad_values.reshape(length, model_width).astype(jnp.bfloat16)
    grad_proj = jnp.concatenate([grad_queries, grad_keys, grad_values], axis=1)
    grad_w_qkv = jnp.einsum("sd,se->de", normed, grad_proj, preferred_element_type=jnp.float32)
    grad_b_query = jnp.sum(grad_queries.astype(jnp.float32), axis=0)
    grad_b_value = jnp.sum(grad_values.astype(jnp.float32), axis=0)
    grad_normed = jnp.einsum("se,de->sd", grad_proj, weight_qkv, preferred_element_type=jnp.float32)
    _, norm_one_pullback = jax.vjp(
        norm_affine, inputs, gain_one.astype(jnp.float32), shift_one.astype(jnp.float32)
    )
    grad_in_norm, grad_gain_one, grad_shift_one = norm_one_pullback(grad_normed)
    grad_inputs = grad_middle + grad_in_norm
    grads = (
        grad_gain_one,
        grad_shift_one,
        grad_w_qkv,
        grad_b_query,
        grad_b_value,
        grad_w_out,
        grad_b_out,
        grad_gain_two,
        grad_shift_two,
        grad_w_up,
        grad_b_up,
        grad_w_down,
        grad_b_down,
    )
    return (grad_inputs, grads)


def bits_of(ndp, nfs):
    core = nfs
    outer = [nfs << i for i in range(1, ndp.bit_length() - 1)]
    inner = [1 << i for i in range(nfs.bit_length() - 1)]
    return core, outer, inner


def stage_orders(ndp, nfs):
    core, outer, inner = bits_of(ndp, nfs)
    first, second = outer[0], inner[0]
    tail = outer[1:] + inner[1:]
    return core, ([first, second] + tail, [second, first] + tail)


def shard_table(ndp, nfs):
    n = ndp * nfs
    core, orders = stage_orders(ndp, nfs)
    table = np.zeros((n, n), np.int32)
    for me in range(n):
        for p in range(n):
            rel = core if p >= n // 2 else 0
            owner = 1 if (me ^ rel) & core else 0
            for i, mask in enumerate(orders[owner]):
                if p & (n >> (i + 2)):
                    rel ^= mask
            table[me, p] = me ^ rel
    return table


def stage_perms(ndp, nfs):
    n = ndp * nfs
    core, orders = stage_orders(ndp, nfs)
    perms = [[(i, i ^ core) for i in range(n)]]
    for a, b in zip(*orders):
        perms.append([(i, i ^ (b if i & core else a)) for i in range(n)])
    return perms


def place_blocks(pieces, table_row, scatter):
    n = pieces[0].shape[0]

    def body(t_ref, *refs):
        ins, outs, sem = refs[: len(pieces)], refs[len(pieces) : -1], refs[-1]
        copies = []
        for src, dst in zip(ins, outs):
            for i in range(n):
                j = t_ref[i]
                s, d = (i, j) if scatter else (j, i)
                copies.append(pltpu.make_async_copy(src.at[s], dst.at[d], sem))
        for c in copies:
            c.start()
        for c in copies:
            c.wait()

    return pl.pallas_call(
        body,
        out_shape=[jax.ShapeDtypeStruct(p.shape, p.dtype) for p in pieces],
        grid_spec=pltpu.PrefetchScalarGridSpec(
            num_scalar_prefetch=1,
            in_specs=[pl.BlockSpec(memory_space=pl.ANY)] * len(pieces),
            out_specs=[pl.BlockSpec(memory_space=pltpu.VMEM)] * len(pieces),
            scratch_shapes=[pltpu.SemaphoreType.DMA],
        ),
        name="place",
    )(table_row, *pieces)


AXES = ("dp", "fsdp")


def gather_relative(shard, perms):
    cur = shard[None]
    for perm in perms[:0:-1]:
        cur = jnp.concatenate([cur, lax.ppermute(cur, AXES, perm)], axis=0)
    return jnp.concatenate([cur, lax.ppermute(cur, AXES, perms[0])], axis=0)


def reduce_relative(rel, perms, wide=jnp.bfloat16):
    cur = rel
    for i, perm in enumerate(perms):
        half = cur.shape[0] // 2
        got = lax.ppermute(cur[half:], AXES, perm)
        total = cur[:half].astype(jnp.float32) + got.astype(jnp.float32)
        cur = total if i == len(perms) - 1 else total.astype(wide)
    return cur[0]


def per_device(ndp, nfs,
    tokens,
    ln1_gain,
    ln1_bias,
    w_qkv,
    bias_q,
    bias_v,
    w_out,
    bias_out,
    ln2_gain,
    ln2_bias,
    w_up,
    bias_up,
    w_down,
    bias_down,
    cot_first,
    cot_second,
    valid,
):
    n = ndp * nfs
    perms = stage_perms(ndp, nfs)
    me = lax.axis_index("dp") * nfs + lax.axis_index("fsdp")
    row = lax.dynamic_slice(jnp.asarray(shard_table(ndp, nfs)), (me, 0), (1, n))[0]
    vectors = (ln1_gain, ln1_bias, bias_q, bias_v, bias_out, ln2_gain, ln2_bias, bias_down, bias_up)
    sizes = [v.shape[0] for v in vectors]
    width = -(-sum(sizes) // 128) * 128
    packed = jnp.pad(jnp.concatenate(vectors), (0, width - sum(sizes)))[None]
    got_small = gather_relative(packed, perms)
    got_qkv = gather_relative(w_qkv, perms)
    got_out = gather_relative(w_out, perms)
    got_up = gather_relative(w_up, perms)
    got_down = gather_relative(w_down, perms)
    full_small = jnp.zeros_like(got_small).at[row].set(got_small)[:, 0]
    parts = []
    offset = 0
    for size in sizes:
        parts.append(full_small[:, offset : offset + size].reshape(-1))
        offset += size
    g1, s1, bq, bv, bo, g2, s2, bd, bu = parts
    (full_qkv,) = place_blocks([got_qkv], row, True)
    (full_out,) = place_blocks([got_out], row, True)
    (full_up,) = place_blocks([got_up], row, True)
    (full_down,) = place_blocks([got_down], row, True)
    flat = lambda w: w.reshape(-1, w.shape[-1])
    gathered = (
        g1,
        s1,
        flat(full_qkv),
        bq,
        bv,
        flat(full_out),
        bo,
        g2,
        s2,
        flat(full_up),
        bu,
        flat(full_down),
        bd,
    )
    start_rows = tokens[0].astype(jnp.float32)
    first_out, saved_first = forward_pass(start_rows, gathered)
    first_low = first_out.astype(jnp.bfloat16)
    second_in = lax.optimization_barrier(first_low).astype(jnp.float32)
    second_out, saved_second = forward_pass(second_in, gathered)
    keep_mask = valid[0].astype(jnp.float32)[:, None]
    grad_second = cot_second[0].astype(jnp.float32) * keep_mask
    grad_between, grads_second = backward_pass(grad_second, saved_second, gathered)
    grad_first = cot_first[0].astype(jnp.float32) * keep_mask + grad_between
    grad_inputs, grads_first = backward_pass(grad_first, saved_first, gathered)
    totals = tuple((left + right for left, right in zip(grads_first, grads_second)))
    (t_g1, t_s1, t_qkv, t_bq, t_bv, t_out, t_bo, t_g2, t_s2, t_up, t_bu, t_down, t_bd) = totals

    def reduce_matrix(total):
        low = total.astype(jnp.bfloat16).reshape(n, total.shape[0] // n, total.shape[1])
        (rel,) = place_blocks([low], row, False)
        return reduce_relative(rel, perms)

    d_down = reduce_matrix(t_down)
    d_up = reduce_matrix(t_up)
    d_out = reduce_matrix(t_out)
    d_qkv = reduce_matrix(t_qkv)
    small = jnp.concatenate(
        [v.reshape(n, -1) for v in (t_g1, t_s1, t_bq, t_bv, t_bo, t_g2, t_s2, t_bd, t_bu)], axis=1
    )
    small = jnp.pad(small, ((0, 0), (0, width - small.shape[1])))[:, None]
    small = reduce_relative(small[row], perms, jnp.float32)[0]
    outs = []
    offset = 0
    for size in sizes:
        outs.append(small[offset : offset + size])
        offset += size
    o_g1, o_s1, o_bq, o_bv, o_bo, o_g2, o_s2, o_bd, o_bu = outs
    return (
        first_low[None],
        second_out.astype(jnp.bfloat16)[None],
        grad_inputs.astype(jnp.bfloat16)[None],
        o_g1,
        o_s1,
        d_qkv,
        o_bq,
        o_bv,
        d_out,
        o_bo,
        o_g2,
        o_s2,
        d_up,
        o_bu,
        d_down,
        o_bd,
    )


def solution(mesh):
    ndp, nfs = mesh.shape["dp"], mesh.shape["fsdp"]
    return jax.shard_map(
        partial(per_device, ndp, nfs),
        mesh=mesh,
        in_specs=(
            P(("dp", "fsdp"), None, None),
            P(("dp", "fsdp")),
            P(("dp", "fsdp")),
            P(("dp", "fsdp"), None),
            P(("dp", "fsdp")),
            P(("dp", "fsdp")),
            P(("dp", "fsdp"), None),
            P(("dp", "fsdp")),
            P(("dp", "fsdp")),
            P(("dp", "fsdp")),
            P(("dp", "fsdp"), None),
            P(("dp", "fsdp")),
            P(("dp", "fsdp"), None),
            P(("dp", "fsdp")),
            P(("dp", "fsdp"), None, None),
            P(("dp", "fsdp"), None, None),
            P(("dp", "fsdp"), None),
        ),
        out_specs=(
            P(("dp", "fsdp"), None, None),
            P(("dp", "fsdp"), None, None),
            P(("dp", "fsdp"), None, None),
            P(("dp", "fsdp")),
            P(("dp", "fsdp")),
            P(("dp", "fsdp"), None),
            P(("dp", "fsdp")),
            P(("dp", "fsdp")),
            P(("dp", "fsdp"), None),
            P(("dp", "fsdp")),
            P(("dp", "fsdp")),
            P(("dp", "fsdp")),
            P(("dp", "fsdp"), None),
            P(("dp", "fsdp")),
            P(("dp", "fsdp"), None),
            P(("dp", "fsdp")),
        ),
        check_vma=False,
    )
```

```python
from functools import partial

import numpy as np
import jax
import jax.numpy as jnp
from jax import lax
from jax.experimental import pallas as pl
from jax.experimental.pallas import tpu as pltpu
from jax.sharding import PartitionSpec as P

EPSILON = 1e-06
HEAD_DIM = 64
LOG2E = 1.4426950408889634
RSQRT_2PI = 0.3989422804014327
TAIL_STEP = 0.305
TAIL_COEFFS = (
    0.12163971608667215,
    0.12246710281167089,
    0.10341891431417467,
    0.12102858688667265,
    -0.03799063399351653,
    0.18573260086829071,
    -0.15299777850455798,
    0.03670153882152772,
)
NT = (((1,), (1,)), ((), ()))
TN = (((0,), (0,)), ((), ()))


def dot(a, b, dims=(((1,), (0,)), ((), ()))):
    return lax.dot_general(a, b, dims, preferred_element_type=jnp.float32)


def whole(shape):
    return pl.BlockSpec(shape, lambda *_: (0,) * len(shape))


def normal_tail(u):
    size = jnp.abs(u)
    t = 1.0 / (1.0 + TAIL_STEP * size)
    bell = jnp.exp(-0.5 * (u * u))
    poly = jnp.full_like(u, TAIL_COEFFS[-1])
    for c in TAIL_COEFFS[-2::-1]:
        poly = poly * t + c
    tail = bell * (t * poly)
    return jnp.where(u < 0, tail, 1.0 - tail), bell


def row_stats(v):
    centre = v - jnp.mean(v, axis=-1, keepdims=True)
    inv = lax.rsqrt(jnp.mean(centre * centre, axis=-1, keepdims=True) + EPSILON)
    return centre * inv, inv


def norm_project(x, gain, shift, weight, bias, tn):
    rows, width = x.shape
    cols = weight.shape[1]

    def body(x_ref, g_ref, s_ref, w_ref, b_ref, a_ref, o_ref):
        @pl.when(pl.program_id(0) == 0)
        def _():
            xhat, _ = row_stats(x_ref[...].astype(jnp.float32))
            a_ref[...] = (xhat * g_ref[...] + s_ref[...]).astype(jnp.bfloat16)

        o_ref[...] = (dot(a_ref[...], w_ref[...]) + b_ref[...]).astype(jnp.bfloat16)

    return pl.pallas_call(
        body,
        grid=(cols // tn,),
        in_specs=[
            whole((rows, width)),
            whole((1, width)),
            whole((1, width)),
            pl.BlockSpec((width, tn), lambda j: (0, j)),
            pl.BlockSpec((1, tn), lambda j: (0, j)),
        ],
        out_specs=[whole((rows, width)), pl.BlockSpec((rows, tn), lambda j: (0, j))],
        out_shape=[
            jax.ShapeDtypeStruct((rows, width), jnp.bfloat16),
            jax.ShapeDtypeStruct((rows, cols), jnp.bfloat16),
        ],
        name="norm_project",
    )(x, gain, shift, weight, bias)


def attention(qkv):
    rows, width = qkv.shape[0], qkv.shape[1] // 3
    pairs = width // (2 * HEAD_DIM)
    span = 2 * HEAD_DIM

    def body(q_ref, k_ref, v_ref, o_ref, l_ref):
        q, k, v = q_ref[...], k_ref[...], v_ref[...]
        lane = lax.broadcasted_iota(jnp.int32, (rows, span), 1)
        outs, logs = [], []
        for h in range(2):
            mine = (lane < HEAD_DIM) if h == 0 else (lane >= HEAD_DIM)
            kh = jnp.where(mine, k, jnp.zeros_like(k))
            s = dot(q, kh, NT) * 0.125
            top = jnp.max(s, axis=-1, keepdims=True)
            e = jnp.exp(s - top)
            total = jnp.sum(e, axis=-1, keepdims=True)
            p = (e * (1.0 / total)).astype(jnp.bfloat16)
            outs.append(dot(p, v))
            logs.append(top + jnp.log(total))
        first = lane < HEAD_DIM
        o_ref[...] = jnp.where(first, outs[0], outs[1]).astype(jnp.bfloat16)
        both = jnp.where(first, logs[0], logs[1])
        turned = both.T
        l_ref[0, 0:1, :] = turned[0:1, :]
        l_ref[0, 1:2, :] = turned[HEAD_DIM : HEAD_DIM + 1, :]

    col = lambda base: pl.BlockSpec((rows, span), lambda j: (0, base + j))
    return pl.pallas_call(
        body,
        grid=(pairs,),
        in_specs=[col(0), col(pairs), col(2 * pairs)],
        out_specs=[col(0), pl.BlockSpec((1, 8, rows), lambda j: (j, 0, 0))],
        out_shape=[
            jax.ShapeDtypeStruct((rows, width), jnp.bfloat16),
            jax.ShapeDtypeStruct((pairs, 8, rows), jnp.float32),
        ],
        name="attention",
    )(qkv, qkv, qkv)


def attention_back(qkv, logs, d_o):
    rows, width = qkv.shape[0], qkv.shape[1] // 3
    pairs = width // (2 * HEAD_DIM)
    span = 2 * HEAD_DIM

    def body(q_ref, k_ref, v_ref, l_ref, do_ref, dq_ref, dk_ref, dv_ref, cq_ref, cv_ref):
        q, k, v, do = q_ref[...], k_ref[...], v_ref[...], do_ref[...]
        lane = lax.broadcasted_iota(jnp.int32, (rows, span), 1)
        dqs, dks, dvs = [], [], []
        for h in range(2):
            mine = (lane < HEAD_DIM) if h == 0 else (lane >= HEAD_DIM)
            kh = jnp.where(mine, k, jnp.zeros_like(k))
            vh = jnp.where(mine, v, jnp.zeros_like(v))
            st = dot(kh, q, NT) * 0.125
            pt = jnp.exp(st - l_ref[0, h : h + 1, :])
            dpt = dot(vh, do, NT)
            w = pt * dpt
            inner = jnp.sum(w, axis=0, keepdims=True)
            dst = (w - pt * inner).astype(jnp.bfloat16)
            dvs.append(dot(pt.astype(jnp.bfloat16), do))
            dks.append(dot(dst, q))
            dqs.append(dot(dst, k, TN))
        first = lane < HEAD_DIM
        dq = (jnp.where(first, dqs[0], dqs[1]) * 0.125).astype(jnp.bfloat16)
        dk = (jnp.where(first, dks[0], dks[1]) * 0.125).astype(jnp.bfloat16)
        dv = jnp.where(first, dvs[0], dvs[1]).astype(jnp.bfloat16)
        dq_ref[...] = dq
        dk_ref[...] = dk
        dv_ref[...] = dv
        cq_ref[...] = jnp.sum(dq.astype(jnp.float32), axis=0, keepdims=True)
        cv_ref[...] = jnp.sum(dv.astype(jnp.float32), axis=0, keepdims=True)

    col = lambda base: pl.BlockSpec((rows, span), lambda j: (0, base + j))
    sums = pl.BlockSpec((1, span), lambda j: (0, j))
    mat = jax.ShapeDtypeStruct((rows, width), jnp.bfloat16)
    vec = jax.ShapeDtypeStruct((1, width), jnp.float32)
    return pl.pallas_call(
        body,
        grid=(pairs,),
        in_specs=[
            col(0),
            col(pairs),
            col(2 * pairs),
            pl.BlockSpec((1, 8, rows), lambda j: (j, 0, 0)),
            col(0),
        ],
        out_specs=[col(0), col(0), col(0), sums, sums],
        out_shape=[mat, mat, mat, vec, vec],
        name="attention_back",
    )(qkv, qkv, qkv, logs, d_o)


def project_norm(o, weight, bias, x, gain, shift):
    rows, width = o.shape
    tm = rows // 2

    def body(o_ref, w_ref, b_ref, x_ref, g_ref, s_ref, x1_ref, a_ref):
        x1 = x_ref[...].astype(jnp.float32) + (dot(o_ref[...], w_ref[...]) + b_ref[...])
        x1_ref[...] = x1
        xhat, _ = row_stats(x1)
        a_ref[...] = (xhat * g_ref[...] + s_ref[...]).astype(jnp.bfloat16)

    rowblk = pl.BlockSpec((tm, width), lambda i: (i, 0))
    vec = whole((1, width))
    return pl.pallas_call(
        body,
        grid=(rows // tm,),
        in_specs=[rowblk, whole((width, width)), vec, rowblk, vec, vec],
        out_specs=[rowblk, rowblk],
        out_shape=[
            jax.ShapeDtypeStruct((rows, width), jnp.float32),
            jax.ShapeDtypeStruct((rows, width), jnp.bfloat16),
        ],
        name="project_norm",
    )(o, weight, bias, x, gain, shift)


def feed_forward(a, up, up_bias, down, down_bias, x1, tf):
    rows, width = a.shape
    hidden = up.shape[1]
    steps = hidden // tf

    def body(a_ref, u_ref, ub_ref, d_ref, db_ref, x_ref, g_ref, gp_ref, y_ref, acc):
        j = pl.program_id(0)
        u = dot(a_ref[...], u_ref[...]) + ub_ref[...]
        phi, bell = normal_tail(u)
        g = (u * phi).astype(jnp.bfloat16)
        g_ref[...] = g
        gp_ref[...] = (phi + (u * RSQRT_2PI) * bell).astype(jnp.bfloat16)

        @pl.when(j == 0)
        def _():
            acc[...] = x_ref[...] + db_ref[...]

        acc[...] += dot(g, d_ref[...])

        @pl.when(j == steps - 1)
        def _():
            y_ref[...] = acc[...].astype(jnp.bfloat16)

    return pl.pallas_call(
        body,
        grid=(steps,),
        in_specs=[
            whole((rows, width)),
            pl.BlockSpec((width, tf), lambda j: (0, j)),
            pl.BlockSpec((1, tf), lambda j: (0, j)),
            pl.BlockSpec((tf, width), lambda j: (j, 0)),
            whole((1, width)),
            whole((rows, width)),
        ],
        out_specs=[
            pl.BlockSpec((rows, tf), lambda j: (0, j)),
            pl.BlockSpec((rows, tf), lambda j: (0, j)),
            whole((rows, width)),
        ],
        out_shape=[
            jax.ShapeDtypeStruct((rows, hidden), jnp.bfloat16),
            jax.ShapeDtypeStruct((rows, hidden), jnp.bfloat16),
            jax.ShapeDtypeStruct((rows, width), jnp.bfloat16),
        ],
        scratch_shapes=[pltpu.VMEM((rows, width), jnp.float32)],
        name="feed_forward",
    )(a, up, up_bias, down, down_bias, x1)


def feed_forward_back(dy, gp, down, up, x1, gain, w_out, tf):
    rows, width = dy.shape
    hidden = gp.shape[1]
    steps = hidden // tf

    def body(
        dy_ref, gp_ref, d_ref, u_ref, x_ref, g_ref, w_ref,
        dm_ref, du_ref, dx_ref, da_ref, do_ref, cdm_ref, cdu_ref, cda_ref, cg_ref, cs_ref, acc,
    ):
        j = pl.program_id(0)

        @pl.when(j == 0)
        def _():
            low = dy_ref[...].astype(jnp.bfloat16)
            dm_ref[...] = low
            cdm_ref[...] = jnp.sum(low.astype(jnp.float32), axis=0, keepdims=True)
            acc[...] = jnp.zeros_like(acc)

        du = (dot(dm_ref[...], d_ref[...], NT) * gp_ref[...].astype(jnp.float32)).astype(jnp.bfloat16)
        du_ref[...] = du
        cdu_ref[...] = jnp.sum(du.astype(jnp.float32), axis=0, keepdims=True)
        acc[...] += dot(du, u_ref[...], NT)

        @pl.when(j == steps - 1)
        def _():
            da2 = acc[...]
            xhat, inv = row_stats(x_ref[...])
            cg_ref[...] = jnp.sum(da2 * xhat, axis=0, keepdims=True)
            cs_ref[...] = jnp.sum(da2, axis=0, keepdims=True)
            t = da2 * g_ref[...]
            m1 = jnp.mean(t, axis=-1, keepdims=True)
            m2 = jnp.mean(t * xhat, axis=-1, keepdims=True)
            dx1 = dy_ref[...] + inv * (t - m1 - xhat * m2)
            dx_ref[...] = dx1
            low = dx1.astype(jnp.bfloat16)
            da_ref[...] = low
            cda_ref[...] = jnp.sum(low.astype(jnp.float32), axis=0, keepdims=True)
            do_ref[...] = dot(low, w_ref[...], NT).astype(jnp.bfloat16)

    full = whole((rows, width))
    vec = whole((1, width))
    f = lambda s, d: jax.ShapeDtypeStruct(s, d)
    return pl.pallas_call(
        body,
        grid=(steps,),
        in_specs=[
            full,
            pl.BlockSpec((rows, tf), lambda j: (0, j)),
            pl.BlockSpec((tf, width), lambda j: (j, 0)),
            pl.BlockSpec((width, tf), lambda j: (0, j)),
            full,
            vec,
            whole((width, width)),
        ],
        out_specs=[
            full,
            pl.BlockSpec((rows, tf), lambda j: (0, j)),
            full,
            full,
            full,
            vec,
            pl.BlockSpec((1, tf), lambda j: (0, j)),
            vec,
            vec,
            vec,
        ],
        out_shape=[
            f((rows, width), jnp.bfloat16),
            f((rows, hidden), jnp.bfloat16),
            f((rows, width), jnp.float32),
            f((rows, width), jnp.bfloat16),
            f((rows, width), jnp.bfloat16),
            f((1, width), jnp.float32),
            f((1, hidden), jnp.float32),
            f((1, width), jnp.float32),
            f((1, width), jnp.float32),
            f((1, width), jnp.float32),
        ],
        scratch_shapes=[pltpu.VMEM((rows, width), jnp.float32)],
        name="feed_forward_back",
    )(dy, gp, down, up, x1, gain, w_out)


def project_back(dq, dk, dv, weight, x, gain, dx1, extra, out_dtype):
    rows, width = dq.shape
    tm = rows // 2
    have = extra is not None

    def body(*refs):
        dq_ref, dk_ref, dv_ref, w_ref, x_ref, g_ref, d_ref = refs[:7]
        out_ref, cg_ref, cs_ref = refs[-3:]
        da = dot(dq_ref[...], w_ref[:, :width], NT)
        da += dot(dk_ref[...], w_ref[:, width : 2 * width], NT)
        da += dot(dv_ref[...], w_ref[:, 2 * width :], NT)
        xhat, inv = row_stats(x_ref[...].astype(jnp.float32))
        cg = jnp.sum(da * xhat, axis=0, keepdims=True)
        cs = jnp.sum(da, axis=0, keepdims=True)

        @pl.when(pl.program_id(0) == 0)
        def _():
            cg_ref[...] = cg
            cs_ref[...] = cs

        @pl.when(pl.program_id(0) > 0)
        def _():
            cg_ref[...] += cg
            cs_ref[...] += cs

        t = da * g_ref[...]
        m1 = jnp.mean(t, axis=-1, keepdims=True)
        m2 = jnp.mean(t * xhat, axis=-1, keepdims=True)
        dx = d_ref[...] + inv * (t - m1 - xhat * m2)
        if have:
            dx = refs[7][...].astype(jnp.float32) * refs[8][...] + dx
        out_ref[...] = dx.astype(out_dtype)

    rowblk = pl.BlockSpec((tm, width), lambda i: (i, 0))
    vec = whole((1, width))
    specs = [rowblk, rowblk, rowblk, whole((width, 3 * width)), rowblk, vec, rowblk]
    args = [dq, dk, dv, weight, x, gain, dx1]
    if have:
        specs += [rowblk, pl.BlockSpec((tm, 1), lambda i: (i, 0))]
        args += list(extra)
    return pl.pallas_call(
        body,
        grid=(rows // tm,),
        in_specs=specs,
        out_specs=[rowblk, vec, vec],
        out_shape=[
            jax.ShapeDtypeStruct((rows, width), out_dtype),
            jax.ShapeDtypeStruct((1, width), jnp.float32),
            jax.ShapeDtypeStruct((1, width), jnp.float32),
        ],
        name="project_back",
    )(*args)


def weight_grad(lefts, rights, tm, tn):
    rows, m = lefts[0].shape
    cols = rights[0].shape[1]
    count = len(lefts)

    def body(*refs):
        a, b, o_ref = refs[:count], refs[count : 2 * count], refs[-1]
        total = dot(a[0][...], b[0][...], TN)
        for x, y in zip(a[1:], b[1:]):
            total += dot(x[...], y[...], TN)
        o_ref[...] = total.astype(jnp.bfloat16)

    return pl.pallas_call(
        body,
        grid=(m // tm, cols // tn),
        in_specs=[pl.BlockSpec((rows, tm), lambda i, j: (0, i))] * count
        + [pl.BlockSpec((rows, tn), lambda i, j: (0, j))] * count,
        out_specs=pl.BlockSpec((tm, tn), lambda i, j: (i, j)),
        out_shape=jax.ShapeDtypeStruct((m, cols), jnp.bfloat16),
        name="weight_grad",
    )(*lefts, *rights)


def vec(v):
    return v.astype(jnp.float32).reshape(1, -1)


def layer_forward(x, w):
    a1, qkv = norm_project(x, w["g1"], w["s1"], w["qkv"], w["bqkv"], 512)
    o, logs = attention(qkv)
    x1, a2 = project_norm(o, w["out"], w["bo"], x, w["g2"], w["s2"])
    g, gp, y = feed_forward(a2, w["up"], w["bu"], w["down"], w["bd"], x1, 512)
    return y, (x, a1, qkv, logs, o, x1, a2, g, gp)


def layer_back(dy, saved, w, extra, out_dtype):
    x, a1, qkv, logs, o, x1, a2, g, gp = saved
    dm, du, dx1, da, do, cdm, cdu, cda, cg2, cs2 = feed_forward_back(
        dy, gp, w["down"], w["up"], x1, w["g2"], w["out"], 512
    )
    dq, dk, dv, cq, cv = attention_back(qkv, logs, do)
    dx, cg1, cs1 = project_back(dq, dk, dv, w["qkv"], x, w["g1"], dx1, extra, out_dtype)
    return dx, (dm, du, da, dq, dk, dv), (cg1, cs1, cq, cv, cda, cg2, cs2, cdm, cdu)


def bits_of(ndp, nfs):
    core = nfs
    outer = [nfs << i for i in range(1, ndp.bit_length() - 1)]
    inner = [1 << i for i in range(nfs.bit_length() - 1)]
    return core, outer, inner


def stage_orders(ndp, nfs):
    core, outer, inner = bits_of(ndp, nfs)
    first, second = outer[0], inner[0]
    tail = outer[1:] + inner[1:]
    return core, ([first, second] + tail, [second, first] + tail)


def shard_table(ndp, nfs):
    n = ndp * nfs
    core, orders = stage_orders(ndp, nfs)
    table = np.zeros((n, n), np.int32)
    for me in range(n):
        for p in range(n):
            rel = core if p >= n // 2 else 0
            owner = 1 if (me ^ rel) & core else 0
            for i, mask in enumerate(orders[owner]):
                if p & (n >> (i + 2)):
                    rel ^= mask
            table[me, p] = me ^ rel
    return table


def stage_perms(ndp, nfs):
    n = ndp * nfs
    core, orders = stage_orders(ndp, nfs)
    perms = [[(i, i ^ core) for i in range(n)]]
    for a, b in zip(*orders):
        perms.append([(i, i ^ (b if i & core else a)) for i in range(n)])
    return perms


def place_blocks(pieces, table_row, scatter):
    n = pieces[0].shape[0]

    def body(t_ref, *refs):
        ins, outs, sem = refs[: len(pieces)], refs[len(pieces) : -1], refs[-1]
        copies = []
        for src, dst in zip(ins, outs):
            for i in range(n):
                j = t_ref[i]
                s, d = (i, j) if scatter else (j, i)
                copies.append(pltpu.make_async_copy(src.at[s], dst.at[d], sem))
        for c in copies:
            c.start()
        for c in copies:
            c.wait()

    return pl.pallas_call(
        body,
        out_shape=[jax.ShapeDtypeStruct(p.shape, p.dtype) for p in pieces],
        grid_spec=pltpu.PrefetchScalarGridSpec(
            num_scalar_prefetch=1,
            in_specs=[pl.BlockSpec(memory_space=pl.ANY)] * len(pieces),
            out_specs=[pl.BlockSpec(memory_space=pltpu.VMEM)] * len(pieces),
            scratch_shapes=[pltpu.SemaphoreType.DMA],
        ),
        name="place",
    )(table_row, *pieces)


AXES = ("dp", "fsdp")


def gather_relative(shard, perms):
    cur = shard[None]
    for perm in perms[:0:-1]:
        cur = jnp.concatenate([cur, lax.ppermute(cur, AXES, perm)], axis=0)
    return jnp.concatenate([cur, lax.ppermute(cur, AXES, perms[0])], axis=0)


def reduce_relative(rel, perms, wide=jnp.bfloat16):
    cur = rel
    for i, perm in enumerate(perms):
        half = cur.shape[0] // 2
        got = lax.ppermute(cur[half:], AXES, perm)
        total = cur[:half].astype(jnp.float32) + got.astype(jnp.float32)
        cur = total if i == len(perms) - 1 else total.astype(wide)
    return cur[0]


def per_device(ndp, nfs,
    tokens,
    ln1_gain,
    ln1_bias,
    w_qkv,
    bias_q,
    bias_v,
    w_out,
    bias_out,
    ln2_gain,
    ln2_bias,
    w_up,
    bias_up,
    w_down,
    bias_down,
    cot_first,
    cot_second,
    valid,
):
    n = ndp * nfs
    perms = stage_perms(ndp, nfs)
    me = lax.axis_index("dp") * nfs + lax.axis_index("fsdp")
    row = lax.dynamic_slice(jnp.asarray(shard_table(ndp, nfs)), (me, 0), (1, n))[0]
    vectors = (ln1_gain, ln1_bias, bias_q, bias_v, bias_out, ln2_gain, ln2_bias, bias_down, bias_up)
    sizes = [v.shape[0] for v in vectors]
    width = -(-sum(sizes) // 128) * 128
    packed = jnp.pad(jnp.concatenate(vectors), (0, width - sum(sizes)))[None]
    got_small = gather_relative(packed, perms)
    got_qkv = gather_relative(w_qkv, perms)
    got_out = gather_relative(w_out, perms)
    got_up = gather_relative(w_up, perms)
    got_down = gather_relative(w_down, perms)
    full_small = jnp.zeros_like(got_small).at[row].set(got_small)[:, 0]
    parts = []
    offset = 0
    for size in sizes:
        parts.append(vec(full_small[:, offset : offset + size]))
        offset += size
    g1, s1, bq, bv, bo, g2, s2, bd, bu = parts
    flat = lambda got: place_blocks([got], row, True)[0].reshape(-1, got.shape[-1])
    w = dict(g1=g1, s1=s1, bo=bo, g2=g2, s2=s2, bd=bd, bu=bu)
    w["bqkv"] = jnp.concatenate([bq, jnp.zeros_like(bq), bv], axis=1)
    w["qkv"] = flat(got_qkv)
    w["out"] = flat(got_out)
    w["up"] = flat(got_up)
    w["down"] = flat(got_down)
    first, saved_first = layer_forward(tokens[0], w)
    second, saved_second = layer_forward(first, w)
    keep_mask = valid[0].astype(jnp.float32)[:, None]
    grad_second = cot_second[0].astype(jnp.float32) * keep_mask
    grad_first, mats_second, sums_second = layer_back(
        grad_second, saved_second, w, (cot_first[0], keep_mask), jnp.float32
    )
    grad_inputs, mats_first, sums_first = layer_back(
        grad_first, saved_first, w, None, jnp.bfloat16
    )
    dm, du, da, dq, dk, dv = zip(mats_first, mats_second)
    saved = list(zip(saved_first, saved_second))

    def reduce_matrix(total):
        (rel,) = place_blocks([total.reshape(n, total.shape[0] // n, total.shape[1])], row, False)
        return reduce_relative(rel, perms)

    d_down = reduce_matrix(weight_grad(saved[7], dm, 512, 512))
    d_up = reduce_matrix(weight_grad(saved[6], du, 512, 512))
    d_out = reduce_matrix(weight_grad(saved[4], da, 512, 512))
    d_qkv = reduce_matrix(
        jnp.concatenate([weight_grad(saved[1], d, 512, 512) for d in (dq, dk, dv)], axis=1)
    )
    small = jnp.concatenate(
        [(a + b).reshape(n, -1) for a, b in zip(sums_first, sums_second)], axis=1
    )
    small = jnp.pad(small, ((0, 0), (0, width - small.shape[1])))[:, None]
    small = reduce_relative(small[row], perms, jnp.float32)[0]
    outs = []
    offset = 0
    for size in sizes:
        outs.append(small[offset : offset + size])
        offset += size
    o_g1, o_s1, o_bq, o_bv, o_bo, o_g2, o_s2, o_bd, o_bu = outs
    return (
        first[None],
        second[None],
        grad_inputs[None],
        o_g1,
        o_s1,
        d_qkv,
        o_bq,
        o_bv,
        d_out,
        o_bo,
        o_g2,
        o_s2,
        d_up,
        o_bu,
        d_down,
        o_bd,
    )


def solution(mesh):
    ndp, nfs = mesh.shape["dp"], mesh.shape["fsdp"]
    return jax.shard_map(
        partial(per_device, ndp, nfs),
        mesh=mesh,
        in_specs=(
            P(("dp", "fsdp"), None, None),
            P(("dp", "fsdp")),
            P(("dp", "fsdp")),
            P(("dp", "fsdp"), None),
            P(("dp", "fsdp")),
            P(("dp", "fsdp")),
            P(("dp", "fsdp"), None),
            P(("dp", "fsdp")),
            P(("dp", "fsdp")),
            P(("dp", "fsdp")),
            P(("dp", "fsdp"), None),
            P(("dp", "fsdp")),
            P(("dp", "fsdp"), None),
            P(("dp", "fsdp")),
            P(("dp", "fsdp"), None, None),
            P(("dp", "fsdp"), None, None),
            P(("dp", "fsdp"), None),
        ),
        out_specs=(
            P(("dp", "fsdp"), None, None),
            P(("dp", "fsdp"), None, None),
            P(("dp", "fsdp"), None, None),
            P(("dp", "fsdp")),
            P(("dp", "fsdp")),
            P(("dp", "fsdp"), None),
            P(("dp", "fsdp")),
            P(("dp", "fsdp")),
            P(("dp", "fsdp"), None),
            P(("dp", "fsdp")),
            P(("dp", "fsdp")),
            P(("dp", "fsdp")),
            P(("dp", "fsdp"), None),
            P(("dp", "fsdp")),
            P(("dp", "fsdp"), None),
            P(("dp", "fsdp")),
        ),
        check_vma=False,
    )
```

```python
from functools import partial

import numpy as np
import jax
import jax.numpy as jnp
from jax import lax
from jax.experimental import pallas as pl
from jax.experimental.pallas import tpu as pltpu
from jax.sharding import PartitionSpec as P

EPSILON = 1e-06
HEAD_DIM = 64
LOG2E = 1.4426950408889634
RSQRT_2PI = 0.3989422804014327
TAIL_STEP = 0.305
TAIL_COEFFS = (
    0.12163971608667215,
    0.12246710281167089,
    0.10341891431417467,
    0.12102858688667265,
    -0.03799063399351653,
    0.18573260086829071,
    -0.15299777850455798,
    0.03670153882152772,
)
NT = (((1,), (1,)), ((), ()))
TN = (((0,), (0,)), ((), ()))


def dot(a, b, dims=(((1,), (0,)), ((), ()))):
    return lax.dot_general(a, b, dims, preferred_element_type=jnp.float32)


def whole(shape):
    return pl.BlockSpec(shape, lambda *_: (0,) * len(shape))


def normal_tail(u):
    size = jnp.abs(u)
    t = 1.0 / (1.0 + TAIL_STEP * size)
    bell = jnp.exp(-0.5 * (u * u))
    poly = jnp.full_like(u, TAIL_COEFFS[-1])
    for c in TAIL_COEFFS[-2::-1]:
        poly = poly * t + c
    tail = bell * (t * poly)
    return jnp.where(u < 0, tail, 1.0 - tail), bell


def row_stats(v):
    centre = v - jnp.mean(v, axis=-1, keepdims=True)
    inv = lax.rsqrt(jnp.mean(centre * centre, axis=-1, keepdims=True) + EPSILON)
    return centre * inv, inv


def norm_project(x, gain, shift, weight, bias, tn, cols):
    rows, width = x.shape

    def body(x_ref, g_ref, s_ref, w_ref, b_ref, a_ref, o_ref):
        @pl.when(pl.program_id(0) == 0)
        def _():
            xhat, _ = row_stats(x_ref[...].astype(jnp.float32))
            a_ref[...] = (xhat * g_ref[...] + s_ref[...]).astype(jnp.bfloat16)

        o_ref[...] = (dot(a_ref[...], w_ref[...]) + b_ref[...]).astype(jnp.bfloat16)

    return pl.pallas_call(
        body,
        grid=(cols // tn,),
        in_specs=[
            whole((rows, width)),
            whole((1, width)),
            whole((1, width)),
            pl.BlockSpec((width, tn), lambda j: (0, j)),
            pl.BlockSpec((1, tn), lambda j: (0, j)),
        ],
        out_specs=[whole((rows, width)), pl.BlockSpec((rows, tn), lambda j: (0, j))],
        out_shape=[
            jax.ShapeDtypeStruct((rows, width), jnp.bfloat16),
            jax.ShapeDtypeStruct((rows, cols), jnp.bfloat16),
        ],
        name="norm_project",
    )(x, gain, shift, weight, bias)


def attention(qkv):
    rows, width = qkv.shape[0], qkv.shape[1] // 3
    pairs = width // (2 * HEAD_DIM)
    span = 2 * HEAD_DIM

    def body(q_ref, k_ref, v_ref, o_ref, l_ref):
        q, k, v = q_ref[...], k_ref[...], v_ref[...]
        lane = lax.broadcasted_iota(jnp.int32, (rows, span), 1)
        outs, logs = [], []
        for h in range(2):
            mine = (lane < HEAD_DIM) if h == 0 else (lane >= HEAD_DIM)
            kh = jnp.where(mine, k, jnp.zeros_like(k))
            s = dot(q, kh, NT) * 0.125
            top = jnp.max(s, axis=-1, keepdims=True)
            e = jnp.exp(s - top)
            total = jnp.sum(e, axis=-1, keepdims=True)
            p = (e * (1.0 / total)).astype(jnp.bfloat16)
            outs.append(dot(p, v))
            logs.append(top + jnp.log(total))
        first = lane < HEAD_DIM
        o_ref[...] = jnp.where(first, outs[0], outs[1]).astype(jnp.bfloat16)
        both = jnp.where(first, logs[0], logs[1])
        turned = both.T
        l_ref[0, 0:1, :] = turned[0:1, :]
        l_ref[0, 1:2, :] = turned[HEAD_DIM : HEAD_DIM + 1, :]

    col = lambda base: pl.BlockSpec((rows, span), lambda j: (0, base + j))
    return pl.pallas_call(
        body,
        grid=(pairs,),
        in_specs=[col(0), col(pairs), col(2 * pairs)],
        out_specs=[col(0), pl.BlockSpec((1, 8, rows), lambda j: (j, 0, 0))],
        out_shape=[
            jax.ShapeDtypeStruct((rows, width), jnp.bfloat16),
            jax.ShapeDtypeStruct((pairs, 8, rows), jnp.float32),
        ],
        name="attention",
    )(qkv, qkv, qkv)


def attention_back(qkv, logs, d_o, first_pair, pairs):
    rows, width = qkv.shape[0], qkv.shape[1] // 3
    every = width // (2 * HEAD_DIM)
    span = 2 * HEAD_DIM

    def body(q_ref, k_ref, v_ref, l_ref, do_ref, d_ref, cq_ref, cv_ref):
        q, k, v, do = q_ref[...], k_ref[...], v_ref[...], do_ref[...]
        lane = lax.broadcasted_iota(jnp.int32, (rows, span), 1)
        dqs, dks, dvs = [], [], []
        for h in range(2):
            mine = (lane < HEAD_DIM) if h == 0 else (lane >= HEAD_DIM)
            kh = jnp.where(mine, k, jnp.zeros_like(k))
            vh = jnp.where(mine, v, jnp.zeros_like(v))
            st = dot(kh, q, NT) * 0.125
            pt = jnp.exp(st - l_ref[0, h : h + 1, :])
            dpt = dot(vh, do, NT)
            w = pt * dpt
            inner = jnp.sum(w, axis=0, keepdims=True)
            dst = (w - pt * inner).astype(jnp.bfloat16)
            dvs.append(dot(pt.astype(jnp.bfloat16), do))
            dks.append(dot(dst, q))
            dqs.append(dot(dst, k, TN))
        first = lane < HEAD_DIM
        dq = (jnp.where(first, dqs[0], dqs[1]) * 0.125).astype(jnp.bfloat16)
        dk = (jnp.where(first, dks[0], dks[1]) * 0.125).astype(jnp.bfloat16)
        dv = jnp.where(first, dvs[0], dvs[1]).astype(jnp.bfloat16)
        d_ref[0] = dq
        d_ref[1] = dk
        d_ref[2] = dv
        cq_ref[...] = jnp.sum(dq.astype(jnp.float32), axis=0, keepdims=True)
        cv_ref[...] = jnp.sum(dv.astype(jnp.float32), axis=0, keepdims=True)

    col = lambda base: pl.BlockSpec((rows, span), lambda j: (0, base + j))
    sums = pl.BlockSpec((1, span), lambda j: (0, j))
    vec_shape = jax.ShapeDtypeStruct((1, pairs * span), jnp.float32)
    return pl.pallas_call(
        body,
        grid=(pairs,),
        in_specs=[
            col(first_pair),
            col(every + first_pair),
            col(2 * every + first_pair),
            pl.BlockSpec((1, 8, rows), lambda j: (first_pair + j, 0, 0)),
            col(first_pair),
        ],
        out_specs=[pl.BlockSpec((3, rows, span), lambda j: (0, 0, j)), sums, sums],
        out_shape=[
            jax.ShapeDtypeStruct((3, rows, pairs * span), jnp.bfloat16),
            vec_shape,
            vec_shape,
        ],
        name="attention_back",
    )(qkv, qkv, qkv, logs, d_o)


def project_norm(o, weight, bias, x, gain, shift, at):
    rows, width = o.shape
    tm = rows // 2

    def body(o_ref, w_ref, b_ref, x_ref, g_ref, s_ref, x1_ref, a_ref):
        x1 = x_ref[...].astype(jnp.float32) + (dot(o_ref[...], w_ref[...]) + b_ref[...])
        x1_ref[...] = x1
        xhat, _ = row_stats(x1)
        a_ref[...] = (xhat * g_ref[...] + s_ref[...]).astype(jnp.bfloat16)

    rowblk = pl.BlockSpec((tm, width), lambda i: (i, 0))
    vec = whole((1, width))
    return pl.pallas_call(
        body,
        grid=(rows // tm,),
        in_specs=[rowblk, pl.BlockSpec((width, width), lambda i: (0, at // width)), vec, rowblk, vec, vec],
        out_specs=[rowblk, rowblk],
        out_shape=[
            jax.ShapeDtypeStruct((rows, width), jnp.float32),
            jax.ShapeDtypeStruct((rows, width), jnp.bfloat16),
        ],
        name="project_norm",
    )(o, weight, bias, x, gain, shift)


def feed_forward(a, up, up_bias, down, down_bias, x1, tf):
    rows, width = a.shape
    hidden = up.shape[1]
    steps = hidden // tf

    def body(a_ref, u_ref, ub_ref, d_ref, db_ref, x_ref, g_ref, gp_ref, y_ref, acc):
        j = pl.program_id(0)
        u = dot(a_ref[...], u_ref[...]) + ub_ref[...]
        phi, bell = normal_tail(u)
        g = (u * phi).astype(jnp.bfloat16)
        g_ref[...] = g
        gp_ref[...] = (phi + (u * RSQRT_2PI) * bell).astype(jnp.bfloat16)

        @pl.when(j == 0)
        def _():
            acc[...] = x_ref[...] + db_ref[...]

        acc[...] += dot(g, d_ref[...])

        @pl.when(j == steps - 1)
        def _():
            y_ref[...] = acc[...].astype(jnp.bfloat16)

    return pl.pallas_call(
        body,
        grid=(steps,),
        in_specs=[
            whole((rows, width)),
            pl.BlockSpec((width, tf), lambda j: (0, j)),
            pl.BlockSpec((1, tf), lambda j: (0, j)),
            pl.BlockSpec((tf, width), lambda j: (j, 0)),
            whole((1, width)),
            whole((rows, width)),
        ],
        out_specs=[
            pl.BlockSpec((rows, tf), lambda j: (0, j)),
            pl.BlockSpec((rows, tf), lambda j: (0, j)),
            whole((rows, width)),
        ],
        out_shape=[
            jax.ShapeDtypeStruct((rows, hidden), jnp.bfloat16),
            jax.ShapeDtypeStruct((rows, hidden), jnp.bfloat16),
            jax.ShapeDtypeStruct((rows, width), jnp.bfloat16),
        ],
        scratch_shapes=[pltpu.VMEM((rows, width), jnp.float32)],
        name="feed_forward",
    )(a, up, up_bias, down, down_bias, x1)


def feed_forward_back(dy, gp, down, up, x1, gain, w_out, at, tf):
    rows, width = dy.shape
    hidden = gp.shape[1]
    steps = hidden // tf

    def body(
        dy_ref, gp_ref, d_ref, u_ref, x_ref, g_ref, w_ref,
        dm_ref, du_ref, dx_ref, da_ref, do_ref, cdm_ref, cdu_ref, cda_ref, cg_ref, cs_ref, acc,
    ):
        j = pl.program_id(0)

        @pl.when(j == 0)
        def _():
            low = dy_ref[...].astype(jnp.bfloat16)
            dm_ref[...] = low
            cdm_ref[...] = jnp.sum(low.astype(jnp.float32), axis=0, keepdims=True)
            acc[...] = jnp.zeros_like(acc)

        du = (dot(dm_ref[...], d_ref[...], NT) * gp_ref[...].astype(jnp.float32)).astype(jnp.bfloat16)
        du_ref[...] = du
        cdu_ref[...] = jnp.sum(du.astype(jnp.float32), axis=0, keepdims=True)
        acc[...] += dot(du, u_ref[...], NT)

        @pl.when(j == steps - 1)
        def _():
            da2 = acc[...]
            xhat, inv = row_stats(x_ref[...])
            cg_ref[...] = jnp.sum(da2 * xhat, axis=0, keepdims=True)
            cs_ref[...] = jnp.sum(da2, axis=0, keepdims=True)
            t = da2 * g_ref[...]
            m1 = jnp.mean(t, axis=-1, keepdims=True)
            m2 = jnp.mean(t * xhat, axis=-1, keepdims=True)
            dx1 = dy_ref[...] + inv * (t - m1 - xhat * m2)
            dx_ref[...] = dx1
            low = dx1.astype(jnp.bfloat16)
            da_ref[...] = low
            cda_ref[...] = jnp.sum(low.astype(jnp.float32), axis=0, keepdims=True)
            do_ref[...] = dot(low, w_ref[...], NT).astype(jnp.bfloat16)

    full = whole((rows, width))
    vec = whole((1, width))
    f = lambda s, d: jax.ShapeDtypeStruct(s, d)
    return pl.pallas_call(
        body,
        grid=(steps,),
        in_specs=[
            full,
            pl.BlockSpec((rows, tf), lambda j: (0, j)),
            pl.BlockSpec((tf, width), lambda j: (j, 0)),
            pl.BlockSpec((width, tf), lambda j: (0, j)),
            full,
            vec,
            pl.BlockSpec((width, width), lambda j: (0, at // width)),
        ],
        out_specs=[
            full,
            pl.BlockSpec((rows, tf), lambda j: (0, j)),
            full,
            full,
            full,
            vec,
            pl.BlockSpec((1, tf), lambda j: (0, j)),
            vec,
            vec,
            vec,
        ],
        out_shape=[
            f((rows, width), jnp.bfloat16),
            f((rows, hidden), jnp.bfloat16),
            f((rows, width), jnp.float32),
            f((rows, width), jnp.bfloat16),
            f((rows, width), jnp.bfloat16),
            f((1, width), jnp.float32),
            f((1, hidden), jnp.float32),
            f((1, width), jnp.float32),
            f((1, width), jnp.float32),
            f((1, width), jnp.float32),
        ],
        scratch_shapes=[pltpu.VMEM((rows, width), jnp.float32)],
        name="feed_forward_back",
    )(dy, gp, down, up, x1, gain, w_out)


def project_back(grads, weight, x, gain, dx1, extra, out_dtype):
    rows, width = x.shape
    tm = rows // 2
    have = extra is not None
    count = len(grads)
    part = width // count

    def body(*refs):
        d_refs = refs[:count]
        w_ref, x_ref, g_ref, dx_ref = refs[count : count + 4]
        more = refs[count + 4 : -3]
        out_ref, cg_ref, cs_ref = refs[-3:]
        da = None
        for kind in range(3):
            for i in range(count):
                at = kind * width + i * part
                term = dot(d_refs[i][kind], w_ref[:, at : at + part], NT)
                da = term if da is None else da + term
        xhat, inv = row_stats(x_ref[...].astype(jnp.float32))
        cg = jnp.sum(da * xhat, axis=0, keepdims=True)
        cs = jnp.sum(da, axis=0, keepdims=True)

        @pl.when(pl.program_id(0) == 0)
        def _():
            cg_ref[...] = cg
            cs_ref[...] = cs

        @pl.when(pl.program_id(0) > 0)
        def _():
            cg_ref[...] += cg
            cs_ref[...] += cs

        t = da * g_ref[...]
        m1 = jnp.mean(t, axis=-1, keepdims=True)
        m2 = jnp.mean(t * xhat, axis=-1, keepdims=True)
        dx = dx_ref[...] + inv * (t - m1 - xhat * m2)
        if have:
            dx = more[0][...].astype(jnp.float32) * more[1][...] + dx
        out_ref[...] = dx.astype(out_dtype)

    rowblk = pl.BlockSpec((tm, width), lambda i: (i, 0))
    vec_spec = whole((1, width))
    specs = [pl.BlockSpec((3, tm, part), lambda i: (0, i, 0))] * count
    specs += [whole((width, 3 * width)), rowblk, vec_spec, rowblk]
    args = list(grads) + [weight, x, gain, dx1]
    if have:
        specs += [rowblk, pl.BlockSpec((tm, 1), lambda i: (i, 0))]
        args += list(extra)
    return pl.pallas_call(
        body,
        grid=(rows // tm,),
        in_specs=specs,
        out_specs=[rowblk, vec_spec, vec_spec],
        out_shape=[
            jax.ShapeDtypeStruct((rows, width), out_dtype),
            jax.ShapeDtypeStruct((1, width), jnp.float32),
            jax.ShapeDtypeStruct((1, width), jnp.float32),
        ],
        name="project_back",
    )(*args)


def weight_grad_half(lefts, rights, index, blocks, tn, arrived=None):
    rows, m = lefts[0].shape
    stacked = rights[0].ndim == 3
    part = rights[0].shape[-1]
    cols = part * 3 if stacked else part
    ndp, nfs, r = blocks
    tiles = ndp // 2
    wide = nfs * r
    count = len(lefts)
    npos = tiles * nfs
    final = arrived is not None
    take = (lambda ref: ref[0]) if stacked else (lambda ref: ref[...])
    if stacked:
        right = pl.BlockSpec((1, rows, tn), lambda j, i_ref: (j * tn // part, 0, j % (part // tn)))
    else:
        right = pl.BlockSpec((rows, tn), lambda j, i_ref: (0, j))

    def body(i_ref, *refs):
        a = refs[: count * tiles]
        b = refs[count * tiles : count * tiles + count]
        rest = refs[count * tiles + count :]
        scr = rest[-1]
        outs = rest[1:-1] if final else rest[:-1]
        for t in range(tiles):
            total = dot(a[t][...], take(b[0]), TN)
            for s in range(1, count):
                total += dot(a[s * tiles + t][...], take(b[s]), TN)
            for f in range(nfs):
                scr[t * nfs + f] = total[f * r : (f + 1) * r]
        for p in range(npos):
            value = scr[i_ref[tiles + p]]
            if final:
                value += rest[0][p].astype(jnp.float32)
            share = npos // len(outs)
            outs[p // share][p % share] = value.astype(jnp.bfloat16)

    left_spec = lambda t: pl.BlockSpec((rows, wide), lambda j, i_ref: (0, i_ref[t]))
    share = npos // 2 if final else npos
    specs = [left_spec(t) for _ in range(count) for t in range(tiles)]
    specs += [right] * count
    args = [left for left in lefts for _ in range(tiles)] + list(rights)
    if final:
        specs.append(pl.BlockSpec((npos, r, tn), lambda j, i_ref: (0, 0, j)))
        args.append(arrived)
    return pl.pallas_call(
        body,
        grid_spec=pltpu.PrefetchScalarGridSpec(
            num_scalar_prefetch=1,
            grid=(cols // tn,),
            in_specs=specs,
            out_specs=[pl.BlockSpec((share, r, tn), lambda j, i_ref: (0, 0, j))] * (npos // share),
            scratch_shapes=[pltpu.VMEM((npos, r, tn), jnp.float32)],
        ),
        out_shape=[jax.ShapeDtypeStruct((share, r, cols), jnp.bfloat16)] * (npos // share),
        name="weight_grad",
    )(index, *args)


def bits_of(ndp, nfs):
    core = nfs
    outer = [nfs << i for i in range(1, ndp.bit_length() - 1)]
    inner = [1 << i for i in range(nfs.bit_length() - 1)]
    return core, outer, inner


def stage_orders(ndp, nfs):
    core, outer, inner = bits_of(ndp, nfs)
    first, second = outer[0], inner[0]
    tail = outer[1:] + inner[1:]
    return core, ([first, second] + tail, [second, first] + tail)


def shard_table(ndp, nfs):
    n = ndp * nfs
    core, orders = stage_orders(ndp, nfs)
    table = np.zeros((n, n), np.int32)
    for me in range(n):
        for p in range(n):
            rel = core if p >= n // 2 else 0
            owner = 1 if (me ^ rel) & core else 0
            for i, mask in enumerate(orders[owner]):
                if p & (n >> (i + 2)):
                    rel ^= mask
            table[me, p] = me ^ rel
    return table


def stage_perms(ndp, nfs):
    n = ndp * nfs
    core, orders = stage_orders(ndp, nfs)
    perms = [[(i, i ^ core) for i in range(n)]]
    for a, b in zip(*orders):
        perms.append([(i, i ^ (b if i & core else a)) for i in range(n)])
    return perms


AXES = ("dp", "fsdp")


def send(x, perm):
    return lax.ppermute(x, AXES, perm)


class Line:
    def __init__(self):
        self.last = None

    def after(self, *arrays):
        if self.last is not None:
            arrays = lax.optimization_barrier((self.last,) + arrays)[1:]
        return arrays

    def mark(self, array):
        self.last = array


def place_shards(groups, table_row, shapes, slots):
    n = sum(p.shape[0] for p in groups[0])
    count = len(groups)

    def body(t_ref, *refs):
        ins = refs[: 4 * count]
        outs = refs[4 * count : 4 * count + len(shapes)]
        bufs = refs[4 * count + len(shapes) : -2]
        in_sem, out_sem = refs[-2:]
        loads, stores = [], []
        for i in range(count):
            which, middle, col = slots[i]
            width = bufs[i].shape[-1]
            for p in range(n):
                piece = ins[4 * i + p // (n // 4)]
                loads.append(
                    pltpu.make_async_copy(piece.at[p % (n // 4)], bufs[i].at[p], in_sem.at[i, p])
                )
                target = outs[which].at[t_ref[p]]
                if middle is not None:
                    target = target.at[middle]
                stores.append(
                    pltpu.make_async_copy(
                        bufs[i].at[p], target.at[:, col : col + width], out_sem.at[i, p]
                    )
                )
        for c in loads:
            c.start()
        for a, b in zip(loads, stores):
            a.wait()
            b.start()
        for b in stores:
            b.wait()

    flat = [p for g in groups for p in g]
    anywhere = pl.BlockSpec(memory_space=pl.ANY)
    return pl.pallas_call(
        body,
        out_shape=[jax.ShapeDtypeStruct(s, jnp.bfloat16) for s in shapes],
        grid_spec=pltpu.PrefetchScalarGridSpec(
            num_scalar_prefetch=1,
            in_specs=[anywhere] * len(flat),
            out_specs=[anywhere] * len(shapes),
            scratch_shapes=[pltpu.VMEM((n,) + g[0].shape[1:], jnp.bfloat16) for g in groups]
            + [pltpu.SemaphoreType.DMA((count, n))] * 2,
        ),
        name="place_shards",
    )(table_row, *flat)


def unpack_vectors(got, inverse_row, sizes, layout):
    n = got.shape[0]

    def body(i_ref, got_ref, *outs):
        for rows, out in zip(layout, outs):
            col = 0
            for r in rows:
                k = sizes[0] if r is None else sizes[r]
                per = 128 // k if k < 128 else 1
                for d in range(0, n, per):
                    if r is None:
                        value = jnp.zeros((1, per * k), jnp.float32)
                    else:
                        value = jnp.concatenate(
                            [got_ref[i_ref[d + e], r : r + 1, 0:k] for e in range(per)], axis=1
                        )
                    out[0:1, col + d * k : col + (d + per) * k] = value
                col += n * k

    widths = [sum(n * (sizes[0] if r is None else sizes[r]) for r in rows) for rows in layout]
    return pl.pallas_call(
        body,
        grid_spec=pltpu.PrefetchScalarGridSpec(
            num_scalar_prefetch=1,
            grid=(1,),
            in_specs=[whole(got.shape)],
            out_specs=[whole((1, w)) for w in widths],
        ),
        out_shape=[jax.ShapeDtypeStruct((1, w), jnp.float32) for w in widths],
        name="unpack_vectors",
    )(inverse_row, got)


def pack_sums(parts, inverse_row, n, rows):
    flat = [a for group in parts for a in group]

    def body(i_ref, *refs):
        out = refs[-1]
        out[...] = jnp.zeros_like(out)
        at = 0
        for r, group in enumerate(parts):
            total = refs[at][...]
            for k in range(1, len(group)):
                total += refs[at + k][...]
            at += len(group)
            k = total.shape[1] // n
            for d in range(n):
                out[i_ref[d], r : r + 1, 0:k] = total[:, d * k : (d + 1) * k]

    return pl.pallas_call(
        body,
        grid_spec=pltpu.PrefetchScalarGridSpec(
            num_scalar_prefetch=1,
            grid=(1,),
            in_specs=[whole(a.shape) for a in flat],
            out_specs=whole((n, rows, 128)),
        ),
        out_shape=jax.ShapeDtypeStruct((n, rows, 128), jnp.float32),
        name="pack_sums",
    )(inverse_row, *flat)


class Reduction:
    def __init__(self, perms, kept, sent, stage):
        self.perms, self.stage = perms, stage
        self.kept, self.got = kept, send(sent, perms[stage])
        self.done = None

    def step(self, line, wide=jnp.bfloat16):
        kept, got = line.after(self.kept, self.got)
        total = kept.astype(jnp.float32) + got.astype(jnp.float32)
        self.stage += 1
        if self.stage == len(self.perms):
            self.done = total[0]
            line.mark(self.done)
            return
        total = total.astype(wide)
        half = total.shape[0] // 2
        sent = total[half:]
        self.kept = total[:half]
        line.mark(sent)
        self.got = send(sent, self.perms[self.stage])


def per_device(ndp, nfs,
    tokens,
    ln1_gain,
    ln1_bias,
    w_qkv,
    bias_q,
    bias_v,
    w_out,
    bias_out,
    ln2_gain,
    ln2_bias,
    w_up,
    bias_up,
    w_down,
    bias_down,
    cot_first,
    cot_second,
    valid,
):
    n = ndp * nfs
    perms = stage_perms(ndp, nfs)
    gather_perms = perms[:0:-1]
    core_perm = perms[0]
    stages = len(gather_perms)
    table = shard_table(ndp, nfs)
    me = lax.axis_index("dp") * nfs + lax.axis_index("fsdp")
    both = np.concatenate([table, np.argsort(table, axis=1).astype(np.int32)], axis=1)
    both = lax.dynamic_slice(jnp.asarray(both), (me, 0), (1, 2 * n))[0]
    row, inverse_row = both[:n], both[n:]
    rows_in, width = tokens.shape[1:]
    r_in, r_ff = w_up.shape[0], w_down.shape[0]
    hidden = w_up.shape[1]
    half_ff = r_ff // 2

    vectors = (ln1_gain, ln1_bias, bias_q, bias_v, bias_out, ln2_gain, ln2_bias, bias_down, bias_up)
    sizes = [v.shape[0] for v in vectors]
    packed = jnp.stack([jnp.pad(v.astype(jnp.float32), (0, 128 - v.shape[0])) for v in vectors])

    line = Line()
    first_cols = jnp.concatenate([w_qkv, w_out], axis=1)
    mid = first_cols.shape[1] // 2
    shards = [
        first_cols[:, :mid],
        first_cols[:, mid:],
        w_up[:, : hidden // 2],
        w_up[:, hidden // 2 :],
        w_down[:half_ff],
        w_down[half_ff:],
    ]
    small = packed[None]
    held = [s[None] for s in shards]
    got = [None] * len(shards)
    pieces = [None] * len(shards)

    def gather_round(index):
        nonlocal small
        for i in range(len(shards)):
            k = index - i
            if k < 0 or k > stages:
                continue
            if 0 < k < stages:
                mine, theirs = line.after(held[i], got[i])
                held[i] = jnp.concatenate([mine, theirs], axis=0)
                line.mark(held[i])
            if k < stages:
                got[i] = send(held[i], gather_perms[k])
            if k == stages - 1:
                pieces[i] = [held[i], None, send(held[i], core_perm), None]
            if k == stages:
                pieces[i][1] = got[i]
                pieces[i][3] = send(got[i], core_perm)
        if index < stages:
            theirs = send(small, gather_perms[index])
            small = jnp.concatenate([small, theirs], axis=0)
        elif index == stages:
            small = jnp.concatenate([small, send(small, core_perm)], axis=0)

    def place(which, shapes, slots):
        flat = [p for i in which for p in pieces[i]]
        flat = line.after(*flat)
        groups = [flat[4 * i : 4 * i + 4] for i in range(len(which))]
        outs = place_shards(groups, row, shapes, slots)
        line.mark(outs[0])
        return outs

    w = {}
    for index in range(stages + 2):
        gather_round(index)
    g1, s1, bqkv, bo, g2, s2, bd, bu = unpack_vectors(
        small, inverse_row, sizes, [[0], [1], [2, None, 3], [4], [5], [6], [7], [8]]
    )
    qkv_cols = w_qkv.shape[1]
    (first_full,) = place([0, 1], [(n, r_in, 2 * mid)], [(0, None, 0), (0, None, mid)])
    first_full = first_full.reshape(n * r_in, 2 * mid)
    w["first"] = first_full

    def forward(x, before=None):
        a1, qkv = norm_project(*line.after(x), g1, s1, w["first"], bqkv, 512, qkv_cols)
        line.mark(a1)
        if before:
            before()
        o, logs = attention(*line.after(qkv))
        line.mark(o)
        if before:
            before()
        x1, a2 = project_norm(*line.after(o), w["first"], bo, x, g2, s2, qkv_cols)
        line.mark(a2)
        if before:
            before()
        a2 = line.after(a2)[0]
        g, gp, y = feed_forward(a2, w["up"], bu, w["down"], bd, x1, 512)
        line.mark(y)
        return y, (x, a1, qkv, logs, o, x1, a2, g, gp)

    calls = [0]

    def more():
        calls[0] += 1
        gather_round(stages + 1 + calls[0])
        if calls[0] == 2:
            (up,) = place([2, 3], [(n, r_in, hidden)], [(0, None, 0), (0, None, hidden // 2)])
            w["up"] = up.reshape(n * r_in, hidden)
        if calls[0] == 3:
            gather_round(stages + 5)
            (down,) = place([4, 5], [(n, 2, half_ff, width)], [(0, 0, 0), (0, 1, 0)])
            w["down"] = down.reshape(n * r_ff, width)

    first, saved_first = forward(tokens[0], more)
    second, saved_second = forward(first)

    keep_mask = valid[0].astype(jnp.float32)[:, None]
    grad_second = cot_second[0].astype(jnp.float32) * keep_mask
    pairs = width // (2 * HEAD_DIM)
    parts = 2

    def ff_back(dy, saved):
        x, a1, qkv, logs, o, x1, a2, g, gp = saved
        outs = feed_forward_back(
            *line.after(dy), gp, w["down"], w["up"], x1, g2, w["first"], qkv_cols, 512
        )
        line.mark(outs[0])
        return outs

    def heads_back(saved, d_o, i):
        outs = attention_back(
            saved[2], saved[3], *line.after(d_o), i * pairs // parts, pairs // parts
        )
        line.mark(outs[0])
        return outs

    def qkv_back(heads, saved, dx1, extra, dtype):
        dx, cg, cs = project_back(
            [line.after(h[0])[0] for h in heads], w["first"], saved[0], g1, dx1, extra, dtype
        )
        line.mark(dx)
        return dx, cg, cs

    dm2, du2, dx2, da2, do2, cdm2, cdu2, cda2, cg22, cs22 = ff_back(grad_second, saved_second)
    heads2 = [heads_back(saved_second, do2, i) for i in range(parts)]
    grad_first, cg12, cs12 = qkv_back(
        heads2, saved_second, dx2, (cot_first[0], keep_mask), jnp.float32
    )

    local = (row // nfs) // 2 * nfs + row % nfs
    half = n // 2
    tiles = ndp // 2
    core = (me // nfs) % 2
    lanes = 2 * jnp.arange(tiles, dtype=jnp.int32)
    index_keep = jnp.concatenate([lanes + core, local[:half]]).astype(jnp.int32)
    index_send = jnp.concatenate([lanes + (1 - core), local[half:]]).astype(jnp.int32)

    def grad_send(lefts, rights, r, tn):
        lefts = line.after(*lefts)
        (out,) = weight_grad_half(lefts, rights, index_send, (ndp, nfs, r), tn)
        line.mark(out)
        return send(out, core_perm)

    def grad_keep(lefts, rights, r, tn, arrived):
        arrived = line.after(arrived)[0]
        kept, sent = weight_grad_half(lefts, rights, index_keep, (ndp, nfs, r), tn, arrived)
        line.mark(sent)
        return kept, sent

    dm1 = grad_first.astype(jnp.bfloat16)
    sg = list(zip(saved_first, saved_second))
    arrived = grad_send(sg[7], (dm1, dm2), r_ff, 256)
    red_down = Reduction(perms, *grad_keep(sg[7], (dm1, dm2), r_ff, 256, arrived), 1)
    _, du1, dx1, da1, do1, cdm1, cdu1, cda1, cg21, cs21 = ff_back(grad_first, saved_first)
    red_down.step(line)
    arrived = grad_send(sg[6], (du1, du2), r_in, 1024)
    red_down.step(line)
    red_up = Reduction(perms, *grad_keep(sg[6], (du1, du2), r_in, 1024, arrived), 1)
    red_down.step(line)
    arrived_out = grad_send(sg[4], (da1, da2), r_in, 1024)
    heads1 = [heads_back(saved_first, do1, 0)]
    kept_out, sent_out = grad_keep(sg[4], (da1, da2), r_in, 1024, arrived_out)
    red_down.step(line)
    rights = lambda i: (heads1[i][0], heads2[i][0])
    arrived = grad_send(sg[1], rights(0), r_in, 512)
    red_up.step(line)
    kept_q, sent_q = grad_keep(sg[1], rights(0), r_in, 512, arrived)
    red_one = Reduction(
        perms,
        jnp.concatenate([kept_out, kept_q], axis=2),
        jnp.concatenate([sent_out, sent_q], axis=2),
        1,
    )
    heads1.append(heads_back(saved_first, do1, 1))
    red_up.step(line)
    arrived = grad_send(sg[1], rights(1), r_in, 512)
    red_two = Reduction(perms, *grad_keep(sg[1], rights(1), r_in, 512, arrived), 1)
    red_one.step(line)
    red_up.step(line)
    grad_inputs, cg11, cs11 = qkv_back(heads1, saved_first, dx1, None, jnp.bfloat16)
    red_one.step(line)
    red_two.step(line)
    cq = [[h[i][1] for h in (heads1, heads2)] for i in range(parts)]
    cv = [[h[i][2] for h in (heads1, heads2)] for i in range(parts)]
    joined = lambda c: [jnp.concatenate([c[i][s] for i in range(parts)], axis=1) for s in range(2)]
    sums = pack_sums(
        [
            [cg11, cg12],
            [cs11, cs12],
            joined(cq),
            joined(cv),
            [cda1, cda2],
            [cg21, cg22],
            [cs21, cs22],
            [cdm1, cdm2],
            [cdu1, cdu2],
        ],
        inverse_row,
        n,
        len(vectors),
    )
    red_small = Reduction(perms, sums[:half], sums[half:], 0)
    red_up.step(line)
    for _ in range(stages):
        for red in (red_one, red_two):
            if red.done is None:
                red.step(line)
        if red_small.done is None:
            red_small.step(line, jnp.float32)
    for red in (red_down, red_up, red_one, red_two):
        while red.done is None:
            red.step(line)
    while red_small.done is None:
        red_small.step(line, jnp.float32)
    outs = [red_small.done[i, : sizes[i]] for i in range(len(vectors))]
    o_g1, o_s1, o_bq, o_bv, o_bo, o_g2, o_s2, o_bd, o_bu = outs
    one = red_one.done
    d_out = one[:, :width]
    third = width // parts
    blocks = []
    for kind in range(3):
        blocks.append(one[:, width + kind * third : width + (kind + 1) * third])
        blocks.append(red_two.done[:, kind * third : (kind + 1) * third])
    d_qkv = jnp.concatenate(blocks, axis=1)
    return (
        first[None],
        second[None],
        grad_inputs[None],
        o_g1,
        o_s1,
        d_qkv,
        o_bq,
        o_bv,
        d_out,
        o_bo,
        o_g2,
        o_s2,
        red_up.done,
        o_bu,
        red_down.done,
        o_bd,
    )


def solution(mesh):
    ndp, nfs = mesh.shape["dp"], mesh.shape["fsdp"]
    return jax.shard_map(
        partial(per_device, ndp, nfs),
        mesh=mesh,
        in_specs=(
            P(("dp", "fsdp"), None, None),
            P(("dp", "fsdp")),
            P(("dp", "fsdp")),
            P(("dp", "fsdp"), None),
            P(("dp", "fsdp")),
            P(("dp", "fsdp")),
            P(("dp", "fsdp"), None),
            P(("dp", "fsdp")),
            P(("dp", "fsdp")),
            P(("dp", "fsdp")),
            P(("dp", "fsdp"), None),
            P(("dp", "fsdp")),
            P(("dp", "fsdp"), None),
            P(("dp", "fsdp")),
            P(("dp", "fsdp"), None, None),
            P(("dp", "fsdp"), None, None),
            P(("dp", "fsdp"), None),
        ),
        out_specs=(
            P(("dp", "fsdp"), None, None),
            P(("dp", "fsdp"), None, None),
            P(("dp", "fsdp"), None, None),
            P(("dp", "fsdp")),
            P(("dp", "fsdp")),
            P(("dp", "fsdp"), None),
            P(("dp", "fsdp")),
            P(("dp", "fsdp")),
            P(("dp", "fsdp"), None),
            P(("dp", "fsdp")),
            P(("dp", "fsdp")),
            P(("dp", "fsdp")),
            P(("dp", "fsdp"), None),
            P(("dp", "fsdp")),
            P(("dp", "fsdp"), None),
            P(("dp", "fsdp")),
        ),
        check_vma=False,
    )
```

```python
from functools import partial

import numpy as np
import jax
import jax.numpy as jnp
from jax import lax
from jax.experimental import pallas as pl
from jax.experimental.pallas import tpu as pltpu
from jax.sharding import PartitionSpec as P

CHEAP = pl.CostEstimate(flops=1, transcendentals=0, bytes_accessed=1)
call = partial(pl.pallas_call, cost_estimate=CHEAP)


EPSILON = 1e-06
HEAD_DIM = 64
LOG2E = 1.4426950408889634
RSQRT_2PI = 0.3989422804014327
SQRT_HALF = 0.7071067811865476
SCORE_SCALE = HEAD_DIM**-0.5 * LOG2E
NT = (((1,), (1,)), ((), ()))
TN = (((0,), (0,)), ((), ()))


def dot(a, b, dims=(((1,), (0,)), ((), ()))):
    return lax.dot_general(a, b, dims, preferred_element_type=jnp.float32)


def whole(shape):
    return pl.BlockSpec(shape, lambda *_: (0,) * len(shape))


def normal_cdf(u):
    return 0.5 + 0.5 * lax.erf(u * SQRT_HALF), jnp.exp2((-0.5 * LOG2E) * (u * u))


def row_stats(v):
    centre = v - jnp.mean(v, axis=-1, keepdims=True)
    inv = lax.rsqrt(jnp.mean(centre * centre, axis=-1, keepdims=True) + EPSILON)
    return centre * inv, inv


def norm_project(x, gain, shift, weight, bias, tn, cols):
    rows, width = x.shape

    def body(x_ref, g_ref, s_ref, w_ref, b_ref, a_ref, o_ref):
        @pl.when(pl.program_id(0) == 0)
        def _():
            xhat, _ = row_stats(x_ref[...].astype(jnp.float32))
            a_ref[...] = (xhat * g_ref[...] + s_ref[...]).astype(jnp.bfloat16)

        o_ref[...] = (dot(a_ref[...], w_ref[...]) + b_ref[...]).astype(jnp.bfloat16)

    return call(
        body,
        grid=(cols // tn,),
        in_specs=[
            whole((rows, width)),
            whole((1, width)),
            whole((1, width)),
            pl.BlockSpec((width, tn), lambda j: (0, j)),
            pl.BlockSpec((1, tn), lambda j: (0, j)),
        ],
        out_specs=[whole((rows, width)), pl.BlockSpec((rows, tn), lambda j: (0, j))],
        out_shape=[
            jax.ShapeDtypeStruct((rows, width), jnp.bfloat16),
            jax.ShapeDtypeStruct((rows, cols), jnp.bfloat16),
        ],
        name="norm_project",
    )(x, gain, shift, weight, bias)


def attention(qkv):
    rows, width = qkv.shape[0], qkv.shape[1] // 3
    pairs = width // (2 * HEAD_DIM)
    span = 2 * HEAD_DIM

    def body(q_ref, k_ref, v_ref, o_ref, l_ref):
        q, k, v = q_ref[...], k_ref[...], v_ref[...]
        lane = lax.broadcasted_iota(jnp.int32, (rows, span), 1)
        outs, logs = [], []
        for h in range(2):
            mine = (lane < HEAD_DIM) if h == 0 else (lane >= HEAD_DIM)
            kh = jnp.where(mine, k, jnp.zeros_like(k))
            s = dot(q, kh, NT)
            top = jnp.max(s, axis=-1, keepdims=True) * SCORE_SCALE
            e = jnp.exp2(s * SCORE_SCALE - top)
            total = jnp.sum(e, axis=-1, keepdims=True)
            outs.append(dot(e.astype(jnp.bfloat16), v) * (1.0 / total))
            logs.append(top + jnp.log2(total))
        first = lane < HEAD_DIM
        o_ref[...] = jnp.where(first, outs[0], outs[1]).astype(jnp.bfloat16)
        both = jnp.where(first, logs[0], logs[1])
        turned = both.T
        l_ref[0, 0:1, :] = turned[0:1, :]
        l_ref[0, 1:2, :] = turned[HEAD_DIM : HEAD_DIM + 1, :]

    col = lambda base: pl.BlockSpec((rows, span), lambda j: (0, base + j))
    return call(
        body,
        grid=(pairs,),
        in_specs=[col(0), col(pairs), col(2 * pairs)],
        out_specs=[col(0), pl.BlockSpec((1, 8, rows), lambda j: (j, 0, 0))],
        out_shape=[
            jax.ShapeDtypeStruct((rows, width), jnp.bfloat16),
            jax.ShapeDtypeStruct((pairs, 8, rows), jnp.float32),
        ],
        name="attention",
    )(qkv, qkv, qkv)


def attention_back(qkv, logs, o, d_o, first_pair, pairs):
    rows, width = qkv.shape[0], qkv.shape[1] // 3
    every = width // (2 * HEAD_DIM)
    span = 2 * HEAD_DIM

    def body(q_ref, k_ref, v_ref, l_ref, o_ref, do_ref, d_ref, cq_ref, cv_ref):
        q, k, v, do = q_ref[...], k_ref[...], v_ref[...], do_ref[...]
        lane = lax.broadcasted_iota(jnp.int32, (rows, span), 1)
        turned = (do.astype(jnp.float32) * o_ref[...].astype(jnp.float32)).T
        dqs, dks, dvs = [], [], []
        for h in range(2):
            mine = (lane < HEAD_DIM) if h == 0 else (lane >= HEAD_DIM)
            kh = jnp.where(mine, k, jnp.zeros_like(k))
            vh = jnp.where(mine, v, jnp.zeros_like(v))
            pt = jnp.exp2(dot(kh, q, NT) * SCORE_SCALE - l_ref[0, h : h + 1, :])
            inner = jnp.sum(turned[h * HEAD_DIM : (h + 1) * HEAD_DIM], axis=0, keepdims=True)
            dst = (pt * (dot(vh, do, NT) - inner)).astype(jnp.bfloat16)
            dvs.append(dot(pt.astype(jnp.bfloat16), do))
            dks.append(dot(dst, q))
            dqs.append(dot(dst, k, TN))
        first = lane < HEAD_DIM
        dq = (jnp.where(first, dqs[0], dqs[1]) * 0.125).astype(jnp.bfloat16)
        dk = (jnp.where(first, dks[0], dks[1]) * 0.125).astype(jnp.bfloat16)
        dv = jnp.where(first, dvs[0], dvs[1]).astype(jnp.bfloat16)
        d_ref[0] = dq
        d_ref[1] = dk
        d_ref[2] = dv
        cq_ref[...] = jnp.sum(dq.astype(jnp.float32), axis=0, keepdims=True)
        cv_ref[...] = jnp.sum(dv.astype(jnp.float32), axis=0, keepdims=True)

    col = lambda base: pl.BlockSpec((rows, span), lambda j: (0, base + j))
    sums = pl.BlockSpec((1, span), lambda j: (0, j))
    vec_shape = jax.ShapeDtypeStruct((1, pairs * span), jnp.float32)
    return call(
        body,
        grid=(pairs,),
        in_specs=[
            col(first_pair),
            col(every + first_pair),
            col(2 * every + first_pair),
            pl.BlockSpec((1, 8, rows), lambda j: (first_pair + j, 0, 0)),
            col(first_pair),
            col(first_pair),
        ],
        out_specs=[pl.BlockSpec((3, rows, span), lambda j: (0, 0, j)), sums, sums],
        out_shape=[
            jax.ShapeDtypeStruct((3, rows, pairs * span), jnp.bfloat16),
            vec_shape,
            vec_shape,
        ],
        name="attention_back",
    )(qkv, qkv, qkv, logs, o, d_o)


def project_norm(o, weight, bias, x, gain, shift, at):
    rows, width = o.shape
    tm = rows // 2

    def body(o_ref, w_ref, b_ref, x_ref, g_ref, s_ref, x1_ref, a_ref):
        x1 = x_ref[...].astype(jnp.float32) + (dot(o_ref[...], w_ref[...]) + b_ref[...])
        x1_ref[...] = x1
        xhat, _ = row_stats(x1)
        a_ref[...] = (xhat * g_ref[...] + s_ref[...]).astype(jnp.bfloat16)

    rowblk = pl.BlockSpec((tm, width), lambda i: (i, 0))
    vec = whole((1, width))
    return call(
        body,
        grid=(rows // tm,),
        in_specs=[rowblk, pl.BlockSpec((width, width), lambda i: (0, at // width)), vec, rowblk, vec, vec],
        out_specs=[rowblk, rowblk],
        out_shape=[
            jax.ShapeDtypeStruct((rows, width), jnp.float32),
            jax.ShapeDtypeStruct((rows, width), jnp.bfloat16),
        ],
        name="project_norm",
    )(o, weight, bias, x, gain, shift)


def flat(ref):
    return ref[...].reshape(-1, ref.shape[-1])


def up_spec(packed, r_in):
    n, _, width = packed.shape
    return pl.BlockSpec((n, r_in, width), lambda j: (0, j, 0))


def down_spec(packed, r_ff):
    width = packed.shape[2]
    return pl.BlockSpec((width // r_ff, r_ff, width), lambda j: (j, 1, 0))


def feed_forward(a, packed, r_in, r_ff, up_bias, down_bias, x1):
    rows, width = a.shape
    hidden = up_bias.shape[1]
    tf = width
    steps = hidden // tf

    def body(a_ref, u_ref, ub_ref, d_ref, db_ref, x_ref, g_ref, gp_ref, y_ref, acc):
        j = pl.program_id(0)
        u = dot(a_ref[...], flat(u_ref)) + ub_ref[...]
        phi, bell = normal_cdf(u)
        g = (u * phi).astype(jnp.bfloat16)
        g_ref[...] = g
        gp_ref[...] = (phi + (u * RSQRT_2PI) * bell).astype(jnp.bfloat16)

        @pl.when(j == 0)
        def _():
            acc[...] = x_ref[...] + db_ref[...]

        acc[...] += dot(g, flat(d_ref))

        @pl.when(j == steps - 1)
        def _():
            y_ref[...] = acc[...].astype(jnp.bfloat16)

    return call(
        body,
        grid=(steps,),
        in_specs=[
            whole((rows, width)),
            up_spec(packed, r_in),
            pl.BlockSpec((1, tf), lambda j: (0, j)),
            down_spec(packed, r_ff),
            whole((1, width)),
            whole((rows, width)),
        ],
        out_specs=[
            pl.BlockSpec((rows, tf), lambda j: (0, j)),
            pl.BlockSpec((rows, tf), lambda j: (0, j)),
            whole((rows, width)),
        ],
        out_shape=[
            jax.ShapeDtypeStruct((rows, hidden), jnp.bfloat16),
            jax.ShapeDtypeStruct((rows, hidden), jnp.bfloat16),
            jax.ShapeDtypeStruct((rows, width), jnp.bfloat16),
        ],
        scratch_shapes=[pltpu.VMEM((rows, width), jnp.float32)],
        name="feed_forward",
    )(a, packed, up_bias, packed, down_bias, x1)


def feed_forward_back(dy, gp, packed, r_in, r_ff, x1, gain, w_out, at):
    rows, width = dy.shape
    hidden = gp.shape[1]
    tf = width
    steps = hidden // tf

    def body(
        dy_ref, gp_ref, d_ref, u_ref, x_ref, g_ref, w_ref,
        dm_ref, du_ref, dx_ref, da_ref, do_ref, cdm_ref, cdu_ref, cda_ref, cg_ref, cs_ref, acc,
    ):
        j = pl.program_id(0)

        @pl.when(j == 0)
        def _():
            low = dy_ref[...].astype(jnp.bfloat16)
            dm_ref[...] = low
            cdm_ref[...] = jnp.sum(low.astype(jnp.float32), axis=0, keepdims=True)
            acc[...] = jnp.zeros_like(acc)

        du = (dot(dm_ref[...], flat(d_ref), NT) * gp_ref[...].astype(jnp.float32)).astype(jnp.bfloat16)
        du_ref[...] = du
        cdu_ref[...] = jnp.sum(du.astype(jnp.float32), axis=0, keepdims=True)
        acc[...] += dot(du, flat(u_ref), NT)

        @pl.when(j == steps - 1)
        def _():
            da2 = acc[...]
            xhat, inv = row_stats(x_ref[...])
            cg_ref[...] = jnp.sum(da2 * xhat, axis=0, keepdims=True)
            cs_ref[...] = jnp.sum(da2, axis=0, keepdims=True)
            t = da2 * g_ref[...]
            m1 = jnp.mean(t, axis=-1, keepdims=True)
            m2 = jnp.mean(t * xhat, axis=-1, keepdims=True)
            dx1 = dy_ref[...] + inv * (t - m1 - xhat * m2)
            dx_ref[...] = dx1
            low = dx1.astype(jnp.bfloat16)
            da_ref[...] = low
            cda_ref[...] = jnp.sum(low.astype(jnp.float32), axis=0, keepdims=True)
            do_ref[...] = dot(low, w_ref[...], NT).astype(jnp.bfloat16)

    full = whole((rows, width))
    vec = whole((1, width))
    f = lambda s, d: jax.ShapeDtypeStruct(s, d)
    return call(
        body,
        grid=(steps,),
        in_specs=[
            full,
            pl.BlockSpec((rows, tf), lambda j: (0, j)),
            down_spec(packed, r_ff),
            up_spec(packed, r_in),
            full,
            vec,
            pl.BlockSpec((width, width), lambda j: (0, at // width)),
        ],
        out_specs=[
            full,
            pl.BlockSpec((rows, tf), lambda j: (0, j)),
            full,
            full,
            full,
            vec,
            pl.BlockSpec((1, tf), lambda j: (0, j)),
            vec,
            vec,
            vec,
        ],
        out_shape=[
            f((rows, width), jnp.bfloat16),
            f((rows, hidden), jnp.bfloat16),
            f((rows, width), jnp.float32),
            f((rows, width), jnp.bfloat16),
            f((rows, width), jnp.bfloat16),
            f((1, width), jnp.float32),
            f((1, hidden), jnp.float32),
            f((1, width), jnp.float32),
            f((1, width), jnp.float32),
            f((1, width), jnp.float32),
        ],
        scratch_shapes=[pltpu.VMEM((rows, width), jnp.float32)],
        name="feed_forward_back",
    )(dy, gp, packed, packed, x1, gain, w_out)


def project_back(grads, weight, x, gain, dx1, extra, out_dtype):
    rows, width = x.shape
    tm = rows // 2
    have = extra is not None
    count = len(grads)
    part = width // count

    def body(*refs):
        d_refs = refs[:count]
        w_ref, x_ref, g_ref, dx_ref = refs[count : count + 4]
        more = refs[count + 4 : -3]
        out_ref, cg_ref, cs_ref = refs[-3:]
        da = None
        for kind in range(3):
            for i in range(count):
                at = kind * width + i * part
                term = dot(d_refs[i][kind], w_ref[:, at : at + part], NT)
                da = term if da is None else da + term
        xhat, inv = row_stats(x_ref[...].astype(jnp.float32))
        cg = jnp.sum(da * xhat, axis=0, keepdims=True)
        cs = jnp.sum(da, axis=0, keepdims=True)

        @pl.when(pl.program_id(0) == 0)
        def _():
            cg_ref[...] = cg
            cs_ref[...] = cs

        @pl.when(pl.program_id(0) > 0)
        def _():
            cg_ref[...] += cg
            cs_ref[...] += cs

        t = da * g_ref[...]
        m1 = jnp.mean(t, axis=-1, keepdims=True)
        m2 = jnp.mean(t * xhat, axis=-1, keepdims=True)
        dx = dx_ref[...] + inv * (t - m1 - xhat * m2)
        if have:
            dx = more[0][...].astype(jnp.float32) * more[1][...] + dx
        out_ref[...] = dx.astype(out_dtype)

    rowblk = pl.BlockSpec((tm, width), lambda i: (i, 0))
    vec_spec = whole((1, width))
    specs = [pl.BlockSpec((3, tm, part), lambda i: (0, i, 0))] * count
    specs += [whole((width, 3 * width)), rowblk, vec_spec, rowblk]
    args = list(grads) + [weight, x, gain, dx1]
    if have:
        specs += [rowblk, pl.BlockSpec((tm, 1), lambda i: (i, 0))]
        args += list(extra)
    return call(
        body,
        grid=(rows // tm,),
        in_specs=specs,
        out_specs=[rowblk, vec_spec, vec_spec],
        out_shape=[
            jax.ShapeDtypeStruct((rows, width), out_dtype),
            jax.ShapeDtypeStruct((1, width), jnp.float32),
            jax.ShapeDtypeStruct((1, width), jnp.float32),
        ],
        name="project_back",
    )(*args)


def weight_grad_half(lefts, rights, index, blocks, tn, arrived=None):
    rows, m = lefts[0].shape
    stacked = rights[0].ndim == 3
    part = rights[0].shape[-1]
    cols = part * 3 if stacked else part
    ndp, nfs, r = blocks
    tiles = ndp // 2
    wide = nfs * r
    count = len(lefts)
    npos = tiles * nfs
    final = arrived is not None
    take = (lambda ref: ref[0]) if stacked else (lambda ref: ref[...])
    if stacked:
        right = pl.BlockSpec((1, rows, tn), lambda j, i_ref: (j * tn // part, 0, j % (part // tn)))
    else:
        right = pl.BlockSpec((rows, tn), lambda j, i_ref: (0, j))

    def body(i_ref, *refs):
        a = refs[: count * tiles]
        b = refs[count * tiles : count * tiles + count]
        rest = refs[count * tiles + count :]
        scr = rest[-1]
        outs = rest[1:-1] if final else rest[:-1]
        for t in range(tiles):
            total = dot(a[t][...], take(b[0]), TN)
            for s in range(1, count):
                total += dot(a[s * tiles + t][...], take(b[s]), TN)
            for f in range(nfs):
                scr[t * nfs + f] = total[f * r : (f + 1) * r]
        for p in range(npos):
            value = scr[i_ref[tiles + p]]
            if final:
                value += rest[0][p].astype(jnp.float32)
            share = npos // len(outs)
            outs[p // share][p % share] = value.astype(jnp.bfloat16)

    left_spec = lambda t: pl.BlockSpec((rows, wide), lambda j, i_ref: (0, i_ref[t]))
    share = npos // 2 if final else npos
    specs = [left_spec(t) for _ in range(count) for t in range(tiles)]
    specs += [right] * count
    args = [left for left in lefts for _ in range(tiles)] + list(rights)
    if final:
        specs.append(pl.BlockSpec((npos, r, tn), lambda j, i_ref: (0, 0, j)))
        args.append(arrived)
    return call(
        body,
        grid_spec=pltpu.PrefetchScalarGridSpec(
            num_scalar_prefetch=1,
            grid=(cols // tn,),
            in_specs=specs,
            out_specs=[pl.BlockSpec((share, r, tn), lambda j, i_ref: (0, 0, j))] * (npos // share),
            scratch_shapes=[pltpu.VMEM((npos, r, tn), jnp.float32)],
        ),
        out_shape=[jax.ShapeDtypeStruct((share, r, cols), jnp.bfloat16)] * (npos // share),
        name="weight_grad",
    )(index, *args)


def bits_of(ndp, nfs):
    core = nfs
    outer = [nfs << i for i in range(1, ndp.bit_length() - 1)]
    inner = [1 << i for i in range(nfs.bit_length() - 1)]
    return core, outer, inner


def stage_orders(ndp, nfs):
    core, outer, inner = bits_of(ndp, nfs)
    first, second = outer[0], inner[0]
    tail = outer[1:] + inner[1:]
    return core, ([first, second] + tail, [second, first] + tail)


def shard_table(ndp, nfs):
    n = ndp * nfs
    core, orders = stage_orders(ndp, nfs)
    table = np.zeros((n, n), np.int32)
    for me in range(n):
        for p in range(n):
            rel = core if p >= n // 2 else 0
            owner = 1 if (me ^ rel) & core else 0
            for i, mask in enumerate(orders[owner]):
                if p & (n >> (i + 2)):
                    rel ^= mask
            table[me, p] = me ^ rel
    return table


def stage_perms(ndp, nfs):
    n = ndp * nfs
    core, orders = stage_orders(ndp, nfs)
    perms = [[(i, i ^ core) for i in range(n)]]
    for a, b in zip(*orders):
        perms.append([(i, i ^ (b if i & core else a)) for i in range(n)])
    return perms


AXES = ("dp", "fsdp")


def send(x, perm):
    return lax.ppermute(x, AXES, perm)


class Line:
    def __init__(self):
        self.last = None

    def after(self, *arrays):
        if self.last is not None:
            arrays = lax.optimization_barrier((self.last,) + arrays)[1:]
        return arrays

    def mark(self, array):
        self.last = array


def place_shards(groups, table_row, shapes, slots):
    n = sum(p.shape[0] for p in groups[0])
    count = len(groups)

    def body(t_ref, *refs):
        ins = refs[: 4 * count]
        outs = refs[4 * count : 4 * count + len(shapes)]
        bufs = refs[4 * count + len(shapes) : -2]
        in_sem, out_sem = refs[-2:]
        loads, stores = [], []
        for i in range(count):
            which, middle, col = slots[i]
            width = bufs[i].shape[-1]
            for p in range(n):
                piece = ins[4 * i + p // (n // 4)].at[p % (n // 4), 0 : bufs[i].shape[1]]
                loads.append(pltpu.make_async_copy(piece, bufs[i].at[p], in_sem.at[i, p]))
                target = outs[which].at[t_ref[p]]
                if middle is not None:
                    target = target.at[middle]
                stores.append(
                    pltpu.make_async_copy(
                        bufs[i].at[p], target.at[:, col : col + width], out_sem.at[i, p]
                    )
                )
        for c in loads:
            c.start()
        for a, b in zip(loads, stores):
            a.wait()
            b.start()
        for b in stores:
            b.wait()

    flat = [p for g in groups for p in g]
    anywhere = pl.BlockSpec(memory_space=pl.ANY)
    return call(
        body,
        out_shape=[jax.ShapeDtypeStruct(s, jnp.bfloat16) for s in shapes],
        grid_spec=pltpu.PrefetchScalarGridSpec(
            num_scalar_prefetch=1,
            in_specs=[anywhere] * len(flat),
            out_specs=[anywhere] * len(shapes),
            scratch_shapes=[
                pltpu.VMEM((n, shapes[s[0]][-2], g[0].shape[-1]), jnp.bfloat16)
                for g, s in zip(groups, slots)
            ]
            + [pltpu.SemaphoreType.DMA((count, n))] * 2,
        ),
        name="place_shards",
    )(table_row, *flat)


def unpack_vectors(pieces, at, inverse_row, sizes, layout):
    per_piece = pieces[0].shape[0]
    n = per_piece * len(pieces)

    def body(i_ref, *refs):
        ins, outs, scr = refs[: len(pieces)], refs[len(pieces) : -1], refs[-1]
        for i, ref in enumerate(ins):
            scr[i * per_piece : (i + 1) * per_piece] = ref[...].astype(jnp.float32)
        for rows, out in zip(layout, outs):
            col = 0
            for r in rows:
                k = sizes[0] if r is None else sizes[r]
                per = 128 // k if k < 128 else 1
                for d in range(0, n, per):
                    if r is None:
                        value = jnp.zeros((1, per * k), jnp.float32)
                    else:
                        value = jnp.concatenate(
                            [scr[i_ref[d + e], 0:1, r * 128 : r * 128 + k] for e in range(per)],
                            axis=1,
                        )
                    out[0:1, col + d * k : col + (d + per) * k] = value
                col += n * k

    widths = [sum(n * (sizes[0] if r is None else sizes[r]) for r in rows) for rows in layout]
    lanes = 128 * len(sizes)
    return call(
        body,
        grid_spec=pltpu.PrefetchScalarGridSpec(
            num_scalar_prefetch=1,
            grid=(1,),
            in_specs=[pl.BlockSpec((per_piece, 8, lanes), lambda i, i_ref: (0, at // 8, 0))]
            * len(pieces),
            out_specs=[pl.BlockSpec((1, w), lambda i, i_ref: (0, 0)) for w in widths],
            scratch_shapes=[pltpu.VMEM((n, 8, lanes), jnp.float32)],
        ),
        out_shape=[jax.ShapeDtypeStruct((1, w), jnp.float32) for w in widths],
        name="unpack_vectors",
    )(inverse_row, *pieces)


def pack_sums(parts, inverse_row, n, rows):
    flat = [a for group in parts for a in group]

    def body(i_ref, *refs):
        out = refs[-1]
        out[...] = jnp.zeros_like(out)
        at = 0
        for r, group in enumerate(parts):
            total = refs[at][...]
            for k in range(1, len(group)):
                total += refs[at + k][...]
            at += len(group)
            k = total.shape[1] // n
            for d in range(n):
                out[i_ref[d], r : r + 1, 0:k] = total[:, d * k : (d + 1) * k]

    return call(
        body,
        grid_spec=pltpu.PrefetchScalarGridSpec(
            num_scalar_prefetch=1,
            grid=(1,),
            in_specs=[whole(a.shape) for a in flat],
            out_specs=whole((n, rows, 128)),
        ),
        out_shape=jax.ShapeDtypeStruct((n, rows, 128), jnp.float32),
        name="pack_sums",
    )(inverse_row, *flat)


class Reduction:
    def __init__(self, perms, kept, sent, stage):
        self.perms, self.stage = perms, stage
        self.kept, self.got = kept, send(sent, perms[stage])
        self.done = None

    def step(self, line, wide=jnp.bfloat16):
        kept, got = line.after(self.kept, self.got)
        total = kept.astype(jnp.float32) + got.astype(jnp.float32)
        self.stage += 1
        if self.stage == len(self.perms):
            self.done = total[0]
            line.mark(self.done)
            return
        total = total.astype(wide)
        half = total.shape[0] // 2
        sent = total[half:]
        self.kept = total[:half]
        line.mark(sent)
        self.got = send(sent, self.perms[self.stage])


def per_device(ndp, nfs,
    tokens,
    ln1_gain,
    ln1_bias,
    w_qkv,
    bias_q,
    bias_v,
    w_out,
    bias_out,
    ln2_gain,
    ln2_bias,
    w_up,
    bias_up,
    w_down,
    bias_down,
    cot_first,
    cot_second,
    valid,
):
    n = ndp * nfs
    perms = stage_perms(ndp, nfs)
    gather_perms = perms[:0:-1]
    core_perm = perms[0]
    stages = len(gather_perms)
    table = shard_table(ndp, nfs)
    me = lax.axis_index("dp") * nfs + lax.axis_index("fsdp")
    both = np.concatenate([table, np.argsort(table, axis=1).astype(np.int32)], axis=1)
    both = lax.dynamic_slice(jnp.asarray(both), (me, 0), (1, 2 * n))[0]
    row, inverse_row = both[:n], both[n:]
    rows_in, width = tokens.shape[1:]
    r_in, r_ff = w_up.shape[0], w_down.shape[0]
    hidden = w_up.shape[1]

    vectors = (ln1_gain, ln1_bias, bias_q, bias_v, bias_out, ln2_gain, ln2_bias, bias_down, bias_up)
    sizes = [v.shape[0] for v in vectors]
    lanes_of = lambda v: jnp.pad(v, (0, 128 - v.shape[0]))
    packed = jnp.concatenate([lanes_of(v) for v in vectors])

    line = Line()
    mid = 2 * width
    packed = jnp.pad(packed[None], ((0, 7), (0, mid - packed.shape[0])))
    shards = [
        jnp.concatenate([w_qkv[:, :mid], packed], axis=0),
        jnp.concatenate([w_qkv[:, mid:], w_out], axis=1),
    ]
    split = w_up.reshape(r_in, hidden // width, width).swapaxes(0, 1).reshape(r_ff, width)
    w = {"ff": lax.all_gather(jnp.concatenate([split, w_down], axis=0), AXES)}
    held = [s[None] for s in shards]
    got = [None] * len(shards)
    pieces = [None] * len(shards)

    def gather_round(index):
        for i in range(len(shards)):
            k = index - i
            if k < 0 or k > stages:
                continue
            if k == 0 and i:
                (held[i],) = line.after(held[i])
            if 0 < k < stages:
                mine, theirs = line.after(held[i], got[i])
                held[i] = jnp.concatenate([mine, theirs], axis=0)
                line.mark(held[i])
            if k < stages:
                got[i] = send(held[i], gather_perms[k])
            if k == stages - 1:
                pieces[i] = [held[i], None, send(held[i], core_perm), None]
            if k == stages:
                pieces[i][1] = got[i]
                pieces[i][3] = send(got[i], core_perm)

    def place(which, shapes, slots):
        flat = [p for i in which for p in pieces[i]]
        flat = line.after(*flat)
        groups = [flat[4 * i : 4 * i + 4] for i in range(len(which))]
        outs = place_shards(groups, row, shapes, slots)
        line.mark(outs[0])
        return outs

    for index in range(stages + 2):
        gather_round(index)
    g1, s1, bqkv, bo, g2, s2, bd, bu = unpack_vectors(
        pieces[0], r_in, inverse_row, sizes, [[0], [1], [2, None, 3], [4], [5], [6], [7], [8]]
    )
    qkv_cols = w_qkv.shape[1]
    (first_full,) = place([0, 1], [(n, r_in, 2 * mid)], [(0, None, 0), (0, None, mid)])
    first_full = first_full.reshape(n * r_in, 2 * mid)
    w["first"] = first_full

    def forward(x):
        a1, qkv = norm_project(*line.after(x), g1, s1, w["first"], bqkv, qkv_cols // 2, qkv_cols)
        line.mark(a1)
        o, logs = attention(*line.after(qkv))
        line.mark(o)
        x1, a2 = project_norm(*line.after(o), w["first"], bo, x, g2, s2, qkv_cols)
        line.mark(a2)
        a2 = line.after(a2)[0]
        g, gp, y = feed_forward(a2, w["ff"], r_in, r_ff, bu, bd, x1)
        line.mark(y)
        return y, (x, a1, qkv, logs, o, x1, a2, g, gp)

    first, saved_first = forward(tokens[0])
    second, saved_second = forward(first)

    keep_mask = valid[0].astype(jnp.float32)[:, None]
    grad_second = cot_second[0].astype(jnp.float32) * keep_mask
    pairs = width // (2 * HEAD_DIM)
    parts = 2

    def ff_back(dy, saved):
        x, a1, qkv, logs, o, x1, a2, g, gp = saved
        outs = feed_forward_back(
            *line.after(dy), gp, w["ff"], r_in, r_ff, x1, g2, w["first"], qkv_cols
        )
        line.mark(outs[0])
        return outs

    def heads_back(saved, d_o, i):
        outs = attention_back(
            saved[2], saved[3], saved[4], *line.after(d_o), i * pairs // parts, pairs // parts
        )
        line.mark(outs[0])
        return outs

    def qkv_back(heads, saved, dx1, extra, dtype):
        dx, cg, cs = project_back(
            [line.after(h[0])[0] for h in heads], w["first"], saved[0], g1, dx1, extra, dtype
        )
        line.mark(dx)
        return dx, cg, cs

    dm2, du2, dx2, da2, do2, cdm2, cdu2, cda2, cg22, cs22 = ff_back(grad_second, saved_second)
    heads2 = [heads_back(saved_second, do2, i) for i in range(parts)]
    grad_first, cg12, cs12 = qkv_back(
        heads2, saved_second, dx2, (cot_first[0], keep_mask), jnp.float32
    )

    local = (row // nfs) // 2 * nfs + row % nfs
    half = n // 2
    tiles = ndp // 2
    core = (me // nfs) % 2
    lanes = 2 * jnp.arange(tiles, dtype=jnp.int32)
    index_keep = jnp.concatenate([lanes + core, local[:half]]).astype(jnp.int32)
    index_send = jnp.concatenate([lanes + (1 - core), local[half:]]).astype(jnp.int32)

    def grad_send(lefts, rights, r, tn):
        lefts = line.after(*lefts)
        (out,) = weight_grad_half(lefts, rights, index_send, (ndp, nfs, r), tn)
        line.mark(out)
        return send(out, core_perm)

    def grad_keep(lefts, rights, r, tn, arrived):
        arrived = line.after(arrived)[0]
        kept, sent = weight_grad_half(lefts, rights, index_keep, (ndp, nfs, r), tn, arrived)
        line.mark(sent)
        return kept, sent

    dm1 = grad_first.astype(jnp.bfloat16)
    sg = list(zip(saved_first, saved_second))
    arrived = grad_send(sg[7], (dm1, dm2), r_ff, 256)
    red_down = Reduction(perms, *grad_keep(sg[7], (dm1, dm2), r_ff, 256, arrived), 1)
    _, du1, dx1, da1, do1, cdm1, cdu1, cda1, cg21, cs21 = ff_back(grad_first, saved_first)
    red_down.step(line)
    arrived = grad_send(sg[6], (du1, du2), r_in, 1024)
    red_down.step(line)
    red_up = Reduction(perms, *grad_keep(sg[6], (du1, du2), r_in, 1024, arrived), 1)
    red_down.step(line)
    arrived_out = grad_send(sg[4], (da1, da2), r_in, 1024)
    heads1 = [heads_back(saved_first, do1, 0)]
    kept_out, sent_out = grad_keep(sg[4], (da1, da2), r_in, 1024, arrived_out)
    red_down.step(line)
    rights = lambda i: (heads1[i][0], heads2[i][0])
    arrived = grad_send(sg[1], rights(0), r_in, 512)
    red_up.step(line)
    kept_q, sent_q = grad_keep(sg[1], rights(0), r_in, 512, arrived)
    red_one = Reduction(
        perms,
        jnp.concatenate([kept_out, kept_q], axis=2),
        jnp.concatenate([sent_out, sent_q], axis=2),
        1,
    )
    heads1.append(heads_back(saved_first, do1, 1))
    red_up.step(line)
    arrived = grad_send(sg[1], rights(1), r_in, 512)
    red_two = Reduction(perms, *grad_keep(sg[1], rights(1), r_in, 512, arrived), 1)
    red_one.step(line)
    red_up.step(line)
    grad_inputs, cg11, cs11 = qkv_back(heads1, saved_first, dx1, None, jnp.bfloat16)
    red_one.step(line)
    red_two.step(line)
    cq = [[h[i][1] for h in (heads1, heads2)] for i in range(parts)]
    cv = [[h[i][2] for h in (heads1, heads2)] for i in range(parts)]
    joined = lambda c: [jnp.concatenate([c[i][s] for i in range(parts)], axis=1) for s in range(2)]
    sums = pack_sums(
        [
            [cg11, cg12],
            [cs11, cs12],
            joined(cq),
            joined(cv),
            [cda1, cda2],
            [cg21, cg22],
            [cs21, cs22],
            [cdm1, cdm2],
            [cdu1, cdu2],
        ],
        inverse_row,
        n,
        len(vectors),
    )
    red_small = Reduction(perms, sums[:half], sums[half:], 0)
    red_up.step(line)
    for _ in range(stages):
        for red in (red_one, red_two):
            if red.done is None:
                red.step(line)
        if red_small.done is None:
            red_small.step(line, jnp.float32)
    for red in (red_down, red_up, red_one, red_two):
        while red.done is None:
            red.step(line)
    while red_small.done is None:
        red_small.step(line, jnp.float32)
    outs = [red_small.done[i, : sizes[i]] for i in range(len(vectors))]
    o_g1, o_s1, o_bq, o_bv, o_bo, o_g2, o_s2, o_bd, o_bu = outs
    one = red_one.done
    d_out = one[:, :width]
    third = width // parts
    blocks = []
    for kind in range(3):
        blocks.append(one[:, width + kind * third : width + (kind + 1) * third])
        blocks.append(red_two.done[:, kind * third : (kind + 1) * third])
    d_qkv = jnp.concatenate(blocks, axis=1)
    return (
        first[None],
        second[None],
        grad_inputs[None],
        o_g1,
        o_s1,
        d_qkv,
        o_bq,
        o_bv,
        d_out,
        o_bo,
        o_g2,
        o_s2,
        red_up.done,
        o_bu,
        red_down.done,
        o_bd,
    )


def solution(mesh):
    ndp, nfs = mesh.shape["dp"], mesh.shape["fsdp"]
    return jax.shard_map(
        partial(per_device, ndp, nfs),
        mesh=mesh,
        in_specs=(
            P(("dp", "fsdp"), None, None),
            P(("dp", "fsdp")),
            P(("dp", "fsdp")),
            P(("dp", "fsdp"), None),
            P(("dp", "fsdp")),
            P(("dp", "fsdp")),
            P(("dp", "fsdp"), None),
            P(("dp", "fsdp")),
            P(("dp", "fsdp")),
            P(("dp", "fsdp")),
            P(("dp", "fsdp"), None),
            P(("dp", "fsdp")),
            P(("dp", "fsdp"), None),
            P(("dp", "fsdp")),
            P(("dp", "fsdp"), None, None),
            P(("dp", "fsdp"), None, None),
            P(("dp", "fsdp"), None),
        ),
        out_specs=(
            P(("dp", "fsdp"), None, None),
            P(("dp", "fsdp"), None, None),
            P(("dp", "fsdp"), None, None),
            P(("dp", "fsdp")),
            P(("dp", "fsdp")),
            P(("dp", "fsdp"), None),
            P(("dp", "fsdp")),
            P(("dp", "fsdp")),
            P(("dp", "fsdp"), None),
            P(("dp", "fsdp")),
            P(("dp", "fsdp")),
            P(("dp", "fsdp")),
            P(("dp", "fsdp"), None),
            P(("dp", "fsdp")),
            P(("dp", "fsdp"), None),
            P(("dp", "fsdp")),
        ),
        check_vma=False,
    )
```

```python
from functools import partial

import numpy as np
import jax
import jax.numpy as jnp
from jax import lax
from jax.experimental import pallas as pl
from jax.experimental.pallas import tpu as pltpu
from jax.sharding import PartitionSpec as P

def call(body, cover=False, **options):
    cost = pl.CostEstimate(flops=10**11 if cover else 1, transcendentals=0, bytes_accessed=1)
    return pl.pallas_call(body, cost_estimate=cost, **options)


EPSILON = 1e-06
HEAD_DIM = 64
LOG2E = 1.4426950408889634
RSQRT_2PI = 0.3989422804014327
SQRT_HALF = 0.7071067811865476
SCORE_SCALE = HEAD_DIM**-0.5 * LOG2E
NT = (((1,), (1,)), ((), ()))
TN = (((0,), (0,)), ((), ()))


def dot(a, b, dims=(((1,), (0,)), ((), ()))):
    return lax.dot_general(a, b, dims, preferred_element_type=jnp.float32)


def whole(shape):
    return pl.BlockSpec(shape, lambda *_: (0,) * len(shape))


def normal_cdf(u):
    return 0.5 + 0.5 * lax.erf(u * SQRT_HALF), jnp.exp2((-0.5 * LOG2E) * (u * u))


def row_stats(v):
    centre = v - jnp.mean(v, axis=-1, keepdims=True)
    inv = lax.rsqrt(jnp.mean(centre * centre, axis=-1, keepdims=True) + EPSILON)
    return centre * inv, inv


def norm_project(x, gain, shift, weight, bias, tn, cols):
    rows, width = x.shape

    def body(x_ref, g_ref, s_ref, w_ref, b_ref, a_ref, o_ref):
        @pl.when(pl.program_id(0) == 0)
        def _():
            xhat, _ = row_stats(x_ref[...].astype(jnp.float32))
            a_ref[...] = (xhat * g_ref[...] + s_ref[...]).astype(jnp.bfloat16)

        o_ref[...] = (dot(a_ref[...], w_ref[...]) + b_ref[...]).astype(jnp.bfloat16)

    return call(
        body,
        grid=(cols // tn,),
        in_specs=[
            whole((rows, width)),
            whole((1, width)),
            whole((1, width)),
            pl.BlockSpec((width, tn), lambda j: (0, j)),
            pl.BlockSpec((1, tn), lambda j: (0, j)),
        ],
        out_specs=[whole((rows, width)), pl.BlockSpec((rows, tn), lambda j: (0, j))],
        out_shape=[
            jax.ShapeDtypeStruct((rows, width), jnp.bfloat16),
            jax.ShapeDtypeStruct((rows, cols), jnp.bfloat16),
        ],
        name="norm_project",
    )(x, gain, shift, weight, bias)


def attention(qkv):
    rows, width = qkv.shape[0], qkv.shape[1] // 3
    pairs = width // (2 * HEAD_DIM)
    span = 2 * HEAD_DIM

    def body(q_ref, k_ref, v_ref, o_ref, l_ref):
        q, k, v = q_ref[...], k_ref[...], v_ref[...]
        lane = lax.broadcasted_iota(jnp.int32, (rows, span), 1)
        outs, logs = [], []
        for h in range(2):
            mine = (lane < HEAD_DIM) if h == 0 else (lane >= HEAD_DIM)
            kh = jnp.where(mine, k, jnp.zeros_like(k))
            s = dot(q, kh, NT)
            top = jnp.max(s, axis=-1, keepdims=True) * SCORE_SCALE
            e = jnp.exp2(s * SCORE_SCALE - top)
            total = jnp.sum(e, axis=-1, keepdims=True)
            outs.append(dot(e.astype(jnp.bfloat16), v) * (1.0 / total))
            logs.append(top + jnp.log2(total))
        first = lane < HEAD_DIM
        o_ref[...] = jnp.where(first, outs[0], outs[1]).astype(jnp.bfloat16)
        both = jnp.where(first, logs[0], logs[1])
        turned = both.T
        l_ref[0, 0:1, :] = turned[0:1, :]
        l_ref[0, 1:2, :] = turned[HEAD_DIM : HEAD_DIM + 1, :]

    col = lambda base: pl.BlockSpec((rows, span), lambda j: (0, base + j))
    return call(
        body,
        grid=(pairs,),
        in_specs=[col(0), col(pairs), col(2 * pairs)],
        out_specs=[col(0), pl.BlockSpec((1, 8, rows), lambda j: (j, 0, 0))],
        out_shape=[
            jax.ShapeDtypeStruct((rows, width), jnp.bfloat16),
            jax.ShapeDtypeStruct((pairs, 8, rows), jnp.float32),
        ],
        name="attention",
    )(qkv, qkv, qkv)


def attention_back(qkv, logs, d_o, first_pair, pairs, cover=True):
    rows, width = qkv.shape[0], qkv.shape[1] // 3
    every = width // (2 * HEAD_DIM)
    span = 2 * HEAD_DIM

    def body(q_ref, k_ref, v_ref, l_ref, do_ref, d_ref, cq_ref, cv_ref):
        q, k, v, do = q_ref[...], k_ref[...], v_ref[...], do_ref[...]
        lane = lax.broadcasted_iota(jnp.int32, (rows, span), 1)
        dqs, dks, dvs = [], [], []
        for h in range(2):
            mine = (lane < HEAD_DIM) if h == 0 else (lane >= HEAD_DIM)
            kh = jnp.where(mine, k, jnp.zeros_like(k))
            vh = jnp.where(mine, v, jnp.zeros_like(v))
            pt = jnp.exp2(dot(kh, q, NT) * SCORE_SCALE - l_ref[0, h : h + 1, :])
            w = pt * dot(vh, do, NT)
            dst = (w - pt * jnp.sum(w, axis=0, keepdims=True)).astype(jnp.bfloat16)
            dvs.append(dot(pt.astype(jnp.bfloat16), do))
            dks.append(dot(dst, q))
            dqs.append(dot(dst, k, TN))
        first = lane < HEAD_DIM
        dq = (jnp.where(first, dqs[0], dqs[1]) * 0.125).astype(jnp.bfloat16)
        dk = (jnp.where(first, dks[0], dks[1]) * 0.125).astype(jnp.bfloat16)
        dv = jnp.where(first, dvs[0], dvs[1]).astype(jnp.bfloat16)
        d_ref[0] = dq
        d_ref[1] = dk
        d_ref[2] = dv
        cq_ref[...] = jnp.sum(dq.astype(jnp.float32), axis=0, keepdims=True)
        cv_ref[...] = jnp.sum(dv.astype(jnp.float32), axis=0, keepdims=True)

    col = lambda base: pl.BlockSpec((rows, span), lambda j: (0, base + j))
    sums = pl.BlockSpec((1, span), lambda j: (0, j))
    vec_shape = jax.ShapeDtypeStruct((1, pairs * span), jnp.float32)
    return call(
        body,
        grid=(pairs,),
        in_specs=[
            col(first_pair),
            col(every + first_pair),
            col(2 * every + first_pair),
            pl.BlockSpec((1, 8, rows), lambda j: (first_pair + j, 0, 0)),
            col(first_pair),
        ],
        out_specs=[pl.BlockSpec((3, rows, span), lambda j: (0, 0, j)), sums, sums],
        out_shape=[
            jax.ShapeDtypeStruct((3, rows, pairs * span), jnp.bfloat16),
            vec_shape,
            vec_shape,
        ],
        name="attention_back",
        cover=cover,
    )(qkv, qkv, qkv, logs, d_o)


def project_norm(o, weight, bias, x, gain, shift, at):
    rows, width = o.shape
    tm = rows // 2

    def body(o_ref, w_ref, b_ref, x_ref, g_ref, s_ref, x1_ref, a_ref):
        x1 = x_ref[...].astype(jnp.float32) + (dot(o_ref[...], w_ref[...]) + b_ref[...])
        x1_ref[...] = x1
        xhat, _ = row_stats(x1)
        a_ref[...] = (xhat * g_ref[...] + s_ref[...]).astype(jnp.bfloat16)

    rowblk = pl.BlockSpec((tm, width), lambda i: (i, 0))
    vec = whole((1, width))
    return call(
        body,
        grid=(rows // tm,),
        in_specs=[rowblk, pl.BlockSpec((width, width), lambda i: (0, at // width)), vec, rowblk, vec, vec],
        out_specs=[rowblk, rowblk],
        out_shape=[
            jax.ShapeDtypeStruct((rows, width), jnp.float32),
            jax.ShapeDtypeStruct((rows, width), jnp.bfloat16),
        ],
        name="project_norm",
    )(o, weight, bias, x, gain, shift)


def flat(ref):
    return ref[...].reshape(-1, ref.shape[-1])


def up_spec(packed, r_in):
    n, _, width = packed.shape
    return pl.BlockSpec((n, r_in, width), lambda j: (0, j, 0))


def down_spec(packed, r_ff):
    width = packed.shape[2]
    return pl.BlockSpec((width // r_ff, r_ff, width), lambda j: (j, 1, 0))


def feed_forward(a, packed, r_in, r_ff, up_bias, down_bias, x1):
    rows, width = a.shape
    hidden = up_bias.shape[1]
    tf = width
    steps = hidden // tf

    def body(a_ref, u_ref, ub_ref, d_ref, db_ref, x_ref, g_ref, gp_ref, y_ref, acc):
        j = pl.program_id(0)
        u = dot(a_ref[...], flat(u_ref)) + ub_ref[...]
        phi, bell = normal_cdf(u)
        g = (u * phi).astype(jnp.bfloat16)
        g_ref[...] = g
        gp_ref[...] = (phi + (u * RSQRT_2PI) * bell).astype(jnp.bfloat16)

        @pl.when(j == 0)
        def _():
            acc[...] = x_ref[...] + db_ref[...]

        acc[...] += dot(g, flat(d_ref))

        @pl.when(j == steps - 1)
        def _():
            y_ref[...] = acc[...].astype(jnp.bfloat16)

    return call(
        body,
        grid=(steps,),
        in_specs=[
            whole((rows, width)),
            up_spec(packed, r_in),
            pl.BlockSpec((1, tf), lambda j: (0, j)),
            down_spec(packed, r_ff),
            whole((1, width)),
            whole((rows, width)),
        ],
        out_specs=[
            pl.BlockSpec((rows, tf), lambda j: (0, j)),
            pl.BlockSpec((rows, tf), lambda j: (0, j)),
            whole((rows, width)),
        ],
        out_shape=[
            jax.ShapeDtypeStruct((rows, hidden), jnp.bfloat16),
            jax.ShapeDtypeStruct((rows, hidden), jnp.bfloat16),
            jax.ShapeDtypeStruct((rows, width), jnp.bfloat16),
        ],
        scratch_shapes=[pltpu.VMEM((rows, width), jnp.float32)],
        name="feed_forward",
    )(a, packed, up_bias, packed, down_bias, x1)


def feed_forward_back(dy, gp, packed, r_in, r_ff, x1, gain, w_out, at):
    rows, width = dy.shape
    hidden = gp.shape[1]
    tf = width
    steps = hidden // tf

    def body(
        dy_ref, gp_ref, d_ref, u_ref, x_ref, g_ref, w_ref,
        dm_ref, du_ref, dx_ref, da_ref, do_ref, cdm_ref, cdu_ref, cda_ref, cg_ref, cs_ref, acc,
    ):
        j = pl.program_id(0)

        @pl.when(j == 0)
        def _():
            low = dy_ref[...].astype(jnp.bfloat16)
            dm_ref[...] = low
            cdm_ref[...] = jnp.sum(low.astype(jnp.float32), axis=0, keepdims=True)
            acc[...] = jnp.zeros_like(acc)

        du = (dot(dm_ref[...], flat(d_ref), NT) * gp_ref[...].astype(jnp.float32)).astype(jnp.bfloat16)
        du_ref[...] = du
        cdu_ref[...] = jnp.sum(du.astype(jnp.float32), axis=0, keepdims=True)
        acc[...] += dot(du, flat(u_ref), NT)

        @pl.when(j == steps - 1)
        def _():
            da2 = acc[...]
            xhat, inv = row_stats(x_ref[...])
            cg_ref[...] = jnp.sum(da2 * xhat, axis=0, keepdims=True)
            cs_ref[...] = jnp.sum(da2, axis=0, keepdims=True)
            t = da2 * g_ref[...]
            m1 = jnp.mean(t, axis=-1, keepdims=True)
            m2 = jnp.mean(t * xhat, axis=-1, keepdims=True)
            dx1 = dy_ref[...] + inv * (t - m1 - xhat * m2)
            dx_ref[...] = dx1
            low = dx1.astype(jnp.bfloat16)
            da_ref[...] = low
            cda_ref[...] = jnp.sum(low.astype(jnp.float32), axis=0, keepdims=True)
            do_ref[...] = dot(low, w_ref[...], NT).astype(jnp.bfloat16)

    full = whole((rows, width))
    vec = whole((1, width))
    f = lambda s, d: jax.ShapeDtypeStruct(s, d)
    return call(
        body,
        grid=(steps,),
        in_specs=[
            full,
            pl.BlockSpec((rows, tf), lambda j: (0, j)),
            down_spec(packed, r_ff),
            up_spec(packed, r_in),
            full,
            vec,
            pl.BlockSpec((width, width), lambda j: (0, at // width)),
        ],
        out_specs=[
            full,
            pl.BlockSpec((rows, tf), lambda j: (0, j)),
            full,
            full,
            full,
            vec,
            pl.BlockSpec((1, tf), lambda j: (0, j)),
            vec,
            vec,
            vec,
        ],
        out_shape=[
            f((rows, width), jnp.bfloat16),
            f((rows, hidden), jnp.bfloat16),
            f((rows, width), jnp.float32),
            f((rows, width), jnp.bfloat16),
            f((rows, width), jnp.bfloat16),
            f((1, width), jnp.float32),
            f((1, hidden), jnp.float32),
            f((1, width), jnp.float32),
            f((1, width), jnp.float32),
            f((1, width), jnp.float32),
        ],
        scratch_shapes=[pltpu.VMEM((rows, width), jnp.float32)],
        name="feed_forward_back",
        cover=True,
    )(dy, gp, packed, packed, x1, gain, w_out)


def project_back(grads, weight, x, gain, dx1, extra, dtypes):
    rows, width = x.shape
    tm = rows // 2
    have = extra is not None
    count = len(grads)
    part = width // count

    def body(*refs):
        d_refs = refs[:count]
        w_ref, x_ref, g_ref, dx_ref = refs[count : count + 4]
        more = refs[count + 4 : -2 - len(dtypes)]
        out_refs = refs[-2 - len(dtypes) : -2]
        cg_ref, cs_ref = refs[-2:]
        da = None
        for kind in range(3):
            for i in range(count):
                at = kind * width + i * part
                term = dot(d_refs[i][kind], w_ref[:, at : at + part], NT)
                da = term if da is None else da + term
        xhat, inv = row_stats(x_ref[...].astype(jnp.float32))
        cg = jnp.sum(da * xhat, axis=0, keepdims=True)
        cs = jnp.sum(da, axis=0, keepdims=True)

        @pl.when(pl.program_id(0) == 0)
        def _():
            cg_ref[...] = cg
            cs_ref[...] = cs

        @pl.when(pl.program_id(0) > 0)
        def _():
            cg_ref[...] += cg
            cs_ref[...] += cs

        t = da * g_ref[...]
        m1 = jnp.mean(t, axis=-1, keepdims=True)
        m2 = jnp.mean(t * xhat, axis=-1, keepdims=True)
        dx = dx_ref[...] + inv * (t - m1 - xhat * m2)
        if have:
            dx = more[0][...].astype(jnp.float32) * more[1][...] + dx
        for ref in out_refs:
            ref[...] = dx.astype(ref.dtype)

    rowblk = pl.BlockSpec((tm, width), lambda i: (i, 0))
    vec_spec = whole((1, width))
    specs = [pl.BlockSpec((3, tm, part), lambda i: (0, i, 0))] * count
    specs += [whole((width, 3 * width)), rowblk, vec_spec, rowblk]
    args = list(grads) + [weight, x, gain, dx1]
    if have:
        specs += [rowblk, pl.BlockSpec((tm, 1), lambda i: (i, 0))]
        args += list(extra)
    return call(
        body,
        grid=(rows // tm,),
        in_specs=specs,
        out_specs=[rowblk] * len(dtypes) + [vec_spec, vec_spec],
        out_shape=[
            *[jax.ShapeDtypeStruct((rows, width), d) for d in dtypes],
            jax.ShapeDtypeStruct((1, width), jnp.float32),
            jax.ShapeDtypeStruct((1, width), jnp.float32),
        ],
        name="project_back",
        cover=True,
    )(*args)


def weight_grad(jobs, index, blocks, chunk, cover=False):
    ndp, nfs, r = blocks
    npos = ndp * nfs // 2
    rows = jobs[0][0][0].shape[0]
    widths = [rs[0].shape[-1] * (3 if rs[0].ndim == 3 else 1) for _, rs in jobs]
    starts = [sum(widths[:k]) for k in range(len(jobs))]
    counts = [len(ls) for ls, _ in jobs]
    steps = ndp * len(jobs)

    def body(i_ref, *refs):
        sent, kept, buf, sem = refs[-4:]
        i = pl.program_id(0)

        def copies(step, start):
            local = step % ndp
            for k in range(len(jobs)):
                for which, where in ((local < ndp // 2, sent), (local >= ndp // 2, kept)):

                    @pl.when((step // ndp == k) & which)
                    def _():
                        for f in range(nfs):
                            p = i_ref[ndp + local * nfs + f]
                            copy = pltpu.make_async_copy(
                                buf.at[step % 2, f, :, 0 : widths[k]],
                                where.at[p, :, starts[k] : starts[k] + widths[k]],
                                sem.at[step % 2, f],
                            )
                            copy.start() if start else copy.wait()

        @pl.when(i >= 2)
        def _():
            copies(i - 2, False)

        at_ref = 0
        for k in range(len(jobs)):
            a = refs[at_ref : at_ref + counts[k]]
            b = refs[at_ref + counts[k] : at_ref + 2 * counts[k]]
            at_ref += 2 * counts[k]

            @pl.when(i // ndp == k)
            def _():
                for at in range(0, widths[k], chunk):
                    part = b[0].shape[-1]
                    if len(b[0].shape) == 3:
                        take = lambda ref: ref[at // part, :, at % part : at % part + chunk]
                    else:
                        take = lambda ref: ref[:, at : at + chunk]
                    total = dot(a[0][...], take(b[0]), TN)
                    for x, y in zip(a[1:], b[1:]):
                        total += dot(x[...], take(y), TN)
                    total = total.astype(jnp.bfloat16).reshape(nfs, r, chunk)
                    buf[i % 2, :, :, at : at + chunk] = total

        copies(i, True)

        @pl.when(i == steps - 1)
        def _():
            copies(steps - 2, False)
            copies(steps - 1, False)

    def left_spec(k):
        step = lambda i: jnp.clip(i - k * ndp, 0, ndp - 1)
        return pl.BlockSpec((rows, nfs * r), lambda i, i_ref: (0, i_ref[step(i)]))

    anywhere = pl.BlockSpec(memory_space=pl.ANY)
    specs, args = [], []
    for k, (ls, rs) in enumerate(jobs):
        specs += [left_spec(k)] * len(ls) + [whole(rs[0].shape)] * len(rs)
        args += list(ls) + list(rs)
    return call(
        body,
        grid_spec=pltpu.PrefetchScalarGridSpec(
            num_scalar_prefetch=1,
            grid=(steps,),
            in_specs=specs,
            out_specs=[anywhere] * 2,
            scratch_shapes=[
                pltpu.VMEM((2, nfs, r, max(widths)), jnp.bfloat16),
                pltpu.SemaphoreType.DMA((2, nfs)),
            ],
        ),
        out_shape=[jax.ShapeDtypeStruct((npos, r, sum(widths)), jnp.bfloat16)] * 2,
        name="weight_grad",
        cover=cover,
    )(index, *args)


def bits_of(ndp, nfs):
    core = nfs
    outer = [nfs << i for i in range(1, ndp.bit_length() - 1)]
    inner = [1 << i for i in range(nfs.bit_length() - 1)]
    return core, outer, inner


def stage_orders(ndp, nfs):
    core, outer, inner = bits_of(ndp, nfs)
    first, second = outer[0], inner[0]
    tail = outer[1:] + inner[1:]
    return core, ([first, second] + tail, [second, first] + tail)


def shard_table(ndp, nfs):
    n = ndp * nfs
    core, orders = stage_orders(ndp, nfs)
    table = np.zeros((n, n), np.int32)
    for me in range(n):
        for p in range(n):
            rel = core if p >= n // 2 else 0
            owner = 1 if (me ^ rel) & core else 0
            for i, mask in enumerate(orders[owner]):
                if p & (n >> (i + 2)):
                    rel ^= mask
            table[me, p] = me ^ rel
    return table


def stage_perms(ndp, nfs):
    n = ndp * nfs
    core, orders = stage_orders(ndp, nfs)
    perms = [[(i, i ^ core) for i in range(n)]]
    for a, b in zip(*orders):
        perms.append([(i, i ^ (b if i & core else a)) for i in range(n)])
    return perms


AXES = ("dp", "fsdp")


def send(x, perm):
    return lax.ppermute(x, AXES, perm)


class Line:
    def __init__(self):
        self.last = None

    def after(self, *arrays):
        if self.last is not None:
            arrays = lax.optimization_barrier((self.last,) + arrays)[1:]
        return arrays

    def mark(self, array):
        self.last = array


def place_shards(groups, table_row, shapes, slots):
    n = sum(p.shape[0] for p in groups[0])
    count = len(groups)

    def body(t_ref, *refs):
        ins = refs[: 4 * count]
        outs = refs[4 * count : 4 * count + len(shapes)]
        bufs = refs[4 * count + len(shapes) : -2]
        in_sem, out_sem = refs[-2:]
        loads, stores = [], []
        for i in range(count):
            which, middle, col = slots[i]
            width = bufs[i].shape[-1]
            for p in range(n):
                piece = ins[4 * i + p // (n // 4)].at[p % (n // 4), 0 : bufs[i].shape[1]]
                loads.append(pltpu.make_async_copy(piece, bufs[i].at[p], in_sem.at[i, p]))
                target = outs[which].at[t_ref[p]]
                if middle is not None:
                    target = target.at[middle]
                stores.append(
                    pltpu.make_async_copy(
                        bufs[i].at[p], target.at[:, col : col + width], out_sem.at[i, p]
                    )
                )
        for c in loads:
            c.start()
        for a, b in zip(loads, stores):
            a.wait()
            b.start()
        for b in stores:
            b.wait()

    flat = [p for g in groups for p in g]
    anywhere = pl.BlockSpec(memory_space=pl.ANY)
    return call(
        body,
        out_shape=[jax.ShapeDtypeStruct(s, jnp.bfloat16) for s in shapes],
        grid_spec=pltpu.PrefetchScalarGridSpec(
            num_scalar_prefetch=1,
            in_specs=[anywhere] * len(flat),
            out_specs=[anywhere] * len(shapes),
            scratch_shapes=[
                pltpu.VMEM((n, shapes[s[0]][-2], g[0].shape[-1]), jnp.bfloat16)
                for g, s in zip(groups, slots)
            ]
            + [pltpu.SemaphoreType.DMA((count, n))] * 2,
        ),
        name="place_shards",
    )(table_row, *flat)


def unpack_vectors(pieces, at, inverse_row, sizes, layout):
    per_piece = pieces[0].shape[0]
    n = per_piece * len(pieces)

    def body(i_ref, *refs):
        ins, outs, scr = refs[: len(pieces)], refs[len(pieces) : -1], refs[-1]
        for i, ref in enumerate(ins):
            scr[i * per_piece : (i + 1) * per_piece] = ref[...].astype(jnp.float32)
        for rows, out in zip(layout, outs):
            col = 0
            for r in rows:
                k = sizes[0] if r is None else sizes[r]
                per = 128 // k if k < 128 else 1
                for d in range(0, n, per):
                    if r is None:
                        value = jnp.zeros((1, per * k), jnp.float32)
                    else:
                        value = jnp.concatenate(
                            [scr[i_ref[d + e], 0:1, r * 128 : r * 128 + k] for e in range(per)],
                            axis=1,
                        )
                    out[0:1, col + d * k : col + (d + per) * k] = value
                col += n * k

    widths = [sum(n * (sizes[0] if r is None else sizes[r]) for r in rows) for rows in layout]
    lanes = 128 * len(sizes)
    return call(
        body,
        grid_spec=pltpu.PrefetchScalarGridSpec(
            num_scalar_prefetch=1,
            grid=(1,),
            in_specs=[pl.BlockSpec((per_piece, 8, lanes), lambda i, i_ref: (0, at // 8, 0))]
            * len(pieces),
            out_specs=[pl.BlockSpec((1, w), lambda i, i_ref: (0, 0)) for w in widths],
            scratch_shapes=[pltpu.VMEM((n, 8, lanes), jnp.float32)],
        ),
        out_shape=[jax.ShapeDtypeStruct((1, w), jnp.float32) for w in widths],
        name="unpack_vectors",
    )(inverse_row, *pieces)


def pack_sums(parts, inverse_row, n, rows):
    flat = [a for group in parts for a in group]

    def body(i_ref, *refs):
        out = refs[-1]
        out[...] = jnp.zeros_like(out)
        at = 0
        for r, group in enumerate(parts):
            total = refs[at][...]
            for k in range(1, len(group)):
                total += refs[at + k][...]
            at += len(group)
            k = total.shape[1] // n
            for d in range(n):
                out[i_ref[d], r : r + 1, 0:k] = total[:, d * k : (d + 1) * k]

    return call(
        body,
        grid_spec=pltpu.PrefetchScalarGridSpec(
            num_scalar_prefetch=1,
            grid=(1,),
            in_specs=[whole(a.shape) for a in flat],
            out_specs=whole((n, rows, 128)),
        ),
        out_shape=jax.ShapeDtypeStruct((n, rows, 128), jnp.float32),
        name="pack_sums",
        cover=True,
    )(inverse_row, *flat)


class Reduction:
    def __init__(self, perms, kept, sent, stage):
        self.perms, self.stage = perms, stage
        self.kept, self.got = kept, send(sent, perms[stage])
        self.done = None

    def step(self, line, wide=jnp.bfloat16):
        kept, got = line.after(self.kept, self.got)
        add = lambda part: kept[part].astype(jnp.float32) + got[part].astype(jnp.float32)
        self.stage += 1
        if self.stage == len(self.perms):
            self.done = add(slice(None))[0]
            line.mark(self.done)
            return
        half = kept.shape[0] // 2
        sent = add(slice(half, None)).astype(wide)
        self.got = send(sent, self.perms[self.stage])
        self.kept = add(slice(0, half)).astype(wide)
        line.mark(self.kept)


def per_device(ndp, nfs,
    tokens,
    ln1_gain,
    ln1_bias,
    w_qkv,
    bias_q,
    bias_v,
    w_out,
    bias_out,
    ln2_gain,
    ln2_bias,
    w_up,
    bias_up,
    w_down,
    bias_down,
    cot_first,
    cot_second,
    valid,
):
    n = ndp * nfs
    perms = stage_perms(ndp, nfs)
    gather_perms = perms[:0:-1]
    core_perm = perms[0]
    stages = len(gather_perms)
    table = shard_table(ndp, nfs)
    me = lax.axis_index("dp") * nfs + lax.axis_index("fsdp")
    both = np.concatenate([table, np.argsort(table, axis=1).astype(np.int32)], axis=1)
    both = lax.dynamic_slice(jnp.asarray(both), (me, 0), (1, 2 * n))[0]
    row, inverse_row = both[:n], both[n:]
    rows_in, width = tokens.shape[1:]
    r_in, r_ff = w_up.shape[0], w_down.shape[0]
    hidden = w_up.shape[1]

    vectors = (ln1_gain, ln1_bias, bias_q, bias_v, bias_out, ln2_gain, ln2_bias, bias_down, bias_up)
    sizes = [v.shape[0] for v in vectors]
    lanes_of = lambda v: jnp.pad(v, (0, 128 - v.shape[0]))
    packed = jnp.concatenate([lanes_of(v) for v in vectors])

    line = Line()
    mid = 2 * width
    packed = jnp.pad(packed[None], ((0, 7), (0, mid - packed.shape[0])))
    shards = [
        jnp.concatenate([w_qkv[:, :mid], packed], axis=0),
        jnp.concatenate([w_qkv[:, mid:], w_out], axis=1),
    ]
    split = w_up.reshape(r_in, hidden // width, width).swapaxes(0, 1).reshape(r_ff, width)
    w = {"ff": lax.all_gather(jnp.concatenate([split, w_down], axis=0), AXES)}
    held = [s[None] for s in shards]
    got = [None] * len(shards)
    pieces = [None] * len(shards)

    def gather_round(index):
        for i in range(len(shards)):
            k = index - i
            if k < 0 or k > stages:
                continue
            if k == 0 and i:
                (held[i],) = line.after(held[i])
            if 0 < k < stages:
                mine, theirs = line.after(held[i], got[i])
                held[i] = jnp.concatenate([mine, theirs], axis=0)
                line.mark(held[i])
            if k < stages:
                got[i] = send(held[i], gather_perms[k])
            if k == stages - 1:
                pieces[i] = [held[i], None, send(held[i], core_perm), None]
            if k == stages:
                pieces[i][1] = got[i]
                pieces[i][3] = send(got[i], core_perm)

    def place(which, shapes, slots):
        flat = [p for i in which for p in pieces[i]]
        flat = line.after(*flat)
        groups = [flat[4 * i : 4 * i + 4] for i in range(len(which))]
        outs = place_shards(groups, row, shapes, slots)
        line.mark(outs[0])
        return outs

    for index in range(stages + 2):
        gather_round(index)
    g1, s1, bqkv, bo, g2, s2, bd, bu = unpack_vectors(
        pieces[0], r_in, inverse_row, sizes, [[0], [1], [2, None, 3], [4], [5], [6], [7], [8]]
    )
    qkv_cols = w_qkv.shape[1]
    (first_full,) = place([0, 1], [(n, r_in, 2 * mid)], [(0, None, 0), (0, None, mid)])
    first_full = first_full.reshape(n * r_in, 2 * mid)
    w["first"] = first_full

    def forward(x):
        a1, qkv = norm_project(*line.after(x), g1, s1, w["first"], bqkv, qkv_cols // 2, qkv_cols)
        line.mark(a1)
        o, logs = attention(*line.after(qkv))
        line.mark(o)
        x1, a2 = project_norm(*line.after(o), w["first"], bo, x, g2, s2, qkv_cols)
        line.mark(a2)
        a2 = line.after(a2)[0]
        g, gp, y = feed_forward(a2, w["ff"], r_in, r_ff, bu, bd, x1)
        line.mark(y)
        return y, (x, a1, qkv, logs, o, x1, a2, g, gp)

    first, saved_first = forward(tokens[0])
    second, saved_second = forward(first)

    keep_mask = valid[0].astype(jnp.float32)[:, None]
    grad_second = cot_second[0].astype(jnp.float32) * keep_mask
    pairs = width // (2 * HEAD_DIM)
    parts = 2

    def ff_back(dy, saved):
        x, a1, qkv, logs, o, x1, a2, g, gp = saved
        outs = feed_forward_back(
            *line.after(dy), gp, w["ff"], r_in, r_ff, x1, g2, w["first"], qkv_cols
        )
        line.mark(outs[0])
        return outs

    def heads_back(saved, d_o, i, cover=True):
        outs = attention_back(
            saved[2], saved[3], *line.after(d_o), i * pairs // parts, pairs // parts, cover
        )
        line.mark(outs[0])
        return outs

    def qkv_back(heads, saved, dx1, extra, dtypes):
        outs = project_back(
            [line.after(h[0])[0] for h in heads], w["first"], saved[0], g1, dx1, extra, dtypes
        )
        line.mark(outs[0])
        return outs

    dm2, du2, dx2, da2, do2, cdm2, cdu2, cda2, cg22, cs22 = ff_back(grad_second, saved_second)
    heads2 = [heads_back(saved_second, do2, i) for i in range(parts)]
    grad_first, dm1, cg12, cs12 = qkv_back(
        heads2, saved_second, dx2, (cot_first[0], keep_mask), (jnp.float32, jnp.bfloat16)
    )

    half = n // 2
    core = (me // nfs) % 2
    evens = 2 * jnp.arange(ndp // 2, dtype=jnp.int32)
    lefts_at = jnp.concatenate([evens + (1 - core), evens + core])
    shards_at = lefts_at[:, None] * nfs + jnp.arange(nfs, dtype=jnp.int32)
    index = jnp.concatenate([lefts_at, inverse_row[shards_at.reshape(-1)] % half])
    index = index.astype(jnp.int32)

    def grads(r, *jobs, cover=False):
        jobs = [(line.after(*ls), rs) for ls, rs in jobs]
        sent, kept = weight_grad(jobs, index, (ndp, nfs, r), 512, cover)
        line.mark(sent)
        return Reduction(perms, kept, sent, 0)

    sg = list(zip(saved_first, saved_second))
    red_down = grads(r_ff, (sg[7], (dm1, dm2)))
    _, du1, dx1, da1, do1, cdm1, cdu1, cda1, cg21, cs21 = ff_back(grad_first, saved_first)
    red_down.step(line)
    red_up = grads(r_in, (sg[6], (du1, du2)))
    red_down.step(line)
    heads1 = [heads_back(saved_first, do1, 0)]
    rights = lambda i: (heads1[i][0], heads2[i][0])
    red_down.step(line)
    red_up.step(line)
    red_one = grads(r_in, (sg[4], (da1, da2)), (sg[1], rights(0)))
    heads1.append(heads_back(saved_first, do1, 1, False))
    red_up.step(line)
    red_down.step(line)
    red_two = grads(r_in, (sg[1], rights(1)), cover=True)
    red_one.step(line)
    red_up.step(line)
    grad_inputs, cg11, cs11 = qkv_back(heads1, saved_first, dx1, None, (jnp.bfloat16,))
    red_two.step(line)
    red_one.step(line)
    red_up.step(line)
    red_down.step(line)
    cq = [[h[i][1] for h in (heads1, heads2)] for i in range(parts)]
    cv = [[h[i][2] for h in (heads1, heads2)] for i in range(parts)]
    joined = lambda c: [jnp.concatenate([c[i][s] for i in range(parts)], axis=1) for s in range(2)]
    sums = pack_sums(
        [
            [cg11, cg12],
            [cs11, cs12],
            joined(cq),
            joined(cv),
            [cda1, cda2],
            [cg21, cg22],
            [cs21, cs22],
            [cdm1, cdm2],
            [cdu1, cdu2],
        ],
        inverse_row,
        n,
        len(vectors),
    )
    red_small = Reduction(perms, sums[:half], sums[half:], 0)
    for _ in range(stages):
        for red in (red_two, red_one, red_up, red_down):
            if red.done is None:
                red.step(line)
        if red_small.done is None:
            red_small.step(line, jnp.float32)
    for red in (red_down, red_up, red_one, red_two):
        while red.done is None:
            red.step(line)
    while red_small.done is None:
        red_small.step(line, jnp.float32)
    outs = [red_small.done[i, : sizes[i]] for i in range(len(vectors))]
    o_g1, o_s1, o_bq, o_bv, o_bo, o_g2, o_s2, o_bd, o_bu = outs
    one = red_one.done
    d_out = one[:, :width]
    third = width // parts
    blocks = []
    for kind in range(3):
        blocks.append(one[:, width + kind * third : width + (kind + 1) * third])
        blocks.append(red_two.done[:, kind * third : (kind + 1) * third])
    d_qkv = jnp.concatenate(blocks, axis=1)
    return (
        first[None],
        second[None],
        grad_inputs[None],
        o_g1,
        o_s1,
        d_qkv,
        o_bq,
        o_bv,
        d_out,
        o_bo,
        o_g2,
        o_s2,
        red_up.done,
        o_bu,
        red_down.done,
        o_bd,
    )


def solution(mesh):
    ndp, nfs = mesh.shape["dp"], mesh.shape["fsdp"]
    return jax.shard_map(
        partial(per_device, ndp, nfs),
        mesh=mesh,
        in_specs=(
            P(("dp", "fsdp"), None, None),
            P(("dp", "fsdp")),
            P(("dp", "fsdp")),
            P(("dp", "fsdp"), None),
            P(("dp", "fsdp")),
            P(("dp", "fsdp")),
            P(("dp", "fsdp"), None),
            P(("dp", "fsdp")),
            P(("dp", "fsdp")),
            P(("dp", "fsdp")),
            P(("dp", "fsdp"), None),
            P(("dp", "fsdp")),
            P(("dp", "fsdp"), None),
            P(("dp", "fsdp")),
            P(("dp", "fsdp"), None, None),
            P(("dp", "fsdp"), None, None),
            P(("dp", "fsdp"), None),
        ),
        out_specs=(
            P(("dp", "fsdp"), None, None),
            P(("dp", "fsdp"), None, None),
            P(("dp", "fsdp"), None, None),
            P(("dp", "fsdp")),
            P(("dp", "fsdp")),
            P(("dp", "fsdp"), None),
            P(("dp", "fsdp")),
            P(("dp", "fsdp")),
            P(("dp", "fsdp"), None),
            P(("dp", "fsdp")),
            P(("dp", "fsdp")),
            P(("dp", "fsdp")),
            P(("dp", "fsdp"), None),
            P(("dp", "fsdp")),
            P(("dp", "fsdp"), None),
            P(("dp", "fsdp")),
        ),
        check_vma=False,
    )
```

```python
from functools import partial

import numpy as np
import jax
import jax.numpy as jnp
from jax import lax
from jax.experimental import pallas as pl
from jax.experimental.pallas import tpu as pltpu
from jax.sharding import PartitionSpec as P

def call(body, cover=False, **options):
    cost = pl.CostEstimate(flops=10**11 if cover else 1, transcendentals=0, bytes_accessed=1)
    return pl.pallas_call(body, cost_estimate=cost, **options)


EPSILON = 1e-06
HEAD_DIM = 64
LOG2E = 1.4426950408889634
RSQRT_2PI = 0.3989422804014327
SQRT_HALF = 0.7071067811865476
SCORE_SCALE = HEAD_DIM**-0.5 * LOG2E
NT = (((1,), (1,)), ((), ()))
TN = (((0,), (0,)), ((), ()))


def dot(a, b, dims=(((1,), (0,)), ((), ()))):
    return lax.dot_general(a, b, dims, preferred_element_type=jnp.float32)


def whole(shape):
    return pl.BlockSpec(shape, lambda *_: (0,) * len(shape))


def normal_cdf(u):
    return 0.5 + 0.5 * lax.erf(u * SQRT_HALF), jnp.exp2((-0.5 * LOG2E) * (u * u))


def row_stats(v):
    centre = v - jnp.mean(v, axis=-1, keepdims=True)
    inv = lax.rsqrt(jnp.mean(centre * centre, axis=-1, keepdims=True) + EPSILON)
    return centre * inv, inv


def norm_project(x, gain, shift, weight, bias, tn, cols):
    rows, width = x.shape

    def body(x_ref, g_ref, s_ref, w_ref, b_ref, a_ref, o_ref):
        @pl.when(pl.program_id(0) == 0)
        def _():
            xhat, _ = row_stats(x_ref[...].astype(jnp.float32))
            a_ref[...] = (xhat * g_ref[...] + s_ref[...]).astype(jnp.bfloat16)

        o_ref[...] = (dot(a_ref[...], w_ref[...]) + b_ref[...]).astype(jnp.bfloat16)

    return call(
        body,
        grid=(cols // tn,),
        in_specs=[
            whole((rows, width)),
            whole((1, width)),
            whole((1, width)),
            pl.BlockSpec((width, tn), lambda j: (0, j)),
            pl.BlockSpec((1, tn), lambda j: (0, j)),
        ],
        out_specs=[whole((rows, width)), pl.BlockSpec((rows, tn), lambda j: (0, j))],
        out_shape=[
            jax.ShapeDtypeStruct((rows, width), jnp.bfloat16),
            jax.ShapeDtypeStruct((rows, cols), jnp.bfloat16),
        ],
        name="norm_project",
    )(x, gain, shift, weight, bias)


def attention(qkv):
    rows, width = qkv.shape[0], qkv.shape[1] // 3
    pairs = width // (2 * HEAD_DIM)
    span = 2 * HEAD_DIM

    def body(q_ref, k_ref, v_ref, o_ref, l_ref):
        q, k, v = q_ref[...], k_ref[...], v_ref[...]
        lane = lax.broadcasted_iota(jnp.int32, (rows, span), 1)
        outs, logs = [], []
        for h in range(2):
            mine = (lane < HEAD_DIM) if h == 0 else (lane >= HEAD_DIM)
            kh = jnp.where(mine, k, jnp.zeros_like(k))
            s = dot(q, kh, NT)
            top = jnp.max(s, axis=-1, keepdims=True) * SCORE_SCALE
            e = jnp.exp2(s * SCORE_SCALE - top)
            total = jnp.sum(e, axis=-1, keepdims=True)
            outs.append(dot(e.astype(jnp.bfloat16), v) * (1.0 / total))
            logs.append(top + jnp.log2(total))
        first = lane < HEAD_DIM
        o_ref[...] = jnp.where(first, outs[0], outs[1]).astype(jnp.bfloat16)
        both = jnp.where(first, logs[0], logs[1])
        turned = both.T
        l_ref[0, 0:1, :] = turned[0:1, :]
        l_ref[0, 1:2, :] = turned[HEAD_DIM : HEAD_DIM + 1, :]

    col = lambda base: pl.BlockSpec((rows, span), lambda j: (0, base + j))
    return call(
        body,
        grid=(pairs,),
        in_specs=[col(0), col(pairs), col(2 * pairs)],
        out_specs=[col(0), pl.BlockSpec((1, 8, rows), lambda j: (j, 0, 0))],
        out_shape=[
            jax.ShapeDtypeStruct((rows, width), jnp.bfloat16),
            jax.ShapeDtypeStruct((pairs, 8, rows), jnp.float32),
        ],
        name="attention",
    )(qkv, qkv, qkv)


def attention_back(qkv, logs, d_o, first_pair, pairs, cover=True):
    rows, width = qkv.shape[0], qkv.shape[1] // 3
    every = width // (2 * HEAD_DIM)
    span = 2 * HEAD_DIM

    def body(q_ref, k_ref, v_ref, l_ref, do_ref, d_ref, cq_ref, cv_ref):
        q, k, v, do = q_ref[...], k_ref[...], v_ref[...], do_ref[...]
        lane = lax.broadcasted_iota(jnp.int32, (rows, span), 1)
        dqs, dks, dvs = [], [], []
        for h in range(2):
            mine = (lane < HEAD_DIM) if h == 0 else (lane >= HEAD_DIM)
            kh = jnp.where(mine, k, jnp.zeros_like(k))
            vh = jnp.where(mine, v, jnp.zeros_like(v))
            pt = jnp.exp2(dot(kh, q, NT) * SCORE_SCALE - l_ref[0, h : h + 1, :])
            w = pt * dot(vh, do, NT)
            dst = (w - pt * jnp.sum(w, axis=0, keepdims=True)).astype(jnp.bfloat16)
            dvs.append(dot(pt.astype(jnp.bfloat16), do))
            dks.append(dot(dst, q))
            dqs.append(dot(dst, k, TN))
        first = lane < HEAD_DIM
        dq = (jnp.where(first, dqs[0], dqs[1]) * 0.125).astype(jnp.bfloat16)
        dk = (jnp.where(first, dks[0], dks[1]) * 0.125).astype(jnp.bfloat16)
        dv = jnp.where(first, dvs[0], dvs[1]).astype(jnp.bfloat16)
        d_ref[0] = dq
        d_ref[1] = dk
        d_ref[2] = dv
        cq_ref[...] = jnp.sum(dq.astype(jnp.float32), axis=0, keepdims=True)
        cv_ref[...] = jnp.sum(dv.astype(jnp.float32), axis=0, keepdims=True)

    col = lambda base: pl.BlockSpec((rows, span), lambda j: (0, base + j))
    sums = pl.BlockSpec((1, span), lambda j: (0, j))
    vec_shape = jax.ShapeDtypeStruct((1, pairs * span), jnp.float32)
    return call(
        body,
        grid=(pairs,),
        in_specs=[
            col(first_pair),
            col(every + first_pair),
            col(2 * every + first_pair),
            pl.BlockSpec((1, 8, rows), lambda j: (first_pair + j, 0, 0)),
            col(first_pair),
        ],
        out_specs=[pl.BlockSpec((3, rows, span), lambda j: (0, 0, j)), sums, sums],
        out_shape=[
            jax.ShapeDtypeStruct((3, rows, pairs * span), jnp.bfloat16),
            vec_shape,
            vec_shape,
        ],
        name="attention_back",
        cover=cover,
    )(qkv, qkv, qkv, logs, d_o)


def project_norm(o, weight, bias, x, gain, shift, at):
    rows, width = o.shape
    tm = rows // 2

    def body(o_ref, w_ref, b_ref, x_ref, g_ref, s_ref, x1_ref, a_ref):
        x1 = x_ref[...].astype(jnp.float32) + (dot(o_ref[...], w_ref[...]) + b_ref[...])
        x1_ref[...] = x1
        xhat, _ = row_stats(x1)
        a_ref[...] = (xhat * g_ref[...] + s_ref[...]).astype(jnp.bfloat16)

    rowblk = pl.BlockSpec((tm, width), lambda i: (i, 0))
    vec = whole((1, width))
    return call(
        body,
        grid=(rows // tm,),
        in_specs=[rowblk, pl.BlockSpec((width, width), lambda i: (0, at // width)), vec, rowblk, vec, vec],
        out_specs=[rowblk, rowblk],
        out_shape=[
            jax.ShapeDtypeStruct((rows, width), jnp.float32),
            jax.ShapeDtypeStruct((rows, width), jnp.bfloat16),
        ],
        name="project_norm",
    )(o, weight, bias, x, gain, shift)


def flat(ref):
    return ref[...].reshape(-1, ref.shape[-1])


def up_spec(packed, r_in):
    n, _, width = packed.shape
    return pl.BlockSpec((n, r_in, width), lambda j: (0, j, 0))


def down_spec(packed, r_ff):
    width = packed.shape[2]
    return pl.BlockSpec((width // r_ff, r_ff, width), lambda j: (j, 1, 0))


def feed_forward(a, packed, r_in, r_ff, up_bias, down_bias, x1):
    rows, width = a.shape
    hidden = up_bias.shape[1]
    tf = width
    steps = hidden // tf

    def body(a_ref, u_ref, ub_ref, d_ref, db_ref, x_ref, g_ref, gp_ref, y_ref, acc):
        j = pl.program_id(0)
        u = dot(a_ref[...], flat(u_ref)) + ub_ref[...]
        phi, bell = normal_cdf(u)
        g = (u * phi).astype(jnp.bfloat16)
        g_ref[...] = g
        gp_ref[...] = (phi + (u * RSQRT_2PI) * bell).astype(jnp.bfloat16)

        @pl.when(j == 0)
        def _():
            acc[...] = x_ref[...] + db_ref[...]

        acc[...] += dot(g, flat(d_ref))

        @pl.when(j == steps - 1)
        def _():
            y_ref[...] = acc[...].astype(jnp.bfloat16)

    return call(
        body,
        grid=(steps,),
        in_specs=[
            whole((rows, width)),
            up_spec(packed, r_in),
            pl.BlockSpec((1, tf), lambda j: (0, j)),
            down_spec(packed, r_ff),
            whole((1, width)),
            whole((rows, width)),
        ],
        out_specs=[
            pl.BlockSpec((rows, tf), lambda j: (0, j)),
            pl.BlockSpec((rows, tf), lambda j: (0, j)),
            whole((rows, width)),
        ],
        out_shape=[
            jax.ShapeDtypeStruct((rows, hidden), jnp.bfloat16),
            jax.ShapeDtypeStruct((rows, hidden), jnp.bfloat16),
            jax.ShapeDtypeStruct((rows, width), jnp.bfloat16),
        ],
        scratch_shapes=[pltpu.VMEM((rows, width), jnp.float32)],
        name="feed_forward",
    )(a, packed, up_bias, packed, down_bias, x1)


def feed_forward_in(a, packed, r_in, up_bias):
    rows, width = a.shape
    hidden = up_bias.shape[1]

    def body(a_ref, u_ref, ub_ref, g_ref, gp_ref):
        u = dot(a_ref[...], flat(u_ref)) + ub_ref[...]
        phi, bell = normal_cdf(u)
        g_ref[...] = (u * phi).astype(jnp.bfloat16)
        gp_ref[...] = (phi + (u * RSQRT_2PI) * bell).astype(jnp.bfloat16)

    block = pl.BlockSpec((rows, width), lambda j: (0, j))
    return call(
        body,
        grid=(hidden // width,),
        in_specs=[
            whole((rows, width)),
            up_spec(packed, r_in),
            pl.BlockSpec((1, width), lambda j: (0, j)),
        ],
        out_specs=[block, block],
        out_shape=[jax.ShapeDtypeStruct((rows, hidden), jnp.bfloat16)] * 2,
        name="feed_forward_in",
    )(a, packed, up_bias)


def feed_forward_out(g, packed, r_ff, down_bias, x1):
    rows, width = x1.shape
    steps = g.shape[1] // width

    def body(g_ref, d_ref, db_ref, x_ref, y_ref, acc):
        j = pl.program_id(0)

        @pl.when(j == 0)
        def _():
            acc[...] = x_ref[...] + db_ref[...]

        acc[...] += dot(g_ref[...], flat(d_ref))

        @pl.when(j == steps - 1)
        def _():
            y_ref[...] = acc[...].astype(jnp.bfloat16)

    return call(
        body,
        grid=(steps,),
        in_specs=[
            pl.BlockSpec((rows, width), lambda j: (0, j)),
            down_spec(packed, r_ff),
            whole((1, width)),
            whole((rows, width)),
        ],
        out_specs=whole((rows, width)),
        out_shape=jax.ShapeDtypeStruct((rows, width), jnp.bfloat16),
        scratch_shapes=[pltpu.VMEM((rows, width), jnp.float32)],
        name="feed_forward_out",
    )(g, packed, down_bias, x1)


def feed_forward_back(dy, gp, packed, r_in, r_ff, x1, gain, w_out, at):
    rows, width = dy.shape
    hidden = gp.shape[1]
    tf = width
    steps = hidden // tf

    def body(
        dy_ref, gp_ref, d_ref, u_ref, x_ref, g_ref, w_ref,
        dm_ref, du_ref, dx_ref, da_ref, do_ref, cdm_ref, cdu_ref, cda_ref, cg_ref, cs_ref, acc,
    ):
        j = pl.program_id(0)

        @pl.when(j == 0)
        def _():
            low = dy_ref[...].astype(jnp.bfloat16)
            dm_ref[...] = low
            cdm_ref[...] = jnp.sum(low.astype(jnp.float32), axis=0, keepdims=True)
            acc[...] = jnp.zeros_like(acc)

        du = (dot(dm_ref[...], flat(d_ref), NT) * gp_ref[...].astype(jnp.float32)).astype(jnp.bfloat16)
        du_ref[...] = du
        cdu_ref[...] = jnp.sum(du.astype(jnp.float32), axis=0, keepdims=True)
        acc[...] += dot(du, flat(u_ref), NT)

        @pl.when(j == steps - 1)
        def _():
            da2 = acc[...]
            xhat, inv = row_stats(x_ref[...])
            cg_ref[...] = jnp.sum(da2 * xhat, axis=0, keepdims=True)
            cs_ref[...] = jnp.sum(da2, axis=0, keepdims=True)
            t = da2 * g_ref[...]
            m1 = jnp.mean(t, axis=-1, keepdims=True)
            m2 = jnp.mean(t * xhat, axis=-1, keepdims=True)
            dx1 = dy_ref[...] + inv * (t - m1 - xhat * m2)
            dx_ref[...] = dx1
            low = dx1.astype(jnp.bfloat16)
            da_ref[...] = low
            cda_ref[...] = jnp.sum(low.astype(jnp.float32), axis=0, keepdims=True)
            do_ref[...] = dot(low, w_ref[...], NT).astype(jnp.bfloat16)

    full = whole((rows, width))
    vec = whole((1, width))
    f = lambda s, d: jax.ShapeDtypeStruct(s, d)
    return call(
        body,
        grid=(steps,),
        in_specs=[
            full,
            pl.BlockSpec((rows, tf), lambda j: (0, j)),
            down_spec(packed, r_ff),
            up_spec(packed, r_in),
            full,
            vec,
            pl.BlockSpec((width, width), lambda j: (0, at // width)),
        ],
        out_specs=[
            full,
            pl.BlockSpec((rows, tf), lambda j: (0, j)),
            full,
            full,
            full,
            vec,
            pl.BlockSpec((1, tf), lambda j: (0, j)),
            vec,
            vec,
            vec,
        ],
        out_shape=[
            f((rows, width), jnp.bfloat16),
            f((rows, hidden), jnp.bfloat16),
            f((rows, width), jnp.float32),
            f((rows, width), jnp.bfloat16),
            f((rows, width), jnp.bfloat16),
            f((1, width), jnp.float32),
            f((1, hidden), jnp.float32),
            f((1, width), jnp.float32),
            f((1, width), jnp.float32),
            f((1, width), jnp.float32),
        ],
        scratch_shapes=[pltpu.VMEM((rows, width), jnp.float32)],
        name="feed_forward_back",
        cover=True,
    )(dy, gp, packed, packed, x1, gain, w_out)


def project_back(grads, weight, x, gain, dx1, extra, dtypes):
    rows, width = x.shape
    tm = rows // 2
    have = extra is not None
    count = len(grads)
    part = width // count

    def body(*refs):
        d_refs = refs[:count]
        w_ref, x_ref, g_ref, dx_ref = refs[count : count + 4]
        more = refs[count + 4 : -2 - len(dtypes)]
        out_refs = refs[-2 - len(dtypes) : -2]
        cg_ref, cs_ref = refs[-2:]
        da = None
        for kind in range(3):
            for i in range(count):
                at = kind * width + i * part
                term = dot(d_refs[i][kind], w_ref[:, at : at + part], NT)
                da = term if da is None else da + term
        xhat, inv = row_stats(x_ref[...].astype(jnp.float32))
        cg = jnp.sum(da * xhat, axis=0, keepdims=True)
        cs = jnp.sum(da, axis=0, keepdims=True)

        @pl.when(pl.program_id(0) == 0)
        def _():
            cg_ref[...] = cg
            cs_ref[...] = cs

        @pl.when(pl.program_id(0) > 0)
        def _():
            cg_ref[...] += cg
            cs_ref[...] += cs

        t = da * g_ref[...]
        m1 = jnp.mean(t, axis=-1, keepdims=True)
        m2 = jnp.mean(t * xhat, axis=-1, keepdims=True)
        dx = dx_ref[...] + inv * (t - m1 - xhat * m2)
        if have:
            dx = more[0][...].astype(jnp.float32) * more[1][...] + dx
        for ref in out_refs:
            ref[...] = dx.astype(ref.dtype)

    rowblk = pl.BlockSpec((tm, width), lambda i: (i, 0))
    vec_spec = whole((1, width))
    specs = [pl.BlockSpec((3, tm, part), lambda i: (0, i, 0))] * count
    specs += [whole((width, 3 * width)), rowblk, vec_spec, rowblk]
    args = list(grads) + [weight, x, gain, dx1]
    if have:
        specs += [rowblk, pl.BlockSpec((tm, 1), lambda i: (i, 0))]
        args += list(extra)
    return call(
        body,
        grid=(rows // tm,),
        in_specs=specs,
        out_specs=[rowblk] * len(dtypes) + [vec_spec, vec_spec],
        out_shape=[
            *[jax.ShapeDtypeStruct((rows, width), d) for d in dtypes],
            jax.ShapeDtypeStruct((1, width), jnp.float32),
            jax.ShapeDtypeStruct((1, width), jnp.float32),
        ],
        name="project_back",
        cover=True,
    )(*args)


def weight_grad(jobs, index, blocks, chunk, cover=False):
    ndp, nfs, r = blocks
    npos = ndp * nfs // 2
    rows = jobs[0][0][0].shape[0]
    widths = [rs[0].shape[-1] * (3 if rs[0].ndim == 3 else 1) for _, rs in jobs]
    starts = [sum(widths[:k]) for k in range(len(jobs))]
    counts = [len(ls) for ls, _ in jobs]
    steps = ndp * len(jobs)

    def body(i_ref, *refs):
        sent, kept, buf, sem = refs[-4:]
        i = pl.program_id(0)

        def copies(step, start):
            local = step % ndp
            for k in range(len(jobs)):
                for which, where in ((local < ndp // 2, sent), (local >= ndp // 2, kept)):

                    @pl.when((step // ndp == k) & which)
                    def _():
                        for f in range(nfs):
                            p = i_ref[ndp + local * nfs + f]
                            copy = pltpu.make_async_copy(
                                buf.at[step % 2, f, :, 0 : widths[k]],
                                where.at[p, :, starts[k] : starts[k] + widths[k]],
                                sem.at[step % 2, f],
                            )
                            copy.start() if start else copy.wait()

        @pl.when(i >= 2)
        def _():
            copies(i - 2, False)

        at_ref = 0
        for k in range(len(jobs)):
            a = refs[at_ref : at_ref + counts[k]]
            b = refs[at_ref + counts[k] : at_ref + 2 * counts[k]]
            at_ref += 2 * counts[k]

            @pl.when(i // ndp == k)
            def _():
                for at in range(0, widths[k], chunk):
                    part = b[0].shape[-1]
                    if len(b[0].shape) == 3:
                        take = lambda ref: ref[at // part, :, at % part : at % part + chunk]
                    else:
                        take = lambda ref: ref[:, at : at + chunk]
                    total = dot(a[0][...], take(b[0]), TN)
                    for x, y in zip(a[1:], b[1:]):
                        total += dot(x[...], take(y), TN)
                    total = total.astype(jnp.bfloat16).reshape(nfs, r, chunk)
                    buf[i % 2, :, :, at : at + chunk] = total

        copies(i, True)

        @pl.when(i == steps - 1)
        def _():
            copies(steps - 2, False)
            copies(steps - 1, False)

    def left_spec(k):
        step = lambda i: jnp.clip(i - k * ndp, 0, ndp - 1)
        return pl.BlockSpec((rows, nfs * r), lambda i, i_ref: (0, i_ref[step(i)]))

    anywhere = pl.BlockSpec(memory_space=pl.ANY)
    specs, args = [], []
    for k, (ls, rs) in enumerate(jobs):
        specs += [left_spec(k)] * len(ls) + [whole(rs[0].shape)] * len(rs)
        args += list(ls) + list(rs)
    return call(
        body,
        grid_spec=pltpu.PrefetchScalarGridSpec(
            num_scalar_prefetch=1,
            grid=(steps,),
            in_specs=specs,
            out_specs=[anywhere] * 2,
            scratch_shapes=[
                pltpu.VMEM((2, nfs, r, max(widths)), jnp.bfloat16),
                pltpu.SemaphoreType.DMA((2, nfs)),
            ],
        ),
        out_shape=[jax.ShapeDtypeStruct((npos, r, sum(widths)), jnp.bfloat16)] * 2,
        name="weight_grad",
        cover=cover,
    )(index, *args)


def bits_of(ndp, nfs):
    core = nfs
    outer = [nfs << i for i in range(1, ndp.bit_length() - 1)]
    inner = [1 << i for i in range(nfs.bit_length() - 1)]
    return core, outer, inner


def stage_orders(ndp, nfs):
    core, outer, inner = bits_of(ndp, nfs)
    first, second = outer[0], inner[0]
    tail = outer[1:] + inner[1:]
    return core, ([first, second] + tail, [second, first] + tail)


def shard_table(ndp, nfs):
    n = ndp * nfs
    core, orders = stage_orders(ndp, nfs)
    table = np.zeros((n, n), np.int32)
    for me in range(n):
        for p in range(n):
            rel = core if p >= n // 2 else 0
            owner = 1 if (me ^ rel) & core else 0
            for i, mask in enumerate(orders[owner]):
                if p & (n >> (i + 2)):
                    rel ^= mask
            table[me, p] = me ^ rel
    return table


def stage_perms(ndp, nfs):
    n = ndp * nfs
    core, orders = stage_orders(ndp, nfs)
    perms = [[(i, i ^ core) for i in range(n)]]
    for a, b in zip(*orders):
        perms.append([(i, i ^ (b if i & core else a)) for i in range(n)])
    return perms


AXES = ("dp", "fsdp")


def send(x, perm):
    return lax.ppermute(x, AXES, perm)


class Line:
    def __init__(self):
        self.last = None

    def after(self, *arrays):
        if self.last is not None:
            arrays = lax.optimization_barrier((self.last,) + arrays)[1:]
        return arrays

    def mark(self, array):
        self.last = array


def place_shards(pieces, table_row, shape, rows_at, rows, into=None, cover=False):
    count = sum(a.shape[0] for a, _ in pieces)
    cols = shape[-1]

    def body(t_ref, *refs):
        ins, out, (buf, in_sem, out_sem) = refs[: len(pieces)], refs[-4], refs[-3:]
        loads, stores = [], []
        for ref, (array, first) in zip(ins, pieces):
            for k in range(array.shape[0]):
                i = len(loads)
                source = ref.at[k, :, 0:cols]
                loads.append(pltpu.make_async_copy(source, buf.at[i], in_sem.at[i]))
                target = out.at[t_ref[first + k], rows_at : rows_at + rows]
                stores.append(pltpu.make_async_copy(buf.at[i], target, out_sem.at[i]))
        for c in loads:
            c.start()
        for a, b in zip(loads, stores):
            a.wait()
            b.start()
        for b in stores:
            b.wait()

    anywhere = pl.BlockSpec(memory_space=pl.ANY)
    args = [a for a, _ in pieces] + ([] if into is None else [into])
    return call(
        body,
        out_shape=jax.ShapeDtypeStruct(shape, jnp.bfloat16),
        grid_spec=pltpu.PrefetchScalarGridSpec(
            num_scalar_prefetch=1,
            in_specs=[anywhere] * len(args),
            out_specs=anywhere,
            scratch_shapes=[pltpu.VMEM((count, rows, cols), jnp.bfloat16)]
            + [pltpu.SemaphoreType.DMA((count,))] * 2,
        ),
        input_output_aliases={} if into is None else {len(args): 0},
        name="place_shards",
        cover=cover,
    )(table_row, *args)


def pack_shard(matrices, vectors):
    rows = matrices[0].shape[0]
    widths = [m.shape[1] for m in matrices]
    lanes = 128 * -(-len(vectors) // 8)

    def body(*refs):
        out, scr = refs[-2:]
        at = 0
        for ref, width in zip(refs, widths):
            out[:, at : at + width] = ref[...]
            at += width
        scr[...] = jnp.zeros_like(scr)
        for r, ref in enumerate(refs[len(widths) : -2]):
            k, col = ref.shape[1], 128 * (r // 8)
            scr[r % 8 : r % 8 + 1, col : col + k] = ref[...].astype(jnp.float32)
        out[:, at:] = scr[...].astype(jnp.bfloat16)

    vectors = [v.reshape(1, -1) for v in vectors]
    cols = sum(widths) + lanes
    return call(
        body,
        grid=(1,),
        in_specs=[whole(a.shape) for a in (*matrices, *vectors)],
        out_specs=whole((rows, cols)),
        out_shape=jax.ShapeDtypeStruct((rows, cols), jnp.bfloat16),
        scratch_shapes=[pltpu.VMEM((rows, lanes), jnp.float32)],
        name="pack_shard",
    )(*matrices, *vectors)


def unpack_vectors(pieces, at, inverse_row, sizes, layout):
    per_piece = pieces[0].shape[0]
    n = per_piece * len(pieces)
    lanes = pieces[0].shape[2] - at

    def body(i_ref, *refs):
        ins, outs, scr = refs[: len(pieces)], refs[len(pieces) : -1], refs[-1]
        for i, ref in enumerate(ins):
            scr[i * per_piece : (i + 1) * per_piece] = ref[...].astype(jnp.float32)
        for rows, out in zip(layout, outs):
            col = 0
            for r in rows:
                k = sizes[0] if r is None else sizes[r]
                per = 128 // k if k < 128 else 1
                for d in range(0, n, per):
                    if r is None:
                        value = jnp.zeros((1, per * k), jnp.float32)
                    else:
                        row, lane = r % 8, 128 * (r // 8)
                        value = jnp.concatenate(
                            [
                                scr[i_ref[d + e], row : row + 1, lane : lane + k]
                                for e in range(per)
                            ],
                            axis=1,
                        )
                    out[0:1, col + d * k : col + (d + per) * k] = value
                col += n * k

    widths = [sum(n * (sizes[0] if r is None else sizes[r]) for r in rows) for rows in layout]
    return call(
        body,
        grid_spec=pltpu.PrefetchScalarGridSpec(
            num_scalar_prefetch=1,
            grid=(1,),
            in_specs=[pl.BlockSpec((per_piece, 8, lanes), lambda i, i_ref: (0, 0, at // lanes))]
            * len(pieces),
            out_specs=[pl.BlockSpec((1, w), lambda i, i_ref: (0, 0)) for w in widths],
            scratch_shapes=[pltpu.VMEM((n, 8, lanes), jnp.float32)],
        ),
        out_shape=[jax.ShapeDtypeStruct((1, w), jnp.float32) for w in widths],
        name="unpack_vectors",
    )(inverse_row, *pieces)


def pack_sums(parts, inverse_row, n, rows):
    flat = [a for group in parts for a in group]

    def body(i_ref, *refs):
        out = refs[-1]
        out[...] = jnp.zeros_like(out)
        at = 0
        for r, group in enumerate(parts):
            total = refs[at][...]
            for k in range(1, len(group)):
                total += refs[at + k][...]
            at += len(group)
            k = total.shape[1] // n
            for d in range(n):
                out[i_ref[d], r : r + 1, 0:k] = total[:, d * k : (d + 1) * k]

    return call(
        body,
        grid_spec=pltpu.PrefetchScalarGridSpec(
            num_scalar_prefetch=1,
            grid=(1,),
            in_specs=[whole(a.shape) for a in flat],
            out_specs=whole((n, rows, 128)),
        ),
        out_shape=jax.ShapeDtypeStruct((n, rows, 128), jnp.float32),
        name="pack_sums",
        cover=True,
    )(inverse_row, *flat)


class Reduction:
    def __init__(self, perms, kept, sent, stage):
        self.perms, self.stage = perms, stage
        self.kept, self.got = kept, send(sent, perms[stage])
        self.done = None

    def step(self, line, wide=jnp.bfloat16):
        kept, got = line.after(self.kept, self.got)
        add = lambda part: kept[part].astype(jnp.float32) + got[part].astype(jnp.float32)
        self.stage += 1
        if self.stage == len(self.perms):
            self.done = add(slice(None))[0]
            line.mark(self.done)
            return
        half = kept.shape[0] // 2
        sent = add(slice(half, None)).astype(wide)
        self.got = send(sent, self.perms[self.stage])
        self.kept = add(slice(0, half)).astype(wide)
        line.mark(self.kept)


def per_device(ndp, nfs,
    tokens,
    ln1_gain,
    ln1_bias,
    w_qkv,
    bias_q,
    bias_v,
    w_out,
    bias_out,
    ln2_gain,
    ln2_bias,
    w_up,
    bias_up,
    w_down,
    bias_down,
    cot_first,
    cot_second,
    valid,
):
    n = ndp * nfs
    perms = stage_perms(ndp, nfs)
    gather_perms = perms[:0:-1]
    core_perm = perms[0]
    stages = len(gather_perms)
    table = shard_table(ndp, nfs)
    me = lax.axis_index("dp") * nfs + lax.axis_index("fsdp")
    both = np.concatenate([table, np.argsort(table, axis=1).astype(np.int32)], axis=1)
    both = lax.dynamic_slice(jnp.asarray(both), (me, 0), (1, 2 * n))[0]
    row, inverse_row = both[:n], both[n:]
    rows_in, width = tokens.shape[1:]
    r_in, r_ff = w_up.shape[0], w_down.shape[0]
    hidden = w_up.shape[1]

    vectors = (ln1_gain, ln1_bias, bias_q, bias_v, bias_out, ln2_gain, ln2_bias, bias_down, bias_up)
    sizes = [v.shape[0] for v in vectors]
    line = Line()
    qkv_cols = w_qkv.shape[1]
    cols = qkv_cols + w_out.shape[1]
    ahead = pack_shard([w_qkv, w_out], vectors)
    split = w_up.reshape(r_in, hidden // width, width).swapaxes(0, 1).reshape(r_ff, width)

    class Gather:
        def __init__(self, shard):
            self.held, self.stage = shard[None], 0
            (self.held,) = line.after(self.held)
            self.got = send(self.held, gather_perms[0])

        def step(self):
            mine, theirs = line.after(self.held, self.got)
            self.held = jnp.concatenate([mine, theirs], axis=0)
            line.mark(self.held)
            self.stage += 1
            self.got = send(self.held, gather_perms[self.stage])
            if self.stage == stages - 1:
                self.early = send(self.held, core_perm)

        def finish(self):
            (self.got,) = line.after(self.got)
            self.late = send(self.got, core_perm)

        def place(self, which, *where, into=None, cover=False):
            quarter = n // 4
            pair = (self.got, self.late) if which else (self.held, self.early)
            pair = line.after(*pair)
            pieces = [(pair[0], which * quarter), (pair[1], half + which * quarter)]
            out = place_shards(pieces, row, *where, into=into, cover=cover)
            line.mark(out)
            return out

    half = n // 2
    chain_a = Gather(ahead)
    for k in range(1, stages - 2):
        chain_a.step()
    chain_b = Gather(split)
    chain_a.step()
    for k in range(1, stages - 2):
        chain_b.step()
    chain_a.step()
    chain_b.step()
    chain_c = Gather(w_down)
    spot_a = ((n, r_in, cols), 0, r_in)
    first = chain_a.place(0, *spot_a, cover=True)
    for k in range(1, stages - 2):
        chain_c.step()
    chain_b.step()
    chain_a.finish()
    first = chain_a.place(1, *spot_a, into=first)
    w = {"first": first.reshape(n * r_in, cols)}
    g1, s1, bqkv, bo, g2, s2, bd, bu = unpack_vectors(
        (chain_a.held, chain_a.got, chain_a.early, chain_a.late),
        cols,
        inverse_row,
        sizes,
        [[0], [1], [2, None, 3], [4], [5], [6], [7], [8]],
    )
    spot_b = ((n, 2 * r_ff, width), 0, r_ff)
    spot_c = ((n, 2 * r_ff, width), r_ff, r_ff)

    def more(index):
        if index == 0:
            chain_c.step()
        if index == 1:
            chain_b.finish()
        if index == 2:
            chain_c.step()
            ff = chain_b.place(0, *spot_b)
            w["ff"] = chain_b.place(1, *spot_b, into=ff)
        if index == 3:
            ff = chain_c.place(0, *spot_c, into=w["ff"])
            chain_c.finish()
            w["ff"] = chain_c.place(1, *spot_c, into=ff)

    def forward(x, more=None):
        a1, qkv = norm_project(*line.after(x), g1, s1, w["first"], bqkv, qkv_cols // 2, qkv_cols)
        line.mark(a1)
        if more:
            more(0)
        o, logs = attention(*line.after(qkv))
        line.mark(o)
        if more:
            more(1)
        x1, a2 = project_norm(*line.after(o), w["first"], bo, x, g2, s2, qkv_cols)
        line.mark(a2)
        if more:
            more(2)
        a2 = line.after(a2)[0]
        if more is None:
            g, gp, y = feed_forward(a2, w["ff"], r_in, r_ff, bu, bd, x1)
        else:
            g, gp = feed_forward_in(a2, w["ff"], r_in, bu)
            line.mark(g)
            more(3)
            y = feed_forward_out(line.after(g)[0], w["ff"], r_ff, bd, x1)
        line.mark(y)
        return y, (x, a1, qkv, logs, o, x1, a2, g, gp)

    first, saved_first = forward(tokens[0], more)
    second, saved_second = forward(first)

    keep_mask = valid[0].astype(jnp.float32)[:, None]
    grad_second = cot_second[0].astype(jnp.float32) * keep_mask
    pairs = width // (2 * HEAD_DIM)
    parts = 2

    def ff_back(dy, saved):
        x, a1, qkv, logs, o, x1, a2, g, gp = saved
        outs = feed_forward_back(
            *line.after(dy), gp, w["ff"], r_in, r_ff, x1, g2, w["first"], qkv_cols
        )
        line.mark(outs[0])
        return outs

    def heads_back(saved, d_o, i, cover=True):
        outs = attention_back(
            saved[2], saved[3], *line.after(d_o), i * pairs // parts, pairs // parts, cover
        )
        line.mark(outs[0])
        return outs

    def qkv_back(heads, saved, dx1, extra, dtypes):
        outs = project_back(
            [line.after(h[0])[0] for h in heads], w["first"], saved[0], g1, dx1, extra, dtypes
        )
        line.mark(outs[0])
        return outs

    dm2, du2, dx2, da2, do2, cdm2, cdu2, cda2, cg22, cs22 = ff_back(grad_second, saved_second)
    heads2 = [heads_back(saved_second, do2, i) for i in range(parts)]
    grad_first, dm1, cg12, cs12 = qkv_back(
        heads2, saved_second, dx2, (cot_first[0], keep_mask), (jnp.float32, jnp.bfloat16)
    )

    core = (me // nfs) % 2
    evens = 2 * jnp.arange(ndp // 2, dtype=jnp.int32)
    lefts_at = jnp.concatenate([evens + (1 - core), evens + core])
    shards_at = lefts_at[:, None] * nfs + jnp.arange(nfs, dtype=jnp.int32)
    index = jnp.concatenate([lefts_at, inverse_row[shards_at.reshape(-1)] % half])
    index = index.astype(jnp.int32)

    def grads(r, *jobs, cover=False):
        jobs = [(line.after(*ls), rs) for ls, rs in jobs]
        sent, kept = weight_grad(jobs, index, (ndp, nfs, r), 512, cover)
        line.mark(sent)
        return Reduction(perms, kept, sent, 0)

    sg = list(zip(saved_first, saved_second))
    red_down = grads(r_ff, (sg[7], (dm1, dm2)))
    _, du1, dx1, da1, do1, cdm1, cdu1, cda1, cg21, cs21 = ff_back(grad_first, saved_first)
    red_down.step(line)
    red_up = grads(r_in, (sg[6], (du1, du2)))
    red_down.step(line)
    heads1 = [heads_back(saved_first, do1, 0)]
    rights = lambda i: (heads1[i][0], heads2[i][0])
    red_down.step(line)
    red_up.step(line)
    red_one = grads(r_in, (sg[4], (da1, da2)), (sg[1], rights(0)))
    heads1.append(heads_back(saved_first, do1, 1, False))
    red_up.step(line)
    red_down.step(line)
    red_two = grads(r_in, (sg[1], rights(1)), cover=True)
    red_one.step(line)
    red_up.step(line)
    grad_inputs, cg11, cs11 = qkv_back(heads1, saved_first, dx1, None, (jnp.bfloat16,))
    red_two.step(line)
    red_one.step(line)
    red_up.step(line)
    red_down.step(line)
    cq = [[h[i][1] for h in (heads1, heads2)] for i in range(parts)]
    cv = [[h[i][2] for h in (heads1, heads2)] for i in range(parts)]
    joined = lambda c: [jnp.concatenate([c[i][s] for i in range(parts)], axis=1) for s in range(2)]
    sums = pack_sums(
        [
            [cg11, cg12],
            [cs11, cs12],
            joined(cq),
            joined(cv),
            [cda1, cda2],
            [cg21, cg22],
            [cs21, cs22],
            [cdm1, cdm2],
            [cdu1, cdu2],
        ],
        inverse_row,
        n,
        len(vectors),
    )
    red_small = Reduction(perms, sums[:half], sums[half:], 0)
    for _ in range(stages):
        for red in (red_two, red_one, red_up, red_down):
            if red.done is None:
                red.step(line)
        if red_small.done is None:
            red_small.step(line, jnp.float32)
    for red in (red_down, red_up, red_one, red_two):
        while red.done is None:
            red.step(line)
    while red_small.done is None:
        red_small.step(line, jnp.float32)
    outs = [red_small.done[i, : sizes[i]] for i in range(len(vectors))]
    o_g1, o_s1, o_bq, o_bv, o_bo, o_g2, o_s2, o_bd, o_bu = outs
    one = red_one.done
    d_out = one[:, :width]
    third = width // parts
    blocks = []
    for kind in range(3):
        blocks.append(one[:, width + kind * third : width + (kind + 1) * third])
        blocks.append(red_two.done[:, kind * third : (kind + 1) * third])
    d_qkv = jnp.concatenate(blocks, axis=1)
    return (
        first[None],
        second[None],
        grad_inputs[None],
        o_g1,
        o_s1,
        d_qkv,
        o_bq,
        o_bv,
        d_out,
        o_bo,
        o_g2,
        o_s2,
        red_up.done,
        o_bu,
        red_down.done,
        o_bd,
    )


def solution(mesh):
    ndp, nfs = mesh.shape["dp"], mesh.shape["fsdp"]
    return jax.shard_map(
        partial(per_device, ndp, nfs),
        mesh=mesh,
        in_specs=(
            P(("dp", "fsdp"), None, None),
            P(("dp", "fsdp")),
            P(("dp", "fsdp")),
            P(("dp", "fsdp"), None),
            P(("dp", "fsdp")),
            P(("dp", "fsdp")),
            P(("dp", "fsdp"), None),
            P(("dp", "fsdp")),
            P(("dp", "fsdp")),
            P(("dp", "fsdp")),
            P(("dp", "fsdp"), None),
            P(("dp", "fsdp")),
            P(("dp", "fsdp"), None),
            P(("dp", "fsdp")),
            P(("dp", "fsdp"), None, None),
            P(("dp", "fsdp"), None, None),
            P(("dp", "fsdp"), None),
        ),
        out_specs=(
            P(("dp", "fsdp"), None, None),
            P(("dp", "fsdp"), None, None),
            P(("dp", "fsdp"), None, None),
            P(("dp", "fsdp")),
            P(("dp", "fsdp")),
            P(("dp", "fsdp"), None),
            P(("dp", "fsdp")),
            P(("dp", "fsdp")),
            P(("dp", "fsdp"), None),
            P(("dp", "fsdp")),
            P(("dp", "fsdp")),
            P(("dp", "fsdp")),
            P(("dp", "fsdp"), None),
            P(("dp", "fsdp")),
            P(("dp", "fsdp"), None),
            P(("dp", "fsdp")),
        ),
        check_vma=False,
    )
```

```python
from functools import partial

import numpy as np
import jax
import jax.numpy as jnp
from jax import lax
from jax.experimental import pallas as pl
from jax.experimental.pallas import tpu as pltpu
from jax.sharding import PartitionSpec as P

def call(body, cover=False, **options):
    cost = pl.CostEstimate(flops=10**11 if cover else 1, transcendentals=0, bytes_accessed=1)
    return pl.pallas_call(body, cost_estimate=cost, **options)


EPSILON = 1e-06
HEAD_DIM = 64
LOG2E = 1.4426950408889634
RSQRT_2PI = 0.3989422804014327
SQRT_HALF = 0.7071067811865476
SCORE_SCALE = HEAD_DIM**-0.5 * LOG2E
NT = (((1,), (1,)), ((), ()))
TN = (((0,), (0,)), ((), ()))


def dot(a, b, dims=(((1,), (0,)), ((), ()))):
    return lax.dot_general(a, b, dims, preferred_element_type=jnp.float32)


def whole(shape):
    return pl.BlockSpec(shape, lambda *_: (0,) * len(shape))


def normal_cdf(u):
    return 0.5 + 0.5 * lax.erf(u * SQRT_HALF), jnp.exp2((-0.5 * LOG2E) * (u * u))


def row_stats(v):
    centre = v - jnp.mean(v, axis=-1, keepdims=True)
    inv = lax.rsqrt(jnp.mean(centre * centre, axis=-1, keepdims=True) + EPSILON)
    return centre * inv, inv


def norm_project(x, gain, shift, weight, bias, tn, cols):
    rows, width = x.shape

    def body(x_ref, g_ref, s_ref, w_ref, b_ref, a_ref, o_ref):
        @pl.when(pl.program_id(0) == 0)
        def _():
            xhat, _ = row_stats(x_ref[...].astype(jnp.float32))
            a_ref[...] = (xhat * g_ref[...] + s_ref[...]).astype(jnp.bfloat16)

        o_ref[...] = (dot(a_ref[...], w_ref[...]) + b_ref[...]).astype(jnp.bfloat16)

    return call(
        body,
        grid=(cols // tn,),
        in_specs=[
            whole((rows, width)),
            whole((1, width)),
            whole((1, width)),
            pl.BlockSpec((width, tn), lambda j: (0, j)),
            pl.BlockSpec((1, tn), lambda j: (0, j)),
        ],
        out_specs=[whole((rows, width)), pl.BlockSpec((rows, tn), lambda j: (0, j))],
        out_shape=[
            jax.ShapeDtypeStruct((rows, width), jnp.bfloat16),
            jax.ShapeDtypeStruct((rows, cols), jnp.bfloat16),
        ],
        name="norm_project",
    )(x, gain, shift, weight, bias)


def attention(qkv):
    rows, width = qkv.shape[0], qkv.shape[1] // 3
    pairs = width // (2 * HEAD_DIM)
    span = 2 * HEAD_DIM

    def body(q_ref, k_ref, v_ref, o_ref, l_ref):
        q, k, v = q_ref[...], k_ref[...], v_ref[...]
        lane = lax.broadcasted_iota(jnp.int32, (rows, span), 1)
        outs, logs = [], []
        for h in range(2):
            mine = (lane < HEAD_DIM) if h == 0 else (lane >= HEAD_DIM)
            kh = jnp.where(mine, k, jnp.zeros_like(k))
            s = dot(q, kh, NT)
            top = jnp.max(s, axis=-1, keepdims=True) * SCORE_SCALE
            e = jnp.exp2(s * SCORE_SCALE - top)
            total = jnp.sum(e, axis=-1, keepdims=True)
            outs.append(dot(e.astype(jnp.bfloat16), v) * (1.0 / total))
            logs.append(top + jnp.log2(total))
        first = lane < HEAD_DIM
        o_ref[...] = jnp.where(first, outs[0], outs[1]).astype(jnp.bfloat16)
        both = jnp.where(first, logs[0], logs[1])
        turned = both.T
        l_ref[0, 0:1, :] = turned[0:1, :]
        l_ref[0, 1:2, :] = turned[HEAD_DIM : HEAD_DIM + 1, :]

    col = lambda base: pl.BlockSpec((rows, span), lambda j: (0, base + j))
    return call(
        body,
        grid=(pairs,),
        in_specs=[col(0), col(pairs), col(2 * pairs)],
        out_specs=[col(0), pl.BlockSpec((1, 8, rows), lambda j: (j, 0, 0))],
        out_shape=[
            jax.ShapeDtypeStruct((rows, width), jnp.bfloat16),
            jax.ShapeDtypeStruct((pairs, 8, rows), jnp.float32),
        ],
        name="attention",
    )(qkv, qkv, qkv)


def attention_back(qkv, logs, d_o, first_pair, pairs, cover=True):
    rows, width = qkv.shape[0], qkv.shape[1] // 3
    every = width // (2 * HEAD_DIM)
    span = 2 * HEAD_DIM

    def body(q_ref, k_ref, v_ref, l_ref, do_ref, d_ref, cq_ref, cv_ref):
        q, k, v, do = q_ref[...], k_ref[...], v_ref[...], do_ref[...]
        lane = lax.broadcasted_iota(jnp.int32, (rows, span), 1)
        dqs, dks, dvs = [], [], []
        for h in range(2):
            mine = (lane < HEAD_DIM) if h == 0 else (lane >= HEAD_DIM)
            kh = jnp.where(mine, k, jnp.zeros_like(k))
            vh = jnp.where(mine, v, jnp.zeros_like(v))
            pt = jnp.exp2(dot(kh, q, NT) * SCORE_SCALE - l_ref[0, h : h + 1, :])
            w = pt * dot(vh, do, NT)
            dst = (w - pt * jnp.sum(w, axis=0, keepdims=True)).astype(jnp.bfloat16)
            dvs.append(dot(pt.astype(jnp.bfloat16), do))
            dks.append(dot(dst, q))
            dqs.append(dot(dst, k, TN))
        first = lane < HEAD_DIM
        dq = (jnp.where(first, dqs[0], dqs[1]) * 0.125).astype(jnp.bfloat16)
        dk = (jnp.where(first, dks[0], dks[1]) * 0.125).astype(jnp.bfloat16)
        dv = jnp.where(first, dvs[0], dvs[1]).astype(jnp.bfloat16)
        d_ref[0] = dq
        d_ref[1] = dk
        d_ref[2] = dv
        cq_ref[...] = jnp.sum(dq.astype(jnp.float32), axis=0, keepdims=True)
        cv_ref[...] = jnp.sum(dv.astype(jnp.float32), axis=0, keepdims=True)

    col = lambda base: pl.BlockSpec((rows, span), lambda j: (0, base + j))
    sums = pl.BlockSpec((1, span), lambda j: (0, j))
    vec_shape = jax.ShapeDtypeStruct((1, pairs * span), jnp.float32)
    return call(
        body,
        grid=(pairs,),
        in_specs=[
            col(first_pair),
            col(every + first_pair),
            col(2 * every + first_pair),
            pl.BlockSpec((1, 8, rows), lambda j: (first_pair + j, 0, 0)),
            col(first_pair),
        ],
        out_specs=[pl.BlockSpec((3, rows, span), lambda j: (0, 0, j)), sums, sums],
        out_shape=[
            jax.ShapeDtypeStruct((3, rows, pairs * span), jnp.bfloat16),
            vec_shape,
            vec_shape,
        ],
        name="attention_back",
        cover=cover,
    )(qkv, qkv, qkv, logs, d_o)


def project_norm(o, weight, bias, x, gain, shift, at):
    rows, width = o.shape
    tm = rows // 2

    def body(o_ref, w_ref, b_ref, x_ref, g_ref, s_ref, x1_ref, a_ref):
        x1 = x_ref[...].astype(jnp.float32) + (dot(o_ref[...], w_ref[...]) + b_ref[...])
        x1_ref[...] = x1
        xhat, _ = row_stats(x1)
        a_ref[...] = (xhat * g_ref[...] + s_ref[...]).astype(jnp.bfloat16)

    rowblk = pl.BlockSpec((tm, width), lambda i: (i, 0))
    vec = whole((1, width))
    return call(
        body,
        grid=(rows // tm,),
        in_specs=[rowblk, pl.BlockSpec((width, width), lambda i: (0, at // width)), vec, rowblk, vec, vec],
        out_specs=[rowblk, rowblk],
        out_shape=[
            jax.ShapeDtypeStruct((rows, width), jnp.float32),
            jax.ShapeDtypeStruct((rows, width), jnp.bfloat16),
        ],
        name="project_norm",
    )(o, weight, bias, x, gain, shift)


def flat(ref):
    return ref[...].reshape(-1, ref.shape[-1])


def up_spec(packed, r_in):
    n, _, width = packed.shape
    return pl.BlockSpec((n, r_in, width), lambda j: (0, j, 0))


def down_spec(packed, r_ff):
    width = packed.shape[2]
    return pl.BlockSpec((width // r_ff, r_ff, width), lambda j: (j, 1, 0))


def feed_forward(a, packed, r_in, r_ff, up_bias, down_bias, x1):
    rows, width = a.shape
    hidden = up_bias.shape[1]
    tf = width
    steps = hidden // tf

    def body(a_ref, u_ref, ub_ref, d_ref, db_ref, x_ref, g_ref, gp_ref, y_ref, acc):
        j = pl.program_id(0)
        u = dot(a_ref[...], flat(u_ref)) + ub_ref[...]
        phi, bell = normal_cdf(u)
        g = (u * phi).astype(jnp.bfloat16)
        g_ref[...] = g
        gp_ref[...] = (phi + (u * RSQRT_2PI) * bell).astype(jnp.bfloat16)

        @pl.when(j == 0)
        def _():
            acc[...] = x_ref[...] + db_ref[...]

        acc[...] += dot(g, flat(d_ref))

        @pl.when(j == steps - 1)
        def _():
            y_ref[...] = acc[...].astype(jnp.bfloat16)

    return call(
        body,
        grid=(steps,),
        in_specs=[
            whole((rows, width)),
            up_spec(packed, r_in),
            pl.BlockSpec((1, tf), lambda j: (0, j)),
            down_spec(packed, r_ff),
            whole((1, width)),
            whole((rows, width)),
        ],
        out_specs=[
            pl.BlockSpec((rows, tf), lambda j: (0, j)),
            pl.BlockSpec((rows, tf), lambda j: (0, j)),
            whole((rows, width)),
        ],
        out_shape=[
            jax.ShapeDtypeStruct((rows, hidden), jnp.bfloat16),
            jax.ShapeDtypeStruct((rows, hidden), jnp.bfloat16),
            jax.ShapeDtypeStruct((rows, width), jnp.bfloat16),
        ],
        scratch_shapes=[pltpu.VMEM((rows, width), jnp.float32)],
        name="feed_forward",
    )(a, packed, up_bias, packed, down_bias, x1)


def feed_forward_in(a, packed, r_in, up_bias):
    rows, width = a.shape
    hidden = up_bias.shape[1]

    def body(a_ref, u_ref, ub_ref, g_ref, gp_ref):
        u = dot(a_ref[...], flat(u_ref)) + ub_ref[...]
        phi, bell = normal_cdf(u)
        g_ref[...] = (u * phi).astype(jnp.bfloat16)
        gp_ref[...] = (phi + (u * RSQRT_2PI) * bell).astype(jnp.bfloat16)

    block = pl.BlockSpec((rows, width), lambda j: (0, j))
    return call(
        body,
        grid=(hidden // width,),
        in_specs=[
            whole((rows, width)),
            up_spec(packed, r_in),
            pl.BlockSpec((1, width), lambda j: (0, j)),
        ],
        out_specs=[block, block],
        out_shape=[jax.ShapeDtypeStruct((rows, hidden), jnp.bfloat16)] * 2,
        name="feed_forward_in",
    )(a, packed, up_bias)


def feed_forward_out(g, packed, r_ff, down_bias, x1):
    rows, width = x1.shape
    steps = g.shape[1] // width

    def body(g_ref, d_ref, db_ref, x_ref, y_ref, acc):
        j = pl.program_id(0)

        @pl.when(j == 0)
        def _():
            acc[...] = x_ref[...] + db_ref[...]

        acc[...] += dot(g_ref[...], flat(d_ref))

        @pl.when(j == steps - 1)
        def _():
            y_ref[...] = acc[...].astype(jnp.bfloat16)

    return call(
        body,
        grid=(steps,),
        in_specs=[
            pl.BlockSpec((rows, width), lambda j: (0, j)),
            down_spec(packed, r_ff),
            whole((1, width)),
            whole((rows, width)),
        ],
        out_specs=whole((rows, width)),
        out_shape=jax.ShapeDtypeStruct((rows, width), jnp.bfloat16),
        scratch_shapes=[pltpu.VMEM((rows, width), jnp.float32)],
        name="feed_forward_out",
    )(g, packed, down_bias, x1)


def feed_forward_back(dy, gp, packed, r_in, r_ff, x1, gain, w_out, at):
    rows, width = dy.shape
    hidden = gp.shape[1]
    tf = width
    steps = hidden // tf

    def body(
        dy_ref, gp_ref, d_ref, u_ref, x_ref, g_ref, w_ref,
        dm_ref, du_ref, dx_ref, da_ref, do_ref, cdm_ref, cdu_ref, cda_ref, cg_ref, cs_ref, acc,
    ):
        j = pl.program_id(0)

        @pl.when(j == 0)
        def _():
            low = dy_ref[...].astype(jnp.bfloat16)
            dm_ref[...] = low
            cdm_ref[...] = jnp.sum(low.astype(jnp.float32), axis=0, keepdims=True)
            acc[...] = jnp.zeros_like(acc)

        du = (dot(dm_ref[...], flat(d_ref), NT) * gp_ref[...].astype(jnp.float32)).astype(jnp.bfloat16)
        du_ref[...] = du
        cdu_ref[...] = jnp.sum(du.astype(jnp.float32), axis=0, keepdims=True)
        acc[...] += dot(du, flat(u_ref), NT)

        @pl.when(j == steps - 1)
        def _():
            da2 = acc[...]
            xhat, inv = row_stats(x_ref[...])
            cg_ref[...] = jnp.sum(da2 * xhat, axis=0, keepdims=True)
            cs_ref[...] = jnp.sum(da2, axis=0, keepdims=True)
            t = da2 * g_ref[...]
            m1 = jnp.mean(t, axis=-1, keepdims=True)
            m2 = jnp.mean(t * xhat, axis=-1, keepdims=True)
            dx1 = dy_ref[...] + inv * (t - m1 - xhat * m2)
            dx_ref[...] = dx1
            low = dx1.astype(jnp.bfloat16)
            da_ref[...] = low
            cda_ref[...] = jnp.sum(low.astype(jnp.float32), axis=0, keepdims=True)
            do_ref[...] = dot(low, w_ref[...], NT).astype(jnp.bfloat16)

    full = whole((rows, width))
    vec = whole((1, width))
    f = lambda s, d: jax.ShapeDtypeStruct(s, d)
    return call(
        body,
        grid=(steps,),
        in_specs=[
            full,
            pl.BlockSpec((rows, tf), lambda j: (0, j)),
            down_spec(packed, r_ff),
            up_spec(packed, r_in),
            full,
            vec,
            pl.BlockSpec((width, width), lambda j: (0, at // width)),
        ],
        out_specs=[
            full,
            pl.BlockSpec((rows, tf), lambda j: (0, j)),
            full,
            full,
            full,
            vec,
            pl.BlockSpec((1, tf), lambda j: (0, j)),
            vec,
            vec,
            vec,
        ],
        out_shape=[
            f((rows, width), jnp.bfloat16),
            f((rows, hidden), jnp.bfloat16),
            f((rows, width), jnp.float32),
            f((rows, width), jnp.bfloat16),
            f((rows, width), jnp.bfloat16),
            f((1, width), jnp.float32),
            f((1, hidden), jnp.float32),
            f((1, width), jnp.float32),
            f((1, width), jnp.float32),
            f((1, width), jnp.float32),
        ],
        scratch_shapes=[pltpu.VMEM((rows, width), jnp.float32)],
        name="feed_forward_back",
        cover=True,
    )(dy, gp, packed, packed, x1, gain, w_out)


def project_back(grads, weight, x, gain, dx1, extra, dtypes):
    rows, width = x.shape
    tm = rows // 2
    have = extra is not None
    count = len(grads)
    part = width // count

    def body(*refs):
        d_refs = refs[:count]
        w_ref, x_ref, g_ref, dx_ref = refs[count : count + 4]
        more = refs[count + 4 : -2 - len(dtypes)]
        out_refs = refs[-2 - len(dtypes) : -2]
        cg_ref, cs_ref = refs[-2:]
        da = None
        for kind in range(3):
            for i in range(count):
                at = kind * width + i * part
                term = dot(d_refs[i][kind], w_ref[:, at : at + part], NT)
                da = term if da is None else da + term
        xhat, inv = row_stats(x_ref[...].astype(jnp.float32))
        cg = jnp.sum(da * xhat, axis=0, keepdims=True)
        cs = jnp.sum(da, axis=0, keepdims=True)

        @pl.when(pl.program_id(0) == 0)
        def _():
            cg_ref[...] = cg
            cs_ref[...] = cs

        @pl.when(pl.program_id(0) > 0)
        def _():
            cg_ref[...] += cg
            cs_ref[...] += cs

        t = da * g_ref[...]
        m1 = jnp.mean(t, axis=-1, keepdims=True)
        m2 = jnp.mean(t * xhat, axis=-1, keepdims=True)
        dx = dx_ref[...] + inv * (t - m1 - xhat * m2)
        if have:
            dx = more[0][...].astype(jnp.float32) * more[1][...] + dx
        for ref in out_refs:
            ref[...] = dx.astype(ref.dtype)

    rowblk = pl.BlockSpec((tm, width), lambda i: (i, 0))
    vec_spec = whole((1, width))
    specs = [pl.BlockSpec((3, tm, part), lambda i: (0, i, 0))] * count
    specs += [whole((width, 3 * width)), rowblk, vec_spec, rowblk]
    args = list(grads) + [weight, x, gain, dx1]
    if have:
        specs += [rowblk, pl.BlockSpec((tm, 1), lambda i: (i, 0))]
        args += list(extra)
    return call(
        body,
        grid=(rows // tm,),
        in_specs=specs,
        out_specs=[rowblk] * len(dtypes) + [vec_spec, vec_spec],
        out_shape=[
            *[jax.ShapeDtypeStruct((rows, width), d) for d in dtypes],
            jax.ShapeDtypeStruct((1, width), jnp.float32),
            jax.ShapeDtypeStruct((1, width), jnp.float32),
        ],
        name="project_back",
    )(*args)


def weight_grad(jobs, index, blocks, chunk, cover=False):
    ndp, nfs, r = blocks
    npos = ndp * nfs // 2
    rows = jobs[0][0][0].shape[0]
    widths = [rs[0].shape[-1] * (3 if rs[0].ndim == 3 else 1) for _, rs in jobs]
    starts = [sum(widths[:k]) for k in range(len(jobs))]
    counts = [len(ls) for ls, _ in jobs]
    steps = ndp * len(jobs)

    def body(i_ref, *refs):
        sent, kept, buf, sem = refs[-4:]
        i = pl.program_id(0)

        def copies(step, start):
            local = step % ndp
            for k in range(len(jobs)):
                for which, where in ((local < ndp // 2, sent), (local >= ndp // 2, kept)):

                    @pl.when((step // ndp == k) & which)
                    def _():
                        for f in range(nfs):
                            p = i_ref[ndp + local * nfs + f]
                            copy = pltpu.make_async_copy(
                                buf.at[step % 2, f, :, 0 : widths[k]],
                                where.at[p, :, starts[k] : starts[k] + widths[k]],
                                sem.at[step % 2, f],
                            )
                            copy.start() if start else copy.wait()

        @pl.when(i >= 2)
        def _():
            copies(i - 2, False)

        at_ref = 0
        for k in range(len(jobs)):
            a = refs[at_ref : at_ref + counts[k]]
            b = refs[at_ref + counts[k] : at_ref + 2 * counts[k]]
            at_ref += 2 * counts[k]

            @pl.when(i // ndp == k)
            def _():
                for at in range(0, widths[k], chunk):
                    part = b[0].shape[-1]
                    if len(b[0].shape) == 3:
                        take = lambda ref: ref[at // part, :, at % part : at % part + chunk]
                    else:
                        take = lambda ref: ref[:, at : at + chunk]
                    total = dot(a[0][...], take(b[0]), TN)
                    for x, y in zip(a[1:], b[1:]):
                        total += dot(x[...], take(y), TN)
                    total = total.astype(jnp.bfloat16).reshape(nfs, r, chunk)
                    buf[i % 2, :, :, at : at + chunk] = total

        copies(i, True)

        @pl.when(i == steps - 1)
        def _():
            copies(steps - 2, False)
            copies(steps - 1, False)

    def left_spec(k):
        step = lambda i: jnp.clip(i - k * ndp, 0, ndp - 1)
        return pl.BlockSpec((rows, nfs * r), lambda i, i_ref: (0, i_ref[step(i)]))

    anywhere = pl.BlockSpec(memory_space=pl.ANY)
    specs, args = [], []
    for k, (ls, rs) in enumerate(jobs):
        specs += [left_spec(k)] * len(ls) + [whole(rs[0].shape)] * len(rs)
        args += list(ls) + list(rs)
    return call(
        body,
        grid_spec=pltpu.PrefetchScalarGridSpec(
            num_scalar_prefetch=1,
            grid=(steps,),
            in_specs=specs,
            out_specs=[anywhere] * 2,
            scratch_shapes=[
                pltpu.VMEM((2, nfs, r, max(widths)), jnp.bfloat16),
                pltpu.SemaphoreType.DMA((2, nfs)),
            ],
        ),
        out_shape=[jax.ShapeDtypeStruct((npos, r, sum(widths)), jnp.bfloat16)] * 2,
        name="weight_grad",
        cover=cover,
    )(index, *args)


def weight_grad_half(lefts, rights, index, blocks):
    ndp, nfs, r = blocks
    steps = ndp // 2
    rows = lefts[0].shape[0]
    cols = rights[0].shape[1]
    count = len(lefts)

    def body(i_ref, *refs):
        a, b = refs[:count], refs[count : 2 * count]
        out, buf, sem = refs[2 * count :]
        i = pl.program_id(0)

        def copies(step, start):
            for f in range(nfs):
                where = out.at[i_ref[steps + step * nfs + f]]
                copy = pltpu.make_async_copy(buf.at[step, f], where, sem.at[step, f])
                copy.start() if start else copy.wait()

        total = dot(a[0][...], b[0][...], TN)
        for x, y in zip(a[1:], b[1:]):
            total += dot(x[...], y[...], TN)
        buf[i] = total.astype(jnp.bfloat16).reshape(nfs, r, cols)
        copies(i, True)

        @pl.when(i == steps - 1)
        def _():
            for step in range(steps):
                copies(step, False)

    return call(
        body,
        grid_spec=pltpu.PrefetchScalarGridSpec(
            num_scalar_prefetch=1,
            grid=(steps,),
            in_specs=[pl.BlockSpec((rows, nfs * r), lambda i, i_ref: (0, i_ref[i]))] * count
            + [whole((rows, cols))] * count,
            out_specs=pl.BlockSpec(memory_space=pl.ANY),
            scratch_shapes=[
                pltpu.VMEM((steps, nfs, r, cols), jnp.bfloat16),
                pltpu.SemaphoreType.DMA((steps, nfs)),
            ],
        ),
        out_shape=jax.ShapeDtypeStruct((steps * nfs, r, cols), jnp.bfloat16),
        name="weight_grad_half",
    )(index, *lefts, *rights)


def bits_of(ndp, nfs):
    core = nfs
    outer = [nfs << i for i in range(1, ndp.bit_length() - 1)]
    inner = [1 << i for i in range(nfs.bit_length() - 1)]
    return core, outer, inner


def stage_orders(ndp, nfs):
    core, outer, inner = bits_of(ndp, nfs)
    first, second = outer[0], inner[0]
    tail = outer[1:] + inner[1:]
    return core, ([first, second] + tail, [second, first] + tail)


def shard_table(ndp, nfs):
    n = ndp * nfs
    core, orders = stage_orders(ndp, nfs)
    table = np.zeros((n, n), np.int32)
    for me in range(n):
        for p in range(n):
            rel = core if p >= n // 2 else 0
            owner = 1 if (me ^ rel) & core else 0
            for i, mask in enumerate(orders[owner]):
                if p & (n >> (i + 2)):
                    rel ^= mask
            table[me, p] = me ^ rel
    return table


def stage_perms(ndp, nfs):
    n = ndp * nfs
    core, orders = stage_orders(ndp, nfs)
    perms = [[(i, i ^ core) for i in range(n)]]
    for a, b in zip(*orders):
        perms.append([(i, i ^ (b if i & core else a)) for i in range(n)])
    return perms


AXES = ("dp", "fsdp")


def send(x, perm):
    return lax.ppermute(x, AXES, perm)


class Line:
    def __init__(self):
        self.last = ()

    def after(self, *arrays):
        return lax.optimization_barrier(self.last + arrays)[len(self.last) :]

    def mark(self, *arrays):
        self.last = arrays


def place_shards(pieces, table_row, shape, rows_at, rows, into=None, cover=False):
    count = sum(a.shape[0] for a, _ in pieces)
    cols = shape[-1]

    def body(t_ref, *refs):
        ins, out, (buf, in_sem, out_sem) = refs[: len(pieces)], refs[-4], refs[-3:]
        loads, stores = [], []
        for ref, (array, first) in zip(ins, pieces):
            for k in range(array.shape[0]):
                i = len(loads)
                source = ref.at[k, :, 0:cols]
                loads.append(pltpu.make_async_copy(source, buf.at[i], in_sem.at[i]))
                target = out.at[t_ref[first + k], rows_at : rows_at + rows]
                stores.append(pltpu.make_async_copy(buf.at[i], target, out_sem.at[i]))
        for c in loads:
            c.start()
        for a, b in zip(loads, stores):
            a.wait()
            b.start()
        for b in stores:
            b.wait()

    anywhere = pl.BlockSpec(memory_space=pl.ANY)
    args = [a for a, _ in pieces] + ([] if into is None else [into])
    return call(
        body,
        out_shape=jax.ShapeDtypeStruct(shape, jnp.bfloat16),
        grid_spec=pltpu.PrefetchScalarGridSpec(
            num_scalar_prefetch=1,
            in_specs=[anywhere] * len(args),
            out_specs=anywhere,
            scratch_shapes=[pltpu.VMEM((count, rows, cols), jnp.bfloat16)]
            + [pltpu.SemaphoreType.DMA((count,))] * 2,
        ),
        input_output_aliases={} if into is None else {len(args): 0},
        name="place_shards",
        cover=cover,
    )(table_row, *args)


def pack_shard(matrices, vectors):
    rows = matrices[0].shape[0]
    widths = [m.shape[1] for m in matrices]
    lanes = 128 * -(-len(vectors) // 8)

    def body(*refs):
        out, scr = refs[-2:]
        at = 0
        for ref, width in zip(refs, widths):
            out[:, at : at + width] = ref[...]
            at += width
        scr[...] = jnp.zeros_like(scr)
        for r, ref in enumerate(refs[len(widths) : -2]):
            k, col = ref.shape[1], 128 * (r // 8)
            scr[r % 8 : r % 8 + 1, col : col + k] = ref[...].astype(jnp.float32)
        out[:, at:] = scr[...].astype(jnp.bfloat16)

    vectors = [v.reshape(1, -1) for v in vectors]
    cols = sum(widths) + lanes
    return call(
        body,
        grid=(1,),
        in_specs=[whole(a.shape) for a in (*matrices, *vectors)],
        out_specs=whole((rows, cols)),
        out_shape=jax.ShapeDtypeStruct((rows, cols), jnp.bfloat16),
        scratch_shapes=[pltpu.VMEM((rows, lanes), jnp.float32)],
        name="pack_shard",
    )(*matrices, *vectors)


def unpack_vectors(pieces, at, inverse_row, sizes, layout):
    per_piece = pieces[0].shape[0]
    n = per_piece * len(pieces)
    lanes = pieces[0].shape[2] - at

    def body(i_ref, *refs):
        ins, outs, scr = refs[: len(pieces)], refs[len(pieces) : -1], refs[-1]
        for i, ref in enumerate(ins):
            scr[i * per_piece : (i + 1) * per_piece] = ref[...].astype(jnp.float32)
        for rows, out in zip(layout, outs):
            col = 0
            for r in rows:
                k = sizes[0] if r is None else sizes[r]
                per = 128 // k if k < 128 else 1
                for d in range(0, n, per):
                    if r is None:
                        value = jnp.zeros((1, per * k), jnp.float32)
                    else:
                        row, lane = r % 8, 128 * (r // 8)
                        value = jnp.concatenate(
                            [
                                scr[i_ref[d + e], row : row + 1, lane : lane + k]
                                for e in range(per)
                            ],
                            axis=1,
                        )
                    out[0:1, col + d * k : col + (d + per) * k] = value
                col += n * k

    widths = [sum(n * (sizes[0] if r is None else sizes[r]) for r in rows) for rows in layout]
    return call(
        body,
        grid_spec=pltpu.PrefetchScalarGridSpec(
            num_scalar_prefetch=1,
            grid=(1,),
            in_specs=[pl.BlockSpec((per_piece, 8, lanes), lambda i, i_ref: (0, 0, at // lanes))]
            * len(pieces),
            out_specs=[pl.BlockSpec((1, w), lambda i, i_ref: (0, 0)) for w in widths],
            scratch_shapes=[pltpu.VMEM((n, 8, lanes), jnp.float32)],
        ),
        out_shape=[jax.ShapeDtypeStruct((1, w), jnp.float32) for w in widths],
        name="unpack_vectors",
    )(inverse_row, *pieces)


def pack_sums(parts, inverse_row, n, rows):
    flat_parts = [a for pieces in parts for group in pieces for a in group]

    def body(i_ref, *refs):
        out = refs[-1]
        out[...] = jnp.zeros_like(out)
        at = 0
        for r, pieces in enumerate(parts):
            per = n // len(pieces)
            for piece, group in enumerate(pieces):
                total = refs[at][...]
                for k in range(1, len(group)):
                    total += refs[at + k][...]
                at += len(group)
                k = total.shape[1] // per
                for d in range(per):
                    out[i_ref[piece * per + d], r : r + 1, 0:k] = total[:, d * k : (d + 1) * k]

    return call(
        body,
        grid_spec=pltpu.PrefetchScalarGridSpec(
            num_scalar_prefetch=1,
            grid=(1,),
            in_specs=[whole(a.shape) for a in flat_parts],
            out_specs=whole((n, rows, 128)),
        ),
        out_shape=jax.ShapeDtypeStruct((n, rows, 128), jnp.float32),
        name="pack_sums",
    )(inverse_row, *flat_parts)


class Reduction:
    def __init__(self, perms, kept, sent, stage):
        self.perms, self.stage = perms, stage
        self.kept, self.got = kept, send(sent, perms[stage])
        self.done = None

    def step(self, line, wide=jnp.bfloat16):
        kept, got = line.after(self.kept, self.got)
        add = lambda part: kept[part].astype(jnp.float32) + got[part].astype(jnp.float32)
        self.stage += 1
        if self.stage == len(self.perms):
            self.done = add(slice(None))[0]
            line.mark(self.done)
            return
        half = kept.shape[0] // 2
        sent = add(slice(half, None)).astype(wide)
        self.got = send(sent, self.perms[self.stage])
        self.kept = add(slice(0, half)).astype(wide)
        line.mark(sent, self.kept)


def per_device(ndp, nfs,
    tokens,
    ln1_gain,
    ln1_bias,
    w_qkv,
    bias_q,
    bias_v,
    w_out,
    bias_out,
    ln2_gain,
    ln2_bias,
    w_up,
    bias_up,
    w_down,
    bias_down,
    cot_first,
    cot_second,
    valid,
):
    n = ndp * nfs
    perms = stage_perms(ndp, nfs)
    gather_perms = perms[:0:-1]
    core_perm = perms[0]
    stages = len(gather_perms)
    table = shard_table(ndp, nfs)
    me = lax.axis_index("dp") * nfs + lax.axis_index("fsdp")
    both = np.concatenate([table, np.argsort(table, axis=1).astype(np.int32)], axis=1)
    both = lax.dynamic_slice(jnp.asarray(both), (me, 0), (1, 2 * n))[0]
    row, inverse_row = both[:n], both[n:]
    rows_in, width = tokens.shape[1:]
    r_in, r_ff = w_up.shape[0], w_down.shape[0]
    hidden = w_up.shape[1]

    vectors = (ln1_gain, ln1_bias, bias_q, bias_v, bias_out, ln2_gain, ln2_bias, bias_down, bias_up)
    sizes = [v.shape[0] for v in vectors]
    line = Line()
    qkv_cols = w_qkv.shape[1]
    cols = qkv_cols + w_out.shape[1]
    ahead = pack_shard([w_qkv, w_out], vectors)
    split = w_up.reshape(r_in, hidden // width, width).swapaxes(0, 1).reshape(r_ff, width)

    class Gather:
        def __init__(self, shard):
            self.held, self.stage = shard[None], 0
            (self.held,) = line.after(self.held)
            self.got = send(self.held, gather_perms[0])

        def step(self):
            mine, theirs = line.after(self.held, self.got)
            self.held = jnp.concatenate([mine, theirs], axis=0)
            line.mark(self.held)
            self.stage += 1
            self.got = send(self.held, gather_perms[self.stage])
            if self.stage == stages - 1:
                self.early = send(self.held, core_perm)

        def finish(self):
            (self.got,) = line.after(self.got)
            self.late = send(self.got, core_perm)

        def place(self, which, *where, into=None, cover=False):
            quarter = n // 4
            pair = (self.got, self.late) if which else (self.held, self.early)
            pair = line.after(*pair)
            pieces = [(pair[0], which * quarter), (pair[1], half + which * quarter)]
            out = place_shards(pieces, row, *where, into=into, cover=cover)
            line.mark(out)
            return out

    half = n // 2
    chain_a = Gather(ahead)
    for k in range(1, stages - 2):
        chain_a.step()
    chain_b = Gather(split)
    chain_a.step()
    for k in range(1, stages - 2):
        chain_b.step()
    chain_a.step()
    chain_b.step()
    chain_c = Gather(w_down)
    spot_a = ((n, r_in, cols), 0, r_in)
    first = chain_a.place(0, *spot_a, cover=True)
    for k in range(1, stages - 2):
        chain_c.step()
    chain_b.step()
    chain_a.finish()
    first = chain_a.place(1, *spot_a, into=first)
    w = {"first": first.reshape(n * r_in, cols)}
    g1, s1, bqkv, bo, g2, s2, bd, bu = unpack_vectors(
        (chain_a.held, chain_a.got, chain_a.early, chain_a.late),
        cols,
        inverse_row,
        sizes,
        [[0], [1], [2, None, 3], [4], [5], [6], [7], [8]],
    )
    spot_b = ((n, 2 * r_ff, width), 0, r_ff)
    spot_c = ((n, 2 * r_ff, width), r_ff, r_ff)

    def more(index):
        if index == 0:
            chain_c.step()
        if index == 1:
            chain_b.finish()
        if index == 2:
            chain_c.step()
            ff = chain_b.place(0, *spot_b)
            w["ff"] = chain_b.place(1, *spot_b, into=ff)
        if index == 3:
            ff = chain_c.place(0, *spot_c, into=w["ff"])
            chain_c.finish()
            w["ff"] = chain_c.place(1, *spot_c, into=ff)

    def forward(x, more=None):
        a1, qkv = norm_project(*line.after(x), g1, s1, w["first"], bqkv, qkv_cols // 2, qkv_cols)
        line.mark(a1)
        if more:
            more(0)
        o, logs = attention(*line.after(qkv))
        line.mark(o)
        if more:
            more(1)
        x1, a2 = project_norm(*line.after(o), w["first"], bo, x, g2, s2, qkv_cols)
        line.mark(a2)
        if more:
            more(2)
        a2 = line.after(a2)[0]
        if more is None:
            g, gp, y = feed_forward(a2, w["ff"], r_in, r_ff, bu, bd, x1)
        else:
            g, gp = feed_forward_in(a2, w["ff"], r_in, bu)
            line.mark(g)
            more(3)
            y = feed_forward_out(line.after(g)[0], w["ff"], r_ff, bd, x1)
        line.mark(y)
        return y, (x, a1, qkv, logs, o, x1, a2, g, gp)

    first, saved_first = forward(tokens[0], more)
    second, saved_second = forward(first)

    keep_mask = valid[0].astype(jnp.float32)[:, None]
    grad_second = cot_second[0].astype(jnp.float32) * keep_mask
    pairs = width // (2 * HEAD_DIM)
    parts = 2

    def ff_back(dy, saved):
        x, a1, qkv, logs, o, x1, a2, g, gp = saved
        outs = feed_forward_back(
            *line.after(dy), gp, w["ff"], r_in, r_ff, x1, g2, w["first"], qkv_cols
        )
        line.mark(outs[0])
        return outs

    def heads_back(saved, d_o, i, cover=True):
        outs = attention_back(
            saved[2], saved[3], *line.after(d_o), i * pairs // parts, pairs // parts, cover
        )
        line.mark(outs[0])
        return outs

    def qkv_back(heads, saved, dx1, extra, dtypes):
        outs = project_back(
            [line.after(h[0])[0] for h in heads], w["first"], saved[0], g1, dx1, extra, dtypes
        )
        line.mark(outs[0])
        return outs

    dm2, du2, dx2, da2, do2, cdm2, cdu2, cda2, cg22, cs22 = ff_back(grad_second, saved_second)
    heads2 = [heads_back(saved_second, do2, i) for i in range(parts)]
    grad_first, dm1, cg12, cs12 = qkv_back(
        heads2, saved_second, dx2, (cot_first[0], keep_mask), (jnp.float32, jnp.bfloat16)
    )

    core = (me // nfs) % 2
    evens = 2 * jnp.arange(ndp // 2, dtype=jnp.int32)
    lefts_at = jnp.concatenate([evens + (1 - core), evens + core])
    shards_at = lefts_at[:, None] * nfs + jnp.arange(nfs, dtype=jnp.int32)
    index = jnp.concatenate([lefts_at, inverse_row[shards_at.reshape(-1)] % half])
    index = index.astype(jnp.int32)

    def grads(r, *jobs, cover=False):
        jobs = [(line.after(*ls), rs) for ls, rs in jobs]
        sent, kept = weight_grad(jobs, index, (ndp, nfs, r), 512, cover)
        line.mark(sent)
        return Reduction(perms, kept, sent, 0)

    def grads_split(r, lefts, rights):
        lefts = line.after(*lefts)
        parts_at = index[:ndp].reshape(2, -1), index[ndp:].reshape(2, -1)
        made = []
        for k in range(2):
            at = jnp.concatenate([parts_at[0][k], parts_at[1][k]])
            made.append(weight_grad_half(line.after(*lefts), rights, at, (ndp, nfs, r)))
            line.mark(made[k])
        return Reduction(perms, made[1], made[0], 0)

    sg = list(zip(saved_first, saved_second))
    red_down = grads_split(r_ff, sg[7], (dm1, dm2))
    _, du1, dx1, da1, do1, cdm1, cdu1, cda1, cg21, cs21 = ff_back(grad_first, saved_first)
    red_down.step(line)
    red_up = grads(r_in, (sg[6], (du1, du2)))
    red_down.step(line)
    heads1 = [heads_back(saved_first, do1, 0)]
    rights = lambda i: (heads1[i][0], heads2[i][0])
    red_down.step(line)
    red_up.step(line)
    red_one = grads(r_in, (sg[4], (da1, da2)), (sg[1], rights(0)))
    heads1.append(heads_back(saved_first, do1, 1, False))
    red_up.step(line)
    red_down.step(line)
    red_two = grads(r_in, (sg[1], rights(1)), cover=True)
    red_one.step(line)
    red_up.step(line)
    red_two.step(line)
    grad_inputs, cg11, cs11 = qkv_back(heads1, saved_first, dx1, None, (jnp.bfloat16,))
    halves = lambda k: [[h[i][k] for h in (heads1, heads2)] for i in range(parts)]
    cg11 = line.after(cg11)[0]
    sums = pack_sums(
        [
            [[cg11, cg12]],
            [[cs11, cs12]],
            halves(1),
            halves(2),
            [[cda1, cda2]],
            [[cg21, cg22]],
            [[cs21, cs22]],
            [[cdm1, cdm2]],
            [[cdu1, cdu2]],
        ],
        inverse_row,
        n,
        len(vectors),
    )
    line.mark(sums)
    red_small = Reduction(perms, sums[:half], sums[half:], 0)
    red_one.step(line)
    red_up.step(line)
    todo = [red_two, red_one, red_up, red_down]
    while todo:
        for red in todo:
            red.step(line)
            if red_small.done is None and red not in (red_up, red_down):
                red_small.step(line, jnp.float32)
        todo = [red for red in todo if red.done is None]
    outs = [red_small.done[i, : sizes[i]] for i in range(len(vectors))]
    o_g1, o_s1, o_bq, o_bv, o_bo, o_g2, o_s2, o_bd, o_bu = outs
    one = red_one.done
    d_out = one[:, :width]
    third = width // parts
    blocks = []
    for kind in range(3):
        blocks.append(one[:, width + kind * third : width + (kind + 1) * third])
        blocks.append(red_two.done[:, kind * third : (kind + 1) * third])
    d_qkv = jnp.concatenate(blocks, axis=1)
    return (
        first[None],
        second[None],
        grad_inputs[None],
        o_g1,
        o_s1,
        d_qkv,
        o_bq,
        o_bv,
        d_out,
        o_bo,
        o_g2,
        o_s2,
        red_up.done,
        o_bu,
        red_down.done,
        o_bd,
    )


def solution(mesh):
    ndp, nfs = mesh.shape["dp"], mesh.shape["fsdp"]
    return jax.shard_map(
        partial(per_device, ndp, nfs),
        mesh=mesh,
        in_specs=(
            P(("dp", "fsdp"), None, None),
            P(("dp", "fsdp")),
            P(("dp", "fsdp")),
            P(("dp", "fsdp"), None),
            P(("dp", "fsdp")),
            P(("dp", "fsdp")),
            P(("dp", "fsdp"), None),
            P(("dp", "fsdp")),
            P(("dp", "fsdp")),
            P(("dp", "fsdp")),
            P(("dp", "fsdp"), None),
            P(("dp", "fsdp")),
            P(("dp", "fsdp"), None),
            P(("dp", "fsdp")),
            P(("dp", "fsdp"), None, None),
            P(("dp", "fsdp"), None, None),
            P(("dp", "fsdp"), None),
        ),
        out_specs=(
            P(("dp", "fsdp"), None, None),
            P(("dp", "fsdp"), None, None),
            P(("dp", "fsdp"), None, None),
            P(("dp", "fsdp")),
            P(("dp", "fsdp")),
            P(("dp", "fsdp"), None),
            P(("dp", "fsdp")),
            P(("dp", "fsdp")),
            P(("dp", "fsdp"), None),
            P(("dp", "fsdp")),
            P(("dp", "fsdp")),
            P(("dp", "fsdp")),
            P(("dp", "fsdp"), None),
            P(("dp", "fsdp")),
            P(("dp", "fsdp"), None),
            P(("dp", "fsdp")),
        ),
        check_vma=False,
    )
```

```python
from functools import partial

import numpy as np
import jax
import jax.numpy as jnp
from jax import lax
from jax.experimental import pallas as pl
from jax.experimental.pallas import tpu as pltpu
from jax.sharding import PartitionSpec as P

def call(body, cover=False, **options):
    cost = pl.CostEstimate(flops=10**11 if cover else 1, transcendentals=0, bytes_accessed=1)
    return pl.pallas_call(body, cost_estimate=cost, **options)


EPSILON = 1e-06
HEAD_DIM = 64
LOG2E = 1.4426950408889634
RSQRT_2PI = 0.3989422804014327
SQRT_HALF = 0.7071067811865476
SCORE_SCALE = HEAD_DIM**-0.5 * LOG2E
NT = (((1,), (1,)), ((), ()))
TN = (((0,), (0,)), ((), ()))


def dot(a, b, dims=(((1,), (0,)), ((), ()))):
    return lax.dot_general(a, b, dims, preferred_element_type=jnp.float32)


def whole(shape):
    return pl.BlockSpec(shape, lambda *_: (0,) * len(shape))


def normal_cdf(u):
    return 0.5 + 0.5 * lax.erf(u * SQRT_HALF), jnp.exp2((-0.5 * LOG2E) * (u * u))


def row_stats(v):
    centre = v - jnp.mean(v, axis=-1, keepdims=True)
    inv = lax.rsqrt(jnp.mean(centre * centre, axis=-1, keepdims=True) + EPSILON)
    return centre * inv, inv


def masked(values, mask):
    rows, width = values.shape

    def body(v_ref, m_ref, o_ref):
        o_ref[...] = v_ref[...].astype(jnp.float32) * m_ref[...]

    return call(
        body,
        grid=(1,),
        in_specs=[whole((rows, width)), whole((rows, 1))],
        out_specs=whole((rows, width)),
        out_shape=jax.ShapeDtypeStruct((rows, width), jnp.float32),
        name="masked",
        cover=True,
    )(values, mask)


def norm_project(x, gain, shift, weight, bias, tn, cols):
    rows, width = x.shape

    def body(x_ref, g_ref, s_ref, w_ref, b_ref, a_ref, o_ref):
        @pl.when(pl.program_id(0) == 0)
        def _():
            xhat, _ = row_stats(x_ref[...].astype(jnp.float32))
            a_ref[...] = (xhat * g_ref[...] + s_ref[...]).astype(jnp.bfloat16)

        o_ref[...] = (dot(a_ref[...], w_ref[...]) + b_ref[...]).astype(jnp.bfloat16)

    return call(
        body,
        grid=(cols // tn,),
        in_specs=[
            whole((rows, width)),
            whole((1, width)),
            whole((1, width)),
            pl.BlockSpec((width, tn), lambda j: (0, j)),
            pl.BlockSpec((1, tn), lambda j: (0, j)),
        ],
        out_specs=[whole((rows, width)), pl.BlockSpec((rows, tn), lambda j: (0, j))],
        out_shape=[
            jax.ShapeDtypeStruct((rows, width), jnp.bfloat16),
            jax.ShapeDtypeStruct((rows, cols), jnp.bfloat16),
        ],
        name="norm_project",
    )(x, gain, shift, weight, bias)


def attention(qkv, mover=None):
    rows, width = qkv.shape[0], qkv.shape[1] // 3
    pairs = width // (2 * HEAD_DIM)
    span = 2 * HEAD_DIM

    def body(q_ref, k_ref, v_ref, o_ref, l_ref):
        q, k, v = q_ref[...], k_ref[...], v_ref[...]
        lane = lax.broadcasted_iota(jnp.int32, (rows, span), 1)
        outs, logs = [], []
        for h in range(2):
            mine = (lane < HEAD_DIM) if h == 0 else (lane >= HEAD_DIM)
            kh = jnp.where(mine, k, jnp.zeros_like(k))
            s = dot(q, kh, NT)
            top = jnp.max(s, axis=-1, keepdims=True) * SCORE_SCALE
            e = jnp.exp2(s * SCORE_SCALE - top)
            total = jnp.sum(e, axis=-1, keepdims=True)
            outs.append(dot(e.astype(jnp.bfloat16), v) * (1.0 / total))
            logs.append(top + jnp.log2(total))
        first = lane < HEAD_DIM
        o_ref[...] = jnp.where(first, outs[0], outs[1]).astype(jnp.bfloat16)
        both = jnp.where(first, logs[0], logs[1])
        turned = both.T
        l_ref[0, 0:1, :] = turned[0:1, :]
        l_ref[0, 1:2, :] = turned[HEAD_DIM : HEAD_DIM + 1, :]

    col = lambda base: pl.BlockSpec((rows, span), lambda j, *_: (0, base + j))
    return riding(
        body,
        mover,
        (pairs,),
        [col(0), col(pairs), col(2 * pairs)],
        [col(0), pl.BlockSpec((1, 8, rows), lambda j, *_: (j, 0, 0))],
        [
            jax.ShapeDtypeStruct((rows, width), jnp.bfloat16),
            jax.ShapeDtypeStruct((pairs, 8, rows), jnp.float32),
        ],
        "attention",
        (qkv, qkv, qkv),
    )


def attention_back(qkv, logs, d_o, first_pair, pairs, cover=True):
    rows, width = qkv.shape[0], qkv.shape[1] // 3
    every = width // (2 * HEAD_DIM)
    span = 2 * HEAD_DIM

    def body(q_ref, k_ref, v_ref, l_ref, do_ref, d_ref, cq_ref, cv_ref):
        q, k, v, do = q_ref[...], k_ref[...], v_ref[...], do_ref[...]
        lane = lax.broadcasted_iota(jnp.int32, (rows, span), 1)
        dqs, dks, dvs = [], [], []
        for h in range(2):
            mine = (lane < HEAD_DIM) if h == 0 else (lane >= HEAD_DIM)
            kh = jnp.where(mine, k, jnp.zeros_like(k))
            vh = jnp.where(mine, v, jnp.zeros_like(v))
            pt = jnp.exp2(dot(kh, q, NT) * SCORE_SCALE - l_ref[0, h : h + 1, :])
            w = pt * dot(vh, do, NT)
            dst = (w - pt * jnp.sum(w, axis=0, keepdims=True)).astype(jnp.bfloat16)
            dvs.append(dot(pt.astype(jnp.bfloat16), do))
            dks.append(dot(dst, q))
            dqs.append(dot(dst, k, TN))
        first = lane < HEAD_DIM
        dq = (jnp.where(first, dqs[0], dqs[1]) * 0.125).astype(jnp.bfloat16)
        dk = (jnp.where(first, dks[0], dks[1]) * 0.125).astype(jnp.bfloat16)
        dv = jnp.where(first, dvs[0], dvs[1]).astype(jnp.bfloat16)
        d_ref[0] = dq
        d_ref[1] = dk
        d_ref[2] = dv
        cq_ref[...] = jnp.sum(dq.astype(jnp.float32), axis=0, keepdims=True)
        cv_ref[...] = jnp.sum(dv.astype(jnp.float32), axis=0, keepdims=True)

    col = lambda base: pl.BlockSpec((rows, span), lambda j: (0, base + j))
    sums = pl.BlockSpec((1, span), lambda j: (0, j))
    vec_shape = jax.ShapeDtypeStruct((1, pairs * span), jnp.float32)
    return call(
        body,
        grid=(pairs,),
        in_specs=[
            col(first_pair),
            col(every + first_pair),
            col(2 * every + first_pair),
            pl.BlockSpec((1, 8, rows), lambda j: (first_pair + j, 0, 0)),
            col(first_pair),
        ],
        out_specs=[pl.BlockSpec((3, rows, span), lambda j: (0, 0, j)), sums, sums],
        out_shape=[
            jax.ShapeDtypeStruct((3, rows, pairs * span), jnp.bfloat16),
            vec_shape,
            vec_shape,
        ],
        name="attention_back",
        cover=cover,
    )(qkv, qkv, qkv, logs, d_o)


def project_norm(o, packed, r_in, block, bias, x, gain, shift):
    rows, width = o.shape
    tm = rows // 2

    def body(o_ref, w_ref, b_ref, x_ref, g_ref, s_ref, x1_ref, a_ref):
        x1 = x_ref[...].astype(jnp.float32) + (dot(o_ref[...], flat(w_ref)) + b_ref[...])
        x1_ref[...] = x1
        xhat, _ = row_stats(x1)
        a_ref[...] = (xhat * g_ref[...] + s_ref[...]).astype(jnp.bfloat16)

    rowblk = pl.BlockSpec((tm, width), lambda i: (i, 0))
    vec = whole((1, width))
    return call(
        body,
        grid=(rows // tm,),
        in_specs=[rowblk, rows_spec(packed, r_in, block), vec, rowblk, vec, vec],
        out_specs=[rowblk, rowblk],
        out_shape=[
            jax.ShapeDtypeStruct((rows, width), jnp.float32),
            jax.ShapeDtypeStruct((rows, width), jnp.bfloat16),
        ],
        name="project_norm",
    )(o, packed, bias, x, gain, shift)


def flat(ref):
    return ref[...].reshape(-1, ref.shape[-1])


def rows_spec(packed, r_in, block):
    n, _, width = packed.shape
    return pl.BlockSpec((n, r_in, width), lambda *_: (0, block, 0))


def up_spec(packed, r_in):
    n, _, width = packed.shape
    return pl.BlockSpec((n, r_in, width), lambda j, *_: (0, j, 0))


def down_spec(packed):
    _, r_ff, width = packed.shape
    return pl.BlockSpec((width // r_ff, r_ff, width), lambda j: (j, 0, 0))


def feed_forward(a, up, down, r_in, up_bias, down_bias, x1):
    rows, width = a.shape
    hidden = up_bias.shape[1]
    tf = width
    steps = hidden // tf

    def body(a_ref, u_ref, ub_ref, d_ref, db_ref, x_ref, g_ref, gp_ref, y_ref, acc):
        j = pl.program_id(0)
        u = dot(a_ref[...], flat(u_ref)) + ub_ref[...]
        phi, bell = normal_cdf(u)
        g = (u * phi).astype(jnp.bfloat16)
        g_ref[...] = g
        gp_ref[...] = (phi + (u * RSQRT_2PI) * bell).astype(jnp.bfloat16)

        @pl.when(j == 0)
        def _():
            acc[...] = x_ref[...] + db_ref[...]

        acc[...] += dot(g, flat(d_ref))

        @pl.when(j == steps - 1)
        def _():
            y_ref[...] = acc[...].astype(jnp.bfloat16)

    return call(
        body,
        grid=(steps,),
        in_specs=[
            whole((rows, width)),
            up_spec(up, r_in),
            pl.BlockSpec((1, tf), lambda j: (0, j)),
            down_spec(down),
            whole((1, width)),
            whole((rows, width)),
        ],
        out_specs=[
            pl.BlockSpec((rows, tf), lambda j: (0, j)),
            pl.BlockSpec((rows, tf), lambda j: (0, j)),
            whole((rows, width)),
        ],
        out_shape=[
            jax.ShapeDtypeStruct((rows, hidden), jnp.bfloat16),
            jax.ShapeDtypeStruct((rows, hidden), jnp.bfloat16),
            jax.ShapeDtypeStruct((rows, width), jnp.bfloat16),
        ],
        scratch_shapes=[pltpu.VMEM((rows, width), jnp.float32)],
        name="feed_forward",
    )(a, up, up_bias, down, down_bias, x1)


def feed_forward_in(a, up, r_in, up_bias, mover=None):
    rows, width = a.shape
    hidden = up_bias.shape[1]

    def body(a_ref, u_ref, ub_ref, g_ref, gp_ref):
        u = dot(a_ref[...], flat(u_ref)) + ub_ref[...]
        phi, bell = normal_cdf(u)
        g_ref[...] = (u * phi).astype(jnp.bfloat16)
        gp_ref[...] = (phi + (u * RSQRT_2PI) * bell).astype(jnp.bfloat16)

    block = pl.BlockSpec((rows, width), lambda j, *_: (0, j))
    return riding(
        body,
        mover,
        (hidden // width,),
        [
            whole((rows, width)),
            up_spec(up, r_in),
            pl.BlockSpec((1, width), lambda j, *_: (0, j)),
        ],
        [block, block],
        [jax.ShapeDtypeStruct((rows, hidden), jnp.bfloat16)] * 2,
        "feed_forward_in",
        (a, up, up_bias),
    )


def feed_forward_out(g, down, down_bias, x1):
    rows, width = x1.shape
    steps = g.shape[1] // width

    def body(g_ref, d_ref, db_ref, x_ref, y_ref, acc):
        j = pl.program_id(0)

        @pl.when(j == 0)
        def _():
            acc[...] = x_ref[...] + db_ref[...]

        acc[...] += dot(g_ref[...], flat(d_ref))

        @pl.when(j == steps - 1)
        def _():
            y_ref[...] = acc[...].astype(jnp.bfloat16)

    return call(
        body,
        grid=(steps,),
        in_specs=[
            pl.BlockSpec((rows, width), lambda j: (0, j)),
            down_spec(down),
            whole((1, width)),
            whole((rows, width)),
        ],
        out_specs=whole((rows, width)),
        out_shape=jax.ShapeDtypeStruct((rows, width), jnp.bfloat16),
        scratch_shapes=[pltpu.VMEM((rows, width), jnp.float32)],
        name="feed_forward_out",
    )(g, down, down_bias, x1)


def feed_forward_back(dy, gp, up, down, r_in, x1, gain, block):
    rows, width = dy.shape
    hidden = gp.shape[1]
    tf = width
    steps = hidden // tf

    def body(
        dy_ref, gp_ref, d_ref, u_ref, x_ref, g_ref, w_ref,
        dm_ref, du_ref, dx_ref, da_ref, do_ref, cdm_ref, cdu_ref, cda_ref, cg_ref, cs_ref, acc,
    ):
        j = pl.program_id(0)

        @pl.when(j == 0)
        def _():
            low = dy_ref[...].astype(jnp.bfloat16)
            dm_ref[...] = low
            cdm_ref[...] = jnp.sum(low.astype(jnp.float32), axis=0, keepdims=True)
            acc[...] = jnp.zeros_like(acc)

        du = (dot(dm_ref[...], flat(d_ref), NT) * gp_ref[...].astype(jnp.float32)).astype(jnp.bfloat16)
        du_ref[...] = du
        cdu_ref[...] = jnp.sum(du.astype(jnp.float32), axis=0, keepdims=True)
        acc[...] += dot(du, flat(u_ref), NT)

        @pl.when(j == steps - 1)
        def _():
            da2 = acc[...]
            xhat, inv = row_stats(x_ref[...])
            cg_ref[...] = jnp.sum(da2 * xhat, axis=0, keepdims=True)
            cs_ref[...] = jnp.sum(da2, axis=0, keepdims=True)
            t = da2 * g_ref[...]
            m1 = jnp.mean(t, axis=-1, keepdims=True)
            m2 = jnp.mean(t * xhat, axis=-1, keepdims=True)
            dx1 = dy_ref[...] + inv * (t - m1 - xhat * m2)
            dx_ref[...] = dx1
            low = dx1.astype(jnp.bfloat16)
            da_ref[...] = low
            cda_ref[...] = jnp.sum(low.astype(jnp.float32), axis=0, keepdims=True)
            do_ref[...] = dot(low, flat(w_ref), NT).astype(jnp.bfloat16)

    full = whole((rows, width))
    vec = whole((1, width))
    f = lambda s, d: jax.ShapeDtypeStruct(s, d)
    return call(
        body,
        grid=(steps,),
        in_specs=[
            full,
            pl.BlockSpec((rows, tf), lambda j: (0, j)),
            down_spec(down),
            up_spec(up, r_in),
            full,
            vec,
            rows_spec(up, r_in, block),
        ],
        out_specs=[
            full,
            pl.BlockSpec((rows, tf), lambda j: (0, j)),
            full,
            full,
            full,
            vec,
            pl.BlockSpec((1, tf), lambda j: (0, j)),
            vec,
            vec,
            vec,
        ],
        out_shape=[
            f((rows, width), jnp.bfloat16),
            f((rows, hidden), jnp.bfloat16),
            f((rows, width), jnp.float32),
            f((rows, width), jnp.bfloat16),
            f((rows, width), jnp.bfloat16),
            f((1, width), jnp.float32),
            f((1, hidden), jnp.float32),
            f((1, width), jnp.float32),
            f((1, width), jnp.float32),
            f((1, width), jnp.float32),
        ],
        scratch_shapes=[pltpu.VMEM((rows, width), jnp.float32)],
        name="feed_forward_back",
        cover=True,
    )(dy, gp, down, up, x1, gain, up)


def project_back(grads, weight, x, gain, dx1, extra, dtypes):
    rows, width = x.shape
    tm = rows // 2
    have = extra is not None
    count = len(grads)
    part = width // count

    def body(*refs):
        d_refs = refs[:count]
        w_ref, x_ref, g_ref, dx_ref = refs[count : count + 4]
        more = refs[count + 4 : -2 - len(dtypes)]
        out_refs = refs[-2 - len(dtypes) : -2]
        cg_ref, cs_ref = refs[-2:]
        da = None
        for kind in range(3):
            for i in range(count):
                at = kind * width + i * part
                term = dot(d_refs[i][kind], w_ref[:, at : at + part], NT)
                da = term if da is None else da + term
        xhat, inv = row_stats(x_ref[...].astype(jnp.float32))
        cg = jnp.sum(da * xhat, axis=0, keepdims=True)
        cs = jnp.sum(da, axis=0, keepdims=True)

        @pl.when(pl.program_id(0) == 0)
        def _():
            cg_ref[...] = cg
            cs_ref[...] = cs

        @pl.when(pl.program_id(0) > 0)
        def _():
            cg_ref[...] += cg
            cs_ref[...] += cs

        t = da * g_ref[...]
        m1 = jnp.mean(t, axis=-1, keepdims=True)
        m2 = jnp.mean(t * xhat, axis=-1, keepdims=True)
        dx = dx_ref[...] + inv * (t - m1 - xhat * m2)
        if have:
            dx = more[0][...].astype(jnp.float32) * more[1][...] + dx
        for ref in out_refs:
            ref[...] = dx.astype(ref.dtype)

    rowblk = pl.BlockSpec((tm, width), lambda i: (i, 0))
    vec_spec = whole((1, width))
    specs = [pl.BlockSpec((3, tm, part), lambda i: (0, i, 0))] * count
    specs += [whole((width, 3 * width)), rowblk, vec_spec, rowblk]
    args = list(grads) + [weight, x, gain, dx1]
    if have:
        specs += [rowblk, pl.BlockSpec((tm, 1), lambda i: (i, 0))]
        args += list(extra)
    return call(
        body,
        grid=(rows // tm,),
        in_specs=specs,
        out_specs=[rowblk] * len(dtypes) + [vec_spec, vec_spec],
        out_shape=[
            *[jax.ShapeDtypeStruct((rows, width), d) for d in dtypes],
            jax.ShapeDtypeStruct((1, width), jnp.float32),
            jax.ShapeDtypeStruct((1, width), jnp.float32),
        ],
        name="project_back",
        cover=True,
    )(*args)


def weight_grad(jobs, index, blocks, chunk, cover=False):
    ndp, nfs, r = blocks
    npos = ndp * nfs // 2
    rows = jobs[0][0][0].shape[0]
    widths = [rs[0].shape[-1] * (3 if rs[0].ndim == 3 else 1) for _, rs in jobs]
    starts = [sum(widths[:k]) for k in range(len(jobs))]
    counts = [len(ls) for ls, _ in jobs]
    steps = ndp * len(jobs)

    def body(i_ref, *refs):
        sent, kept, buf, sem = refs[-4:]
        i = pl.program_id(0)

        def copies(step, start):
            local = step % ndp
            for k in range(len(jobs)):
                for which, where in ((local < ndp // 2, sent), (local >= ndp // 2, kept)):

                    @pl.when((step // ndp == k) & which)
                    def _():
                        for f in range(nfs):
                            p = i_ref[ndp + local * nfs + f]
                            copy = pltpu.make_async_copy(
                                buf.at[step % 2, f, :, 0 : widths[k]],
                                where.at[p, :, starts[k] : starts[k] + widths[k]],
                                sem.at[step % 2, f],
                            )
                            copy.start() if start else copy.wait()

        @pl.when(i >= 2)
        def _():
            copies(i - 2, False)

        at_ref = 0
        for k in range(len(jobs)):
            a = refs[at_ref : at_ref + counts[k]]
            b = refs[at_ref + counts[k] : at_ref + 2 * counts[k]]
            at_ref += 2 * counts[k]

            @pl.when(i // ndp == k)
            def _():
                for at in range(0, widths[k], chunk):
                    part = b[0].shape[-1]
                    if len(b[0].shape) == 3:
                        take = lambda ref: ref[at // part, :, at % part : at % part + chunk]
                    else:
                        take = lambda ref: ref[:, at : at + chunk]
                    total = dot(a[0][...], take(b[0]), TN)
                    for x, y in zip(a[1:], b[1:]):
                        total += dot(x[...], take(y), TN)
                    total = total.astype(jnp.bfloat16).reshape(nfs, r, chunk)
                    buf[i % 2, :, :, at : at + chunk] = total

        copies(i, True)

        @pl.when(i == steps - 1)
        def _():
            copies(steps - 2, False)
            copies(steps - 1, False)

    def left_spec(k):
        step = lambda i: jnp.clip(i - k * ndp, 0, ndp - 1)
        return pl.BlockSpec((rows, nfs * r), lambda i, i_ref: (0, i_ref[step(i)]))

    anywhere = pl.BlockSpec(memory_space=pl.ANY)
    specs, args = [], []
    for k, (ls, rs) in enumerate(jobs):
        specs += [left_spec(k)] * len(ls) + [whole(rs[0].shape)] * len(rs)
        args += list(ls) + list(rs)
    return call(
        body,
        grid_spec=pltpu.PrefetchScalarGridSpec(
            num_scalar_prefetch=1,
            grid=(steps,),
            in_specs=specs,
            out_specs=[anywhere] * 2,
            scratch_shapes=[
                pltpu.VMEM((2, nfs, r, max(widths)), jnp.bfloat16),
                pltpu.SemaphoreType.DMA((2, nfs)),
            ],
        ),
        out_shape=[jax.ShapeDtypeStruct((npos, r, sum(widths)), jnp.bfloat16)] * 2,
        name="weight_grad",
        cover=cover,
    )(index, *args)


def weight_grad_half(lefts, rights, index, blocks):
    ndp, nfs, r = blocks
    steps = ndp // 2
    rows = lefts[0].shape[0]
    cols = rights[0].shape[1]
    count = len(lefts)

    def body(i_ref, *refs):
        a, b = refs[:count], refs[count : 2 * count]
        out, buf, sem = refs[2 * count :]
        i = pl.program_id(0)

        def copies(step, start):
            for f in range(nfs):
                where = out.at[i_ref[steps + step * nfs + f]]
                copy = pltpu.make_async_copy(buf.at[step, f], where, sem.at[step, f])
                copy.start() if start else copy.wait()

        total = dot(a[0][...], b[0][...], TN)
        for x, y in zip(a[1:], b[1:]):
            total += dot(x[...], y[...], TN)
        buf[i] = total.astype(jnp.bfloat16).reshape(nfs, r, cols)
        copies(i, True)

        @pl.when(i == steps - 1)
        def _():
            for step in range(steps):
                copies(step, False)

    return call(
        body,
        grid_spec=pltpu.PrefetchScalarGridSpec(
            num_scalar_prefetch=1,
            grid=(steps,),
            in_specs=[pl.BlockSpec((rows, nfs * r), lambda i, i_ref: (0, i_ref[i]))] * count
            + [whole((rows, cols))] * count,
            out_specs=pl.BlockSpec(memory_space=pl.ANY),
            scratch_shapes=[
                pltpu.VMEM((steps, nfs, r, cols), jnp.bfloat16),
                pltpu.SemaphoreType.DMA((steps, nfs)),
            ],
        ),
        out_shape=jax.ShapeDtypeStruct((steps * nfs, r, cols), jnp.bfloat16),
        name="weight_grad_half",
    )(index, *lefts, *rights)


def bits_of(ndp, nfs):
    core = nfs
    outer = [nfs << i for i in range(1, ndp.bit_length() - 1)]
    inner = [1 << i for i in range(nfs.bit_length() - 1)]
    return core, outer, inner


def stage_orders(ndp, nfs):
    core, outer, inner = bits_of(ndp, nfs)
    first, second = outer[0], inner[0]
    tail = outer[1:] + inner[1:]
    return core, ([first, second] + tail, [second, first] + tail)


def shard_table(ndp, nfs):
    n = ndp * nfs
    core, orders = stage_orders(ndp, nfs)
    table = np.zeros((n, n), np.int32)
    for me in range(n):
        for p in range(n):
            rel = core if p >= n // 2 else 0
            owner = 1 if (me ^ rel) & core else 0
            for i, mask in enumerate(orders[owner]):
                if p & (n >> (i + 2)):
                    rel ^= mask
            table[me, p] = me ^ rel
    return table


def stage_perms(ndp, nfs):
    n = ndp * nfs
    core, orders = stage_orders(ndp, nfs)
    perms = [[(i, i ^ core) for i in range(n)]]
    for a, b in zip(*orders):
        perms.append([(i, i ^ (b if i & core else a)) for i in range(n)])
    return perms


AXES = ("dp", "fsdp")


def send(x, perm):
    return lax.ppermute(x, AXES, perm)


class Line:
    def __init__(self):
        self.last = ()

    def after(self, *arrays):
        return lax.optimization_barrier(self.last + arrays)[len(self.last) :]

    def mark(self, *arrays):
        self.last = arrays


class Mover:
    def __init__(self, pieces, table, shape, into=None):
        self.pieces, self.table, self.into = pieces, table, into
        self.args = [p[0] for p in pieces] + ([] if into is None else [into])
        self.specs = [pl.BlockSpec(memory_space=pl.ANY)] * len(self.args)
        self.out_spec = pl.BlockSpec(memory_space=pl.ANY)
        self.out_shape = jax.ShapeDtypeStruct(shape, jnp.bfloat16)
        counts = [p[0].shape[0] for p in pieces]
        self.scratch = [
            pltpu.VMEM((k, p[3], shape[-1]), jnp.bfloat16) for k, p in zip(counts, pieces)
        ] + [pltpu.SemaphoreType.DMA((sum(counts),))] * 2

    def copies(self, t_ref, ins, out, scratch):
        loads, stores = [], []
        in_sem, out_sem = scratch[-2:]
        for ref, buf, (array, first, rows_at, rows) in zip(ins, scratch, self.pieces):
            for k in range(array.shape[0]):
                i = len(loads)
                source = ref.at[k, :, 0 : buf.shape[-1]]
                loads.append(pltpu.make_async_copy(source, buf.at[k], in_sem.at[i]))
                target = out.at[t_ref[first + k], rows_at : rows_at + rows]
                stores.append(pltpu.make_async_copy(buf.at[k], target, out_sem.at[i]))
        return loads, stores

    def ride(self, step, last, *refs):
        loads, stores = self.copies(*refs)

        @pl.when(step == 0)
        def _():
            for c in loads:
                c.start()

        @pl.when(step == 1)
        def _():
            for a, b in zip(loads, stores):
                a.wait()
                b.start()

        @pl.when(step == last)
        def _():
            for c in stores:
                c.wait()


def place_shards(mover, cover=False):
    count = len(mover.args)

    def body(t_ref, *refs):
        loads, stores = mover.copies(t_ref, refs, refs[count], refs[count + 1 :])
        for c in loads:
            c.start()
        for a, b in zip(loads, stores):
            a.wait()
            b.start()
        for b in stores:
            b.wait()

    return call(
        body,
        out_shape=mover.out_shape,
        grid_spec=pltpu.PrefetchScalarGridSpec(
            num_scalar_prefetch=1,
            in_specs=mover.specs,
            out_specs=mover.out_spec,
            scratch_shapes=mover.scratch,
        ),
        input_output_aliases={} if mover.into is None else {count: 0},
        name="place_shards",
        cover=cover,
    )(mover.table, *mover.args)


def riding(body, mover, grid, in_specs, out_specs, out_shape, name, args):
    if mover is None:
        return call(
            body, grid=grid, in_specs=in_specs, out_specs=out_specs, out_shape=out_shape, name=name
        )(*args)
    ins, outs, extra = len(in_specs), len(out_specs), len(mover.args)

    def both(t_ref, *refs):
        own = refs[:ins] + refs[ins + extra : ins + extra + outs]
        moved = refs[ins : ins + extra], refs[ins + extra + outs], refs[ins + extra + outs + 1 :]
        mover.ride(pl.program_id(0), grid[0] - 1, t_ref, *moved)
        body(*own)

    return call(
        both,
        grid_spec=pltpu.PrefetchScalarGridSpec(
            num_scalar_prefetch=1,
            grid=grid,
            in_specs=in_specs + mover.specs,
            out_specs=out_specs + [mover.out_spec],
            scratch_shapes=mover.scratch,
        ),
        out_shape=out_shape + [mover.out_shape],
        input_output_aliases={} if mover.into is None else {ins + extra: outs},
        name=name,
    )(mover.table, *args, *mover.args)


def pack_shard(matrices, vectors):
    rows = matrices[0].shape[0]
    widths = [m.shape[1] for m in matrices]
    lanes = 128 * -(-len(vectors) // 8)

    def body(*refs):
        out, scr = refs[-2:]
        at = 0
        for ref, width in zip(refs, widths):
            out[:, at : at + width] = ref[...]
            at += width
        scr[...] = jnp.zeros_like(scr)
        for r, ref in enumerate(refs[len(widths) : -2]):
            k, col = ref.shape[1], 128 * (r // 8)
            scr[r % 8 : r % 8 + 1, col : col + k] = ref[...].astype(jnp.float32)
        out[:, at:] = scr[...].astype(jnp.bfloat16)

    vectors = [v.reshape(1, -1) for v in vectors]
    cols = sum(widths) + lanes
    return call(
        body,
        grid=(1,),
        in_specs=[whole(a.shape) for a in (*matrices, *vectors)],
        out_specs=whole((rows, cols)),
        out_shape=jax.ShapeDtypeStruct((rows, cols), jnp.bfloat16),
        scratch_shapes=[pltpu.VMEM((rows, lanes), jnp.float32)],
        name="pack_shard",
    )(*matrices, *vectors)


def unpack_vectors(pieces, at, inverse_row, sizes, layout):
    per_piece = pieces[0].shape[0]
    n = per_piece * len(pieces)
    lanes = pieces[0].shape[2] - at

    def body(i_ref, *refs):
        ins, outs, scr = refs[: len(pieces)], refs[len(pieces) : -1], refs[-1]
        for i, ref in enumerate(ins):
            scr[i * per_piece : (i + 1) * per_piece] = ref[...].astype(jnp.float32)
        for rows, out in zip(layout, outs):
            col = 0
            for r in rows:
                k = sizes[0] if r is None else sizes[r]
                per = 128 // k if k < 128 else 1
                for d in range(0, n, per):
                    if r is None:
                        value = jnp.zeros((1, per * k), jnp.float32)
                    else:
                        row, lane = r % 8, 128 * (r // 8)
                        value = jnp.concatenate(
                            [
                                scr[i_ref[d + e], row : row + 1, lane : lane + k]
                                for e in range(per)
                            ],
                            axis=1,
                        )
                    out[0:1, col + d * k : col + (d + per) * k] = value
                col += n * k

    widths = [sum(n * (sizes[0] if r is None else sizes[r]) for r in rows) for rows in layout]
    return call(
        body,
        grid_spec=pltpu.PrefetchScalarGridSpec(
            num_scalar_prefetch=1,
            grid=(1,),
            in_specs=[pl.BlockSpec((per_piece, 8, lanes), lambda i, i_ref: (0, 0, at // lanes))]
            * len(pieces),
            out_specs=[pl.BlockSpec((1, w), lambda i, i_ref: (0, 0)) for w in widths],
            scratch_shapes=[pltpu.VMEM((n, 8, lanes), jnp.float32)],
        ),
        out_shape=[jax.ShapeDtypeStruct((1, w), jnp.float32) for w in widths],
        name="unpack_vectors",
    )(inverse_row, *pieces)


def pack_sums(parts, inverse_row, n, rows):
    flat_parts = [a for pieces in parts for group in pieces for a in group]

    def body(i_ref, *refs):
        out = refs[-1]
        out[...] = jnp.zeros_like(out)
        at = 0
        for r, pieces in enumerate(parts):
            per = n // len(pieces)
            for piece, group in enumerate(pieces):
                total = refs[at][...]
                for k in range(1, len(group)):
                    total += refs[at + k][...]
                at += len(group)
                k = total.shape[1] // per
                for d in range(per):
                    out[i_ref[piece * per + d], r : r + 1, 0:k] = total[:, d * k : (d + 1) * k]

    return call(
        body,
        grid_spec=pltpu.PrefetchScalarGridSpec(
            num_scalar_prefetch=1,
            grid=(1,),
            in_specs=[whole(a.shape) for a in flat_parts],
            out_specs=whole((n, rows, 128)),
        ),
        out_shape=jax.ShapeDtypeStruct((n, rows, 128), jnp.float32),
        name="pack_sums",
    )(inverse_row, *flat_parts)


class Reduction:
    def __init__(self, perms, kept, sent, stage):
        self.perms, self.stage = perms, stage
        self.kept, self.got = kept, send(sent, perms[stage])
        self.done = None

    def step(self, line, wide=jnp.bfloat16):
        kept, got = line.after(self.kept, self.got)
        add = lambda part: kept[part].astype(jnp.float32) + got[part].astype(jnp.float32)
        self.stage += 1
        if self.stage == len(self.perms):
            self.done = add(slice(None))[0]
            line.mark(self.done)
            return
        half = kept.shape[0] // 2
        sent = add(slice(half, None)).astype(wide)
        self.got = send(sent, self.perms[self.stage])
        self.kept = add(slice(0, half)).astype(wide)
        line.mark(sent, self.kept)


def per_device(ndp, nfs,
    tokens,
    ln1_gain,
    ln1_bias,
    w_qkv,
    bias_q,
    bias_v,
    w_out,
    bias_out,
    ln2_gain,
    ln2_bias,
    w_up,
    bias_up,
    w_down,
    bias_down,
    cot_first,
    cot_second,
    valid,
):
    n = ndp * nfs
    perms = stage_perms(ndp, nfs)
    gather_perms = perms[:0:-1]
    core_perm = perms[0]
    stages = len(gather_perms)
    table = shard_table(ndp, nfs)
    me = lax.axis_index("dp") * nfs + lax.axis_index("fsdp")
    both = np.concatenate([table, np.argsort(table, axis=1).astype(np.int32)], axis=1)
    both = lax.dynamic_slice(jnp.asarray(both), (me, 0), (1, 2 * n))[0]
    row, inverse_row = both[:n], both[n:]
    rows_in, width = tokens.shape[1:]
    r_in, r_ff = w_up.shape[0], w_down.shape[0]
    hidden = w_up.shape[1]

    vectors = (ln1_gain, ln1_bias, bias_q, bias_v, bias_out, ln2_gain, ln2_bias, bias_down, bias_up)
    sizes = [v.shape[0] for v in vectors]
    line = Line()
    qkv_cols = w_qkv.shape[1]
    ahead = pack_shard([w_qkv], vectors)
    split = w_up.reshape(r_in, hidden // width, width).swapaxes(0, 1).reshape(r_ff, width)
    split = jnp.concatenate([split, w_out], axis=0)
    out_at = hidden // width

    class Gather:
        def __init__(self, shard):
            self.perms, self.rows = gather_perms, shard.shape[0]
            self.held, self.stage = shard[None], 0
            (self.held,) = line.after(self.held)
            self.got = send(self.held, self.perms[0])

        def step(self):
            mine, theirs = line.after(self.held, self.got)
            self.held = jnp.concatenate([mine, theirs], axis=0)
            line.mark(self.held)
            self.stage += 1
            self.got = send(self.held, self.perms[self.stage])
            if self.stage == stages - 1:
                self.early = send(self.held, core_perm)

        def finish(self):
            (self.got,) = line.after(self.got)
            self.late = send(self.got, core_perm)

        def pieces(self, which):
            quarter = n // 4
            pair = (self.got, self.late) if which else (self.held, self.early)
            pair = line.after(*pair)
            firsts = which * quarter, half + which * quarter
            return [(a, f, 0, self.rows) for a, f in zip(pair, firsts)]

    def place(pieces, shape, into=None, cover=False):
        out = place_shards(Mover(pieces, row, shape, into), cover)
        line.mark(out)
        return out

    half = n // 2
    ff_shape, first_shape = (n, r_ff, width), (n, r_in, qkv_cols)
    mid_shape = (n, r_ff + r_in, width)
    chain_a = Gather(ahead)
    for k in range(1, stages - 2):
        chain_a.step()
    chain_b = Gather(split)
    chain_a.step()
    keep_mask = valid[0].astype(jnp.float32)[:, None]
    grad_second = masked(*line.after(cot_second[0]), keep_mask)
    line.mark(grad_second)
    for k in range(1, stages - 2):
        chain_b.step()
    chain_a.step()
    chain_b.step()
    chain_c = Gather(w_down)
    chain_a.finish()
    first = place(chain_a.pieces(0), first_shape)
    first = place(chain_a.pieces(1), first_shape, first)
    for k in range(1, stages - 2):
        chain_c.step()
    chain_b.step()
    w = {"qkv": first.reshape(n * r_in, qkv_cols)}
    g1, s1, bqkv, bo, g2, s2, bd, bu = unpack_vectors(
        (chain_a.held, chain_a.got, chain_a.early, chain_a.late),
        qkv_cols,
        inverse_row,
        sizes,
        [[0], [1], [2, None, 3], [4], [5], [6], [7], [8]],
    )
    def attend(qkv):
        chain_c.step()
        o, logs = attention(*line.after(qkv))
        line.mark(o)
        up = place(chain_b.pieces(0), mid_shape)
        chain_b.finish()
        chain_c.step()
        w["up"] = place(chain_b.pieces(1), mid_shape, up)
        return o, logs

    def feed(a2, x1):
        g, gp = feed_forward_in(*line.after(a2), w["up"], r_in, bu)
        line.mark(g)
        down = place(chain_c.pieces(0), ff_shape)
        chain_c.finish()
        w["down"] = place(chain_c.pieces(1), ff_shape, down)
        y = feed_forward_out(line.after(g)[0], w["down"], bd, x1)
        return g, gp, y

    def forward(x, gathering=False):
        a1, qkv = norm_project(
            *line.after(x), g1, s1, w["qkv"], bqkv, qkv_cols // 2, qkv_cols
        )
        line.mark(a1)
        o, logs = attend(qkv) if gathering else attention(*line.after(qkv))
        if not gathering:
            line.mark(o)
        x1, a2 = project_norm(*line.after(o), w["up"], r_in, out_at, bo, x, g2, s2)
        line.mark(a2)
        if gathering:
            g, gp, y = feed(a2, x1)
        else:
            g, gp, y = feed_forward(*line.after(a2), w["up"], w["down"], r_in, bu, bd, x1)
        line.mark(y)
        return y, (x, a1, qkv, logs, o, x1, a2, g, gp)

    first, saved_first = forward(tokens[0], True)
    second, saved_second = forward(first)

    pairs = width // (2 * HEAD_DIM)
    parts = 2

    def ff_back(dy, saved):
        x, a1, qkv, logs, o, x1, a2, g, gp = saved
        outs = feed_forward_back(
            *line.after(dy), gp, w["up"], w["down"], r_in, x1, g2, out_at
        )
        line.mark(outs[0])
        return outs

    def heads_back(saved, d_o, i, cover=True):
        outs = attention_back(
            saved[2], saved[3], *line.after(d_o), i * pairs // parts, pairs // parts, cover
        )
        line.mark(outs[0])
        return outs

    def qkv_back(heads, saved, dx1, extra, dtypes):
        outs = project_back(
            [line.after(h[0])[0] for h in heads], w["qkv"], saved[0], g1, dx1, extra, dtypes
        )
        line.mark(outs[0])
        return outs

    dm2, du2, dx2, da2, do2, cdm2, cdu2, cda2, cg22, cs22 = ff_back(grad_second, saved_second)
    heads2 = [heads_back(saved_second, do2, i) for i in range(parts)]
    grad_first, dm1, cg12, cs12 = qkv_back(
        heads2, saved_second, dx2, (cot_first[0], keep_mask), (jnp.float32, jnp.bfloat16)
    )

    core = (me // nfs) % 2
    evens = 2 * jnp.arange(ndp // 2, dtype=jnp.int32)
    lefts_at = jnp.concatenate([evens + (1 - core), evens + core])
    shards_at = lefts_at[:, None] * nfs + jnp.arange(nfs, dtype=jnp.int32)
    index = jnp.concatenate([lefts_at, inverse_row[shards_at.reshape(-1)] % half])
    index = index.astype(jnp.int32)

    def grads(r, *jobs, cover=False):
        jobs = [(line.after(*ls), rs) for ls, rs in jobs]
        sent, kept = weight_grad(jobs, index, (ndp, nfs, r), 512, cover)
        line.mark(sent)
        return Reduction(perms, kept, sent, 0)

    def grads_split(r, lefts, rights):
        lefts = line.after(*lefts)
        parts_at = index[:ndp].reshape(2, -1), index[ndp:].reshape(2, -1)
        made = []
        for k in range(2):
            at = jnp.concatenate([parts_at[0][k], parts_at[1][k]])
            made.append(weight_grad_half(line.after(*lefts), rights, at, (ndp, nfs, r)))
            line.mark(made[k])
        return Reduction(perms, made[1], made[0], 0)

    sg = list(zip(saved_first, saved_second))
    red_down = grads_split(r_ff, sg[7], (dm1, dm2))
    _, du1, dx1, da1, do1, cdm1, cdu1, cda1, cg21, cs21 = ff_back(grad_first, saved_first)
    red_down.step(line)
    red_up = grads(r_in, (sg[6], (du1, du2)))
    red_down.step(line)
    heads1 = [heads_back(saved_first, do1, 0)]
    rights = lambda i: (heads1[i][0], heads2[i][0])
    red_down.step(line)
    red_up.step(line)
    red_one = grads(r_in, (sg[4], (da1, da2)), (sg[1], rights(0)))
    heads1.append(heads_back(saved_first, do1, 1, False))
    red_up.step(line)
    red_down.step(line)
    red_two = grads(r_in, (sg[1], rights(1)), cover=True)
    red_one.step(line)
    red_up.step(line)
    red_two.step(line)
    grad_inputs, cg11, cs11 = qkv_back(heads1, saved_first, dx1, None, (jnp.bfloat16,))
    halves = lambda k: [[h[i][k] for h in (heads1, heads2)] for i in range(parts)]
    cg11 = line.after(cg11)[0]
    sums = pack_sums(
        [
            [[cg11, cg12]],
            [[cs11, cs12]],
            halves(1),
            halves(2),
            [[cda1, cda2]],
            [[cg21, cg22]],
            [[cs21, cs22]],
            [[cdm1, cdm2]],
            [[cdu1, cdu2]],
        ],
        inverse_row,
        n,
        len(vectors),
    )
    line.mark(sums)
    red_small = Reduction(perms, sums[:half], sums[half:], 0)
    red_one.step(line)
    red_up.step(line)
    todo = [red_two, red_one, red_up, red_down]
    while todo:
        for red in todo:
            red.step(line)
            if red_small.done is None and red not in (red_up, red_down):
                red_small.step(line, jnp.float32)
        todo = [red for red in todo if red.done is None]
    outs = [red_small.done[i, : sizes[i]] for i in range(len(vectors))]
    o_g1, o_s1, o_bq, o_bv, o_bo, o_g2, o_s2, o_bd, o_bu = outs
    one = red_one.done
    d_out = one[:, :width]
    third = width // parts
    blocks = []
    for kind in range(3):
        blocks.append(one[:, width + kind * third : width + (kind + 1) * third])
        blocks.append(red_two.done[:, kind * third : (kind + 1) * third])
    d_qkv = jnp.concatenate(blocks, axis=1)
    return (
        first[None],
        second[None],
        grad_inputs[None],
        o_g1,
        o_s1,
        d_qkv,
        o_bq,
        o_bv,
        d_out,
        o_bo,
        o_g2,
        o_s2,
        red_up.done,
        o_bu,
        red_down.done,
        o_bd,
    )


def solution(mesh):
    ndp, nfs = mesh.shape["dp"], mesh.shape["fsdp"]
    return jax.shard_map(
        partial(per_device, ndp, nfs),
        mesh=mesh,
        in_specs=(
            P(("dp", "fsdp"), None, None),
            P(("dp", "fsdp")),
            P(("dp", "fsdp")),
            P(("dp", "fsdp"), None),
            P(("dp", "fsdp")),
            P(("dp", "fsdp")),
            P(("dp", "fsdp"), None),
            P(("dp", "fsdp")),
            P(("dp", "fsdp")),
            P(("dp", "fsdp")),
            P(("dp", "fsdp"), None),
            P(("dp", "fsdp")),
            P(("dp", "fsdp"), None),
            P(("dp", "fsdp")),
            P(("dp", "fsdp"), None, None),
            P(("dp", "fsdp"), None, None),
            P(("dp", "fsdp"), None),
        ),
        out_specs=(
            P(("dp", "fsdp"), None, None),
            P(("dp", "fsdp"), None, None),
            P(("dp", "fsdp"), None, None),
            P(("dp", "fsdp")),
            P(("dp", "fsdp")),
            P(("dp", "fsdp"), None),
            P(("dp", "fsdp")),
            P(("dp", "fsdp")),
            P(("dp", "fsdp"), None),
            P(("dp", "fsdp")),
            P(("dp", "fsdp")),
            P(("dp", "fsdp")),
            P(("dp", "fsdp"), None),
            P(("dp", "fsdp")),
            P(("dp", "fsdp"), None),
            P(("dp", "fsdp")),
        ),
        check_vma=False,
    )
```

```python
from functools import partial

import numpy as np
import jax
import jax.numpy as jnp
from jax import lax
from jax.experimental import pallas as pl
from jax.experimental.pallas import tpu as pltpu
from jax.sharding import PartitionSpec as P

def call(body, cover=False, **options):
    cost = pl.CostEstimate(flops=10**11 if cover else 1, transcendentals=0, bytes_accessed=1)
    return pl.pallas_call(body, cost_estimate=cost, **options)


EPSILON = 1e-06
HEAD_DIM = 64
LOG2E = 1.4426950408889634
RSQRT_2PI = 0.3989422804014327
SQRT_HALF = 0.7071067811865476
SCORE_SCALE = HEAD_DIM**-0.5 * LOG2E
NT = (((1,), (1,)), ((), ()))
TN = (((0,), (0,)), ((), ()))


def dot(a, b, dims=(((1,), (0,)), ((), ()))):
    return lax.dot_general(a, b, dims, preferred_element_type=jnp.float32)


def whole(shape):
    return pl.BlockSpec(shape, lambda *_: (0,) * len(shape))


def normal_cdf(u):
    return 0.5 + 0.5 * lax.erf(u * SQRT_HALF), jnp.exp2((-0.5 * LOG2E) * (u * u))


def row_stats(v):
    centre = v - jnp.mean(v, axis=-1, keepdims=True)
    inv = lax.rsqrt(jnp.mean(centre * centre, axis=-1, keepdims=True) + EPSILON)
    return centre * inv, inv


def masked(values, mask):
    rows, width = values.shape

    def body(v_ref, m_ref, o_ref):
        o_ref[...] = v_ref[...].astype(jnp.float32) * m_ref[...]

    return call(
        body,
        grid=(1,),
        in_specs=[whole((rows, width)), whole((rows, 1))],
        out_specs=whole((rows, width)),
        out_shape=jax.ShapeDtypeStruct((rows, width), jnp.float32),
        name="masked",
        cover=True,
    )(values, mask)


def norm_project(x, gain, shift, weight, bias, tn, cols):
    rows, width = x.shape

    def body(x_ref, g_ref, s_ref, w_ref, b_ref, a_ref, o_ref):
        @pl.when(pl.program_id(0) == 0)
        def _():
            xhat, _ = row_stats(x_ref[...].astype(jnp.float32))
            a_ref[...] = (xhat * g_ref[...] + s_ref[...]).astype(jnp.bfloat16)

        o_ref[...] = (dot(a_ref[...], w_ref[...]) + b_ref[...]).astype(jnp.bfloat16)

    return call(
        body,
        grid=(cols // tn,),
        in_specs=[
            whole((rows, width)),
            whole((1, width)),
            whole((1, width)),
            pl.BlockSpec((width, tn), lambda j: (0, j)),
            pl.BlockSpec((1, tn), lambda j: (0, j)),
        ],
        out_specs=[whole((rows, width)), pl.BlockSpec((rows, tn), lambda j: (0, j))],
        out_shape=[
            jax.ShapeDtypeStruct((rows, width), jnp.bfloat16),
            jax.ShapeDtypeStruct((rows, cols), jnp.bfloat16),
        ],
        name="norm_project",
    )(x, gain, shift, weight, bias)


def attention(qkv, mover=None):
    rows, width = qkv.shape[0], qkv.shape[1] // 3
    pairs = width // (2 * HEAD_DIM)
    span = 2 * HEAD_DIM

    def body(q_ref, k_ref, v_ref, o_ref, l_ref):
        q, k, v = q_ref[...], k_ref[...], v_ref[...]
        lane = lax.broadcasted_iota(jnp.int32, (rows, span), 1)
        outs, logs = [], []
        for h in range(2):
            mine = (lane < HEAD_DIM) if h == 0 else (lane >= HEAD_DIM)
            kh = jnp.where(mine, k, jnp.zeros_like(k))
            s = dot(q, kh, NT)
            top = jnp.max(s, axis=-1, keepdims=True) * SCORE_SCALE
            e = jnp.exp2(s * SCORE_SCALE - top)
            total = jnp.sum(e, axis=-1, keepdims=True)
            outs.append(dot(e.astype(jnp.bfloat16), v) * (1.0 / total))
            logs.append(top + jnp.log2(total))
        first = lane < HEAD_DIM
        o_ref[...] = jnp.where(first, outs[0], outs[1]).astype(jnp.bfloat16)
        both = jnp.where(first, logs[0], logs[1])
        turned = both.T
        l_ref[0, 0:1, :] = turned[0:1, :]
        l_ref[0, 1:2, :] = turned[HEAD_DIM : HEAD_DIM + 1, :]

    col = lambda base: pl.BlockSpec((rows, span), lambda j, *_: (0, base + j))
    return riding(
        body,
        mover,
        (pairs,),
        [col(0), col(pairs), col(2 * pairs)],
        [col(0), pl.BlockSpec((1, 8, rows), lambda j, *_: (j, 0, 0))],
        [
            jax.ShapeDtypeStruct((rows, width), jnp.bfloat16),
            jax.ShapeDtypeStruct((pairs, 8, rows), jnp.float32),
        ],
        "attention",
        (qkv, qkv, qkv),
    )


def attention_back(qkv, logs, d_o, first_pair, pairs, cover=True):
    rows, width = qkv.shape[0], qkv.shape[1] // 3
    every = width // (2 * HEAD_DIM)
    span = 2 * HEAD_DIM

    def body(q_ref, k_ref, v_ref, l_ref, do_ref, d_ref, cq_ref, cv_ref):
        q, k, v, do = q_ref[...], k_ref[...], v_ref[...], do_ref[...]
        lane = lax.broadcasted_iota(jnp.int32, (rows, span), 1)
        dqs, dks, dvs = [], [], []
        for h in range(2):
            mine = (lane < HEAD_DIM) if h == 0 else (lane >= HEAD_DIM)
            kh = jnp.where(mine, k, jnp.zeros_like(k))
            vh = jnp.where(mine, v, jnp.zeros_like(v))
            pt = jnp.exp2(dot(kh, q, NT) * SCORE_SCALE - l_ref[0, h : h + 1, :])
            w = pt * dot(vh, do, NT)
            dst = (w - pt * jnp.sum(w, axis=0, keepdims=True)).astype(jnp.bfloat16)
            dvs.append(dot(pt.astype(jnp.bfloat16), do))
            dks.append(dot(dst, q))
            dqs.append(dot(dst, k, TN))
        first = lane < HEAD_DIM
        dq = (jnp.where(first, dqs[0], dqs[1]) * 0.125).astype(jnp.bfloat16)
        dk = (jnp.where(first, dks[0], dks[1]) * 0.125).astype(jnp.bfloat16)
        dv = jnp.where(first, dvs[0], dvs[1]).astype(jnp.bfloat16)
        d_ref[0] = dq
        d_ref[1] = dk
        d_ref[2] = dv
        cq_ref[...] = jnp.sum(dq.astype(jnp.float32), axis=0, keepdims=True)
        cv_ref[...] = jnp.sum(dv.astype(jnp.float32), axis=0, keepdims=True)

    col = lambda base: pl.BlockSpec((rows, span), lambda j: (0, base + j))
    sums = pl.BlockSpec((1, span), lambda j: (0, j))
    vec_shape = jax.ShapeDtypeStruct((1, pairs * span), jnp.float32)
    return call(
        body,
        grid=(pairs,),
        in_specs=[
            col(first_pair),
            col(every + first_pair),
            col(2 * every + first_pair),
            pl.BlockSpec((1, 8, rows), lambda j: (first_pair + j, 0, 0)),
            col(first_pair),
        ],
        out_specs=[pl.BlockSpec((3, rows, span), lambda j: (0, 0, j)), sums, sums],
        out_shape=[
            jax.ShapeDtypeStruct((3, rows, pairs * span), jnp.bfloat16),
            vec_shape,
            vec_shape,
        ],
        name="attention_back",
        cover=cover,
    )(qkv, qkv, qkv, logs, d_o)


def project_norm(o, packed, r_in, block, bias, x, gain, shift):
    rows, width = o.shape
    tm = rows // 2

    def body(o_ref, w_ref, b_ref, x_ref, g_ref, s_ref, x1_ref, a_ref):
        x1 = x_ref[...].astype(jnp.float32) + (dot(o_ref[...], flat(w_ref)) + b_ref[...])
        x1_ref[...] = x1
        xhat, _ = row_stats(x1)
        a_ref[...] = (xhat * g_ref[...] + s_ref[...]).astype(jnp.bfloat16)

    rowblk = pl.BlockSpec((tm, width), lambda i: (i, 0))
    vec = whole((1, width))
    return call(
        body,
        grid=(rows // tm,),
        in_specs=[rowblk, rows_spec(packed, r_in, block), vec, rowblk, vec, vec],
        out_specs=[rowblk, rowblk],
        out_shape=[
            jax.ShapeDtypeStruct((rows, width), jnp.float32),
            jax.ShapeDtypeStruct((rows, width), jnp.bfloat16),
        ],
        name="project_norm",
    )(o, packed, bias, x, gain, shift)


def flat(ref):
    return ref[...].reshape(-1, ref.shape[-1])


def rows_spec(packed, r_in, block):
    n, _, width = packed.shape
    return pl.BlockSpec((n, r_in, width), lambda *_: (0, block, 0))


def up_spec(packed, r_in):
    n, _, width = packed.shape
    return pl.BlockSpec((n, r_in, width), lambda j, *_: (0, j, 0))


def down_spec(packed):
    _, r_ff, width = packed.shape
    return pl.BlockSpec((width // r_ff, r_ff, width), lambda j: (j, 0, 0))


def feed_forward(a, up, down, r_in, up_bias, down_bias, x1):
    rows, width = a.shape
    hidden = up_bias.shape[1]
    tf = width
    steps = hidden // tf

    def body(a_ref, u_ref, ub_ref, d_ref, db_ref, x_ref, g_ref, gp_ref, y_ref, acc):
        j = pl.program_id(0)
        u = dot(a_ref[...], flat(u_ref)) + ub_ref[...]
        phi, bell = normal_cdf(u)
        g = (u * phi).astype(jnp.bfloat16)
        g_ref[...] = g
        gp_ref[...] = (phi + (u * RSQRT_2PI) * bell).astype(jnp.bfloat16)

        @pl.when(j == 0)
        def _():
            acc[...] = x_ref[...] + db_ref[...]

        acc[...] += dot(g, flat(d_ref))

        @pl.when(j == steps - 1)
        def _():
            y_ref[...] = acc[...].astype(jnp.bfloat16)

    return call(
        body,
        grid=(steps,),
        in_specs=[
            whole((rows, width)),
            up_spec(up, r_in),
            pl.BlockSpec((1, tf), lambda j: (0, j)),
            down_spec(down),
            whole((1, width)),
            whole((rows, width)),
        ],
        out_specs=[
            pl.BlockSpec((rows, tf), lambda j: (0, j)),
            pl.BlockSpec((rows, tf), lambda j: (0, j)),
            whole((rows, width)),
        ],
        out_shape=[
            jax.ShapeDtypeStruct((rows, hidden), jnp.bfloat16),
            jax.ShapeDtypeStruct((rows, hidden), jnp.bfloat16),
            jax.ShapeDtypeStruct((rows, width), jnp.bfloat16),
        ],
        scratch_shapes=[pltpu.VMEM((rows, width), jnp.float32)],
        name="feed_forward",
    )(a, up, up_bias, down, down_bias, x1)


def feed_forward_in(a, up, r_in, up_bias, mover=None):
    rows, width = a.shape
    hidden = up_bias.shape[1]

    def body(a_ref, u_ref, ub_ref, g_ref, gp_ref):
        u = dot(a_ref[...], flat(u_ref)) + ub_ref[...]
        phi, bell = normal_cdf(u)
        g_ref[...] = (u * phi).astype(jnp.bfloat16)
        gp_ref[...] = (phi + (u * RSQRT_2PI) * bell).astype(jnp.bfloat16)

    block = pl.BlockSpec((rows, width), lambda j, *_: (0, j))
    return riding(
        body,
        mover,
        (hidden // width,),
        [
            whole((rows, width)),
            up_spec(up, r_in),
            pl.BlockSpec((1, width), lambda j, *_: (0, j)),
        ],
        [block, block],
        [jax.ShapeDtypeStruct((rows, hidden), jnp.bfloat16)] * 2,
        "feed_forward_in",
        (a, up, up_bias),
    )


def feed_forward_out(g, down, down_bias, x1):
    rows, width = x1.shape
    steps = g.shape[1] // width

    def body(g_ref, d_ref, db_ref, x_ref, y_ref, acc):
        j = pl.program_id(0)

        @pl.when(j == 0)
        def _():
            acc[...] = x_ref[...] + db_ref[...]

        acc[...] += dot(g_ref[...], flat(d_ref))

        @pl.when(j == steps - 1)
        def _():
            y_ref[...] = acc[...].astype(jnp.bfloat16)

    return call(
        body,
        grid=(steps,),
        in_specs=[
            pl.BlockSpec((rows, width), lambda j: (0, j)),
            down_spec(down),
            whole((1, width)),
            whole((rows, width)),
        ],
        out_specs=whole((rows, width)),
        out_shape=jax.ShapeDtypeStruct((rows, width), jnp.bfloat16),
        scratch_shapes=[pltpu.VMEM((rows, width), jnp.float32)],
        name="feed_forward_out",
    )(g, down, down_bias, x1)


def feed_forward_back(dy, gp, up, down, r_in, x1, gain, block):
    rows, width = dy.shape
    hidden = gp.shape[1]
    tf = width
    steps = hidden // tf

    def body(
        dy_ref, gp_ref, d_ref, u_ref, x_ref, g_ref, w_ref,
        dm_ref, du_ref, dx_ref, da_ref, do_ref, cdm_ref, cdu_ref, cda_ref, cg_ref, cs_ref, acc,
    ):
        j = pl.program_id(0)

        @pl.when(j == 0)
        def _():
            low = dy_ref[...].astype(jnp.bfloat16)
            dm_ref[...] = low
            cdm_ref[...] = jnp.sum(low.astype(jnp.float32), axis=0, keepdims=True)
            acc[...] = jnp.zeros_like(acc)

        du = (dot(dm_ref[...], flat(d_ref), NT) * gp_ref[...].astype(jnp.float32)).astype(jnp.bfloat16)
        du_ref[...] = du
        cdu_ref[...] = jnp.sum(du.astype(jnp.float32), axis=0, keepdims=True)
        acc[...] += dot(du, flat(u_ref), NT)

        @pl.when(j == steps - 1)
        def _():
            da2 = acc[...]
            xhat, inv = row_stats(x_ref[...])
            cg_ref[...] = jnp.sum(da2 * xhat, axis=0, keepdims=True)
            cs_ref[...] = jnp.sum(da2, axis=0, keepdims=True)
            t = da2 * g_ref[...]
            m1 = jnp.mean(t, axis=-1, keepdims=True)
            m2 = jnp.mean(t * xhat, axis=-1, keepdims=True)
            dx1 = dy_ref[...] + inv * (t - m1 - xhat * m2)
            dx_ref[...] = dx1
            low = dx1.astype(jnp.bfloat16)
            da_ref[...] = low
            cda_ref[...] = jnp.sum(low.astype(jnp.float32), axis=0, keepdims=True)
            do_ref[...] = dot(low, flat(w_ref), NT).astype(jnp.bfloat16)

    full = whole((rows, width))
    vec = whole((1, width))
    f = lambda s, d: jax.ShapeDtypeStruct(s, d)
    return call(
        body,
        grid=(steps,),
        in_specs=[
            full,
            pl.BlockSpec((rows, tf), lambda j: (0, j)),
            down_spec(down),
            up_spec(up, r_in),
            full,
            vec,
            rows_spec(up, r_in, block),
        ],
        out_specs=[
            full,
            pl.BlockSpec((rows, tf), lambda j: (0, j)),
            full,
            full,
            full,
            vec,
            pl.BlockSpec((1, tf), lambda j: (0, j)),
            vec,
            vec,
            vec,
        ],
        out_shape=[
            f((rows, width), jnp.bfloat16),
            f((rows, hidden), jnp.bfloat16),
            f((rows, width), jnp.float32),
            f((rows, width), jnp.bfloat16),
            f((rows, width), jnp.bfloat16),
            f((1, width), jnp.float32),
            f((1, hidden), jnp.float32),
            f((1, width), jnp.float32),
            f((1, width), jnp.float32),
            f((1, width), jnp.float32),
        ],
        scratch_shapes=[pltpu.VMEM((rows, width), jnp.float32)],
        name="feed_forward_back",
        cover=True,
    )(dy, gp, down, up, x1, gain, up)


def project_back(grads, weight, x, gain, dx1, extra, dtypes):
    rows, width = x.shape
    tm = rows // 2
    have = extra is not None
    count = len(grads)
    part = width // count

    def body(*refs):
        d_refs = refs[:count]
        w_ref, x_ref, g_ref, dx_ref = refs[count : count + 4]
        more = refs[count + 4 : -2 - len(dtypes)]
        out_refs = refs[-2 - len(dtypes) : -2]
        cg_ref, cs_ref = refs[-2:]
        da = None
        for kind in range(3):
            for i in range(count):
                at = kind * width + i * part
                term = dot(d_refs[i][kind], w_ref[:, at : at + part], NT)
                da = term if da is None else da + term
        xhat, inv = row_stats(x_ref[...].astype(jnp.float32))
        cg = jnp.sum(da * xhat, axis=0, keepdims=True)
        cs = jnp.sum(da, axis=0, keepdims=True)

        @pl.when(pl.program_id(0) == 0)
        def _():
            cg_ref[...] = cg
            cs_ref[...] = cs

        @pl.when(pl.program_id(0) > 0)
        def _():
            cg_ref[...] += cg
            cs_ref[...] += cs

        t = da * g_ref[...]
        m1 = jnp.mean(t, axis=-1, keepdims=True)
        m2 = jnp.mean(t * xhat, axis=-1, keepdims=True)
        dx = dx_ref[...] + inv * (t - m1 - xhat * m2)
        if have:
            dx = more[0][...].astype(jnp.float32) * more[1][...] + dx
        for ref in out_refs:
            ref[...] = dx.astype(ref.dtype)

    rowblk = pl.BlockSpec((tm, width), lambda i: (i, 0))
    vec_spec = whole((1, width))
    specs = [pl.BlockSpec((3, tm, part), lambda i: (0, i, 0))] * count
    specs += [whole((width, 3 * width)), rowblk, vec_spec, rowblk]
    args = list(grads) + [weight, x, gain, dx1]
    if have:
        specs += [rowblk, pl.BlockSpec((tm, 1), lambda i: (i, 0))]
        args += list(extra)
    return call(
        body,
        grid=(rows // tm,),
        in_specs=specs,
        out_specs=[rowblk] * len(dtypes) + [vec_spec, vec_spec],
        out_shape=[
            *[jax.ShapeDtypeStruct((rows, width), d) for d in dtypes],
            jax.ShapeDtypeStruct((1, width), jnp.float32),
            jax.ShapeDtypeStruct((1, width), jnp.float32),
        ],
        name="project_back",
        cover=True,
    )(*args)


def weight_grad(jobs, index, blocks, chunk, cover=False):
    ndp, nfs, r = blocks
    npos = ndp * nfs // 2
    rows = jobs[0][0][0].shape[0]
    widths = [rs[0].shape[-1] * (3 if rs[0].ndim == 3 else 1) for _, rs in jobs]
    starts = [sum(widths[:k]) for k in range(len(jobs))]
    counts = [len(ls) for ls, _ in jobs]
    steps = ndp * len(jobs)

    def body(i_ref, *refs):
        sent, kept, buf, sem = refs[-4:]
        i = pl.program_id(0)

        def copies(step, start):
            local = step % ndp
            for k in range(len(jobs)):
                for which, where in ((local < ndp // 2, sent), (local >= ndp // 2, kept)):

                    @pl.when((step // ndp == k) & which)
                    def _():
                        for f in range(nfs):
                            p = i_ref[ndp + local * nfs + f]
                            copy = pltpu.make_async_copy(
                                buf.at[step % 2, f, :, 0 : widths[k]],
                                where.at[p, :, starts[k] : starts[k] + widths[k]],
                                sem.at[step % 2, f],
                            )
                            copy.start() if start else copy.wait()

        @pl.when(i >= 2)
        def _():
            copies(i - 2, False)

        at_ref = 0
        for k in range(len(jobs)):
            a = refs[at_ref : at_ref + counts[k]]
            b = refs[at_ref + counts[k] : at_ref + 2 * counts[k]]
            at_ref += 2 * counts[k]

            @pl.when(i // ndp == k)
            def _():
                for at in range(0, widths[k], chunk):
                    part = b[0].shape[-1]
                    if len(b[0].shape) == 3:
                        take = lambda ref: ref[at // part, :, at % part : at % part + chunk]
                    else:
                        take = lambda ref: ref[:, at : at + chunk]
                    total = dot(a[0][...], take(b[0]), TN)
                    for x, y in zip(a[1:], b[1:]):
                        total += dot(x[...], take(y), TN)
                    total = total.astype(jnp.bfloat16).reshape(nfs, r, chunk)
                    buf[i % 2, :, :, at : at + chunk] = total

        copies(i, True)

        @pl.when(i == steps - 1)
        def _():
            copies(steps - 2, False)
            copies(steps - 1, False)

    def left_spec(k):
        step = lambda i: jnp.clip(i - k * ndp, 0, ndp - 1)
        return pl.BlockSpec((rows, nfs * r), lambda i, i_ref: (0, i_ref[step(i)]))

    anywhere = pl.BlockSpec(memory_space=pl.ANY)
    specs, args = [], []
    for k, (ls, rs) in enumerate(jobs):
        specs += [left_spec(k)] * len(ls) + [whole(rs[0].shape)] * len(rs)
        args += list(ls) + list(rs)
    return call(
        body,
        grid_spec=pltpu.PrefetchScalarGridSpec(
            num_scalar_prefetch=1,
            grid=(steps,),
            in_specs=specs,
            out_specs=[anywhere] * 2,
            scratch_shapes=[
                pltpu.VMEM((2, nfs, r, max(widths)), jnp.bfloat16),
                pltpu.SemaphoreType.DMA((2, nfs)),
            ],
        ),
        out_shape=[jax.ShapeDtypeStruct((npos, r, sum(widths)), jnp.bfloat16)] * 2,
        name="weight_grad",
        cover=cover,
    )(index, *args)


def weight_grad_half(lefts, rights, index, blocks):
    ndp, nfs, r = blocks
    steps = ndp // 2
    rows = lefts[0].shape[0]
    cols = rights[0].shape[1]
    count = len(lefts)

    def body(i_ref, *refs):
        a, b = refs[:count], refs[count : 2 * count]
        out, buf, sem = refs[2 * count :]
        i = pl.program_id(0)

        def copies(step, start):
            for f in range(nfs):
                where = out.at[i_ref[steps + step * nfs + f]]
                copy = pltpu.make_async_copy(buf.at[step, f], where, sem.at[step, f])
                copy.start() if start else copy.wait()

        total = dot(a[0][...], b[0][...], TN)
        for x, y in zip(a[1:], b[1:]):
            total += dot(x[...], y[...], TN)
        buf[i] = total.astype(jnp.bfloat16).reshape(nfs, r, cols)
        copies(i, True)

        @pl.when(i == steps - 1)
        def _():
            for step in range(steps):
                copies(step, False)

    return call(
        body,
        grid_spec=pltpu.PrefetchScalarGridSpec(
            num_scalar_prefetch=1,
            grid=(steps,),
            in_specs=[pl.BlockSpec((rows, nfs * r), lambda i, i_ref: (0, i_ref[i]))] * count
            + [whole((rows, cols))] * count,
            out_specs=pl.BlockSpec(memory_space=pl.ANY),
            scratch_shapes=[
                pltpu.VMEM((steps, nfs, r, cols), jnp.bfloat16),
                pltpu.SemaphoreType.DMA((steps, nfs)),
            ],
        ),
        out_shape=jax.ShapeDtypeStruct((steps * nfs, r, cols), jnp.bfloat16),
        name="weight_grad_half",
    )(index, *lefts, *rights)


def bits_of(ndp, nfs):
    core = nfs
    outer = [nfs << i for i in range(1, ndp.bit_length() - 1)]
    inner = [1 << i for i in range(nfs.bit_length() - 1)]
    return core, outer, inner


def stage_orders(ndp, nfs):
    core, outer, inner = bits_of(ndp, nfs)
    first, second = outer[0], inner[0]
    tail = outer[1:] + inner[1:]
    return core, ([first, second] + tail, [second, first] + tail)


def shard_table(ndp, nfs):
    n = ndp * nfs
    core, orders = stage_orders(ndp, nfs)
    table = np.zeros((n, n), np.int32)
    for me in range(n):
        for p in range(n):
            rel = core if p >= n // 2 else 0
            owner = 1 if (me ^ rel) & core else 0
            for i, mask in enumerate(orders[owner]):
                if p & (n >> (i + 2)):
                    rel ^= mask
            table[me, p] = me ^ rel
    return table


def stage_perms(ndp, nfs):
    n = ndp * nfs
    core, orders = stage_orders(ndp, nfs)
    perms = [[(i, i ^ core) for i in range(n)]]
    for a, b in zip(*orders):
        perms.append([(i, i ^ (b if i & core else a)) for i in range(n)])
    return perms


AXES = ("dp", "fsdp")


def send(x, perm):
    return lax.ppermute(x, AXES, perm)


class Line:
    def __init__(self):
        self.last = ()

    def after(self, *arrays):
        return lax.optimization_barrier(self.last + arrays)[len(self.last) :]

    def mark(self, *arrays):
        self.last = arrays


class Mover:
    def __init__(self, pieces, table, shape, into=None):
        self.pieces, self.table, self.into = pieces, table, into
        self.args = [p[0] for p in pieces] + ([] if into is None else [into])
        self.specs = [pl.BlockSpec(memory_space=pl.ANY)] * len(self.args)
        self.out_spec = pl.BlockSpec(memory_space=pl.ANY)
        self.out_shape = jax.ShapeDtypeStruct(shape, jnp.bfloat16)
        counts = [p[0].shape[0] for p in pieces]
        self.scratch = [
            pltpu.VMEM((k, p[3], shape[-1]), jnp.bfloat16) for k, p in zip(counts, pieces)
        ] + [pltpu.SemaphoreType.DMA((sum(counts),))] * 2

    def copies(self, t_ref, ins, out, scratch):
        loads, stores = [], []
        in_sem, out_sem = scratch[-2:]
        for ref, buf, (array, first, rows_at, rows) in zip(ins, scratch, self.pieces):
            for k in range(array.shape[0]):
                i = len(loads)
                source = ref.at[k, :, 0 : buf.shape[-1]]
                loads.append(pltpu.make_async_copy(source, buf.at[k], in_sem.at[i]))
                target = out.at[t_ref[first + k], rows_at : rows_at + rows]
                stores.append(pltpu.make_async_copy(buf.at[k], target, out_sem.at[i]))
        return loads, stores

    def ride(self, step, last, *refs):
        loads, stores = self.copies(*refs)

        @pl.when(step == 0)
        def _():
            for c in loads:
                c.start()

        @pl.when(step == 1)
        def _():
            for a, b in zip(loads, stores):
                a.wait()
                b.start()

        @pl.when(step == last)
        def _():
            for c in stores:
                c.wait()


def place_shards(mover, cover=False):
    count = len(mover.args)

    def body(t_ref, *refs):
        loads, stores = mover.copies(t_ref, refs, refs[count], refs[count + 1 :])
        for c in loads:
            c.start()
        for a, b in zip(loads, stores):
            a.wait()
            b.start()
        for b in stores:
            b.wait()

    return call(
        body,
        out_shape=mover.out_shape,
        grid_spec=pltpu.PrefetchScalarGridSpec(
            num_scalar_prefetch=1,
            in_specs=mover.specs,
            out_specs=mover.out_spec,
            scratch_shapes=mover.scratch,
        ),
        input_output_aliases={} if mover.into is None else {count: 0},
        name="place_shards",
        cover=cover,
    )(mover.table, *mover.args)


def riding(body, mover, grid, in_specs, out_specs, out_shape, name, args):
    if mover is None:
        return call(
            body, grid=grid, in_specs=in_specs, out_specs=out_specs, out_shape=out_shape, name=name
        )(*args)
    ins, outs, extra = len(in_specs), len(out_specs), len(mover.args)

    def both(t_ref, *refs):
        own = refs[:ins] + refs[ins + extra : ins + extra + outs]
        moved = refs[ins : ins + extra], refs[ins + extra + outs], refs[ins + extra + outs + 1 :]
        mover.ride(pl.program_id(0), grid[0] - 1, t_ref, *moved)
        body(*own)

    return call(
        both,
        grid_spec=pltpu.PrefetchScalarGridSpec(
            num_scalar_prefetch=1,
            grid=grid,
            in_specs=in_specs + mover.specs,
            out_specs=out_specs + [mover.out_spec],
            scratch_shapes=mover.scratch,
        ),
        out_shape=out_shape + [mover.out_shape],
        input_output_aliases={} if mover.into is None else {ins + extra: outs},
        name=name,
    )(mover.table, *args, *mover.args)


def pack_shard(matrices, vectors):
    rows = matrices[0].shape[0]
    widths = [m.shape[1] for m in matrices]
    lanes = 128 * -(-len(vectors) // 8)

    def body(*refs):
        out, scr = refs[-2:]
        at = 0
        for ref, width in zip(refs, widths):
            out[:, at : at + width] = ref[...]
            at += width
        scr[...] = jnp.zeros_like(scr)
        for r, ref in enumerate(refs[len(widths) : -2]):
            k, col = ref.shape[1], 128 * (r // 8)
            scr[r % 8 : r % 8 + 1, col : col + k] = ref[...].astype(jnp.float32)
        out[:, at:] = scr[...].astype(jnp.bfloat16)

    vectors = [v.reshape(1, -1) for v in vectors]
    cols = sum(widths) + lanes
    return call(
        body,
        grid=(1,),
        in_specs=[whole(a.shape) for a in (*matrices, *vectors)],
        out_specs=whole((rows, cols)),
        out_shape=jax.ShapeDtypeStruct((rows, cols), jnp.bfloat16),
        scratch_shapes=[pltpu.VMEM((rows, lanes), jnp.float32)],
        name="pack_shard",
    )(*matrices, *vectors)


def unpack_vectors(pieces, at, inverse_row, sizes, layout):
    per_piece = pieces[0].shape[0]
    n = per_piece * len(pieces)
    lanes = pieces[0].shape[2] - at

    def body(i_ref, *refs):
        ins, outs, scr = refs[: len(pieces)], refs[len(pieces) : -1], refs[-1]
        for i, ref in enumerate(ins):
            scr[i * per_piece : (i + 1) * per_piece] = ref[...].astype(jnp.float32)
        for rows, out in zip(layout, outs):
            col = 0
            for r in rows:
                k = sizes[0] if r is None else sizes[r]
                per = 128 // k if k < 128 else 1
                for d in range(0, n, per):
                    if r is None:
                        value = jnp.zeros((1, per * k), jnp.float32)
                    else:
                        row, lane = r % 8, 128 * (r // 8)
                        value = jnp.concatenate(
                            [
                                scr[i_ref[d + e], row : row + 1, lane : lane + k]
                                for e in range(per)
                            ],
                            axis=1,
                        )
                    out[0:1, col + d * k : col + (d + per) * k] = value
                col += n * k

    widths = [sum(n * (sizes[0] if r is None else sizes[r]) for r in rows) for rows in layout]
    return call(
        body,
        grid_spec=pltpu.PrefetchScalarGridSpec(
            num_scalar_prefetch=1,
            grid=(1,),
            in_specs=[pl.BlockSpec((per_piece, 8, lanes), lambda i, i_ref: (0, 0, at // lanes))]
            * len(pieces),
            out_specs=[pl.BlockSpec((1, w), lambda i, i_ref: (0, 0)) for w in widths],
            scratch_shapes=[pltpu.VMEM((n, 8, lanes), jnp.float32)],
        ),
        out_shape=[jax.ShapeDtypeStruct((1, w), jnp.float32) for w in widths],
        name="unpack_vectors",
    )(inverse_row, *pieces)


def pack_sums(parts, inverse_row, n, rows):
    flat_parts = [a for pieces in parts for group in pieces for a in group]

    def body(i_ref, *refs):
        out = refs[-1]
        out[...] = jnp.zeros_like(out)
        at = 0
        for r, pieces in enumerate(parts):
            per = n // len(pieces)
            for piece, group in enumerate(pieces):
                total = refs[at][...]
                for k in range(1, len(group)):
                    total += refs[at + k][...]
                at += len(group)
                k = total.shape[1] // per
                for d in range(per):
                    out[i_ref[piece * per + d], r : r + 1, 0:k] = total[:, d * k : (d + 1) * k]

    return call(
        body,
        grid_spec=pltpu.PrefetchScalarGridSpec(
            num_scalar_prefetch=1,
            grid=(1,),
            in_specs=[whole(a.shape) for a in flat_parts],
            out_specs=whole((n, rows, 128)),
        ),
        out_shape=jax.ShapeDtypeStruct((n, rows, 128), jnp.float32),
        name="pack_sums",
    )(inverse_row, *flat_parts)


class Reduction:
    def __init__(self, perms, kept, sent, stage):
        self.perms, self.stage = perms, stage
        self.kept, self.got = kept, send(sent, perms[stage])
        self.done = None

    def step(self, line, wide=jnp.bfloat16):
        kept, got = line.after(self.kept, self.got)
        add = lambda part: kept[part].astype(jnp.float32) + got[part].astype(jnp.float32)
        self.stage += 1
        if self.stage == len(self.perms):
            self.done = add(slice(None))[0]
            line.mark(self.done)
            return
        half = kept.shape[0] // 2
        sent = add(slice(half, None)).astype(wide)
        self.got = send(sent, self.perms[self.stage])
        self.kept = add(slice(0, half)).astype(wide)
        line.mark(sent, self.kept)


def per_device(ndp, nfs,
    tokens,
    ln1_gain,
    ln1_bias,
    w_qkv,
    bias_q,
    bias_v,
    w_out,
    bias_out,
    ln2_gain,
    ln2_bias,
    w_up,
    bias_up,
    w_down,
    bias_down,
    cot_first,
    cot_second,
    valid,
):
    n = ndp * nfs
    perms = stage_perms(ndp, nfs)
    gather_perms = perms[:0:-1]
    core_perm = perms[0]
    stages = len(gather_perms)
    table = shard_table(ndp, nfs)
    me = lax.axis_index("dp") * nfs + lax.axis_index("fsdp")
    both = np.concatenate([table, np.argsort(table, axis=1).astype(np.int32)], axis=1)
    both = lax.dynamic_slice(jnp.asarray(both), (me, 0), (1, 2 * n))[0]
    row, inverse_row = both[:n], both[n:]
    rows_in, width = tokens.shape[1:]
    r_in, r_ff = w_up.shape[0], w_down.shape[0]
    hidden = w_up.shape[1]

    vectors = (ln1_gain, ln1_bias, bias_q, bias_v, bias_out, ln2_gain, ln2_bias, bias_down, bias_up)
    sizes = [v.shape[0] for v in vectors]
    line = Line()
    qkv_cols = w_qkv.shape[1]
    ahead = pack_shard([w_qkv], vectors)
    split = w_up.reshape(r_in, hidden // width, width).swapaxes(0, 1).reshape(r_ff, width)
    split = jnp.concatenate([split, w_out], axis=0)
    out_at = hidden // width

    class Gather:
        def __init__(self, shard):
            self.perms, self.rows = gather_perms, shard.shape[0]
            self.held, self.stage = shard[None], 0
            (self.held,) = line.after(self.held)
            self.got = send(self.held, self.perms[0])

        def step(self):
            mine, theirs = line.after(self.held, self.got)
            self.held = jnp.concatenate([mine, theirs], axis=0)
            line.mark(self.held)
            self.stage += 1
            self.got = send(self.held, self.perms[self.stage])
            if self.stage == stages - 1:
                self.early = send(self.held, core_perm)

        def finish(self):
            (self.got,) = line.after(self.got)
            self.late = send(self.got, core_perm)

        def pieces(self, which):
            quarter = n // 4
            pair = (self.got, self.late) if which else (self.held, self.early)
            pair = line.after(*pair)
            firsts = which * quarter, half + which * quarter
            return [(a, f, 0, self.rows) for a, f in zip(pair, firsts)]

    def place(pieces, shape, into=None, cover=False):
        out = place_shards(Mover(pieces, row, shape, into), cover)
        line.mark(out)
        return out

    half = n // 2
    ff_shape, first_shape = (n, r_ff, width), (n, r_in, qkv_cols)
    mid_shape = (n, r_ff + r_in, width)
    chain_a = Gather(ahead)
    for k in range(1, stages - 2):
        chain_a.step()
    chain_b = Gather(split)
    chain_a.step()
    keep_mask = valid[0].astype(jnp.float32)[:, None]
    grad_second = masked(*line.after(cot_second[0]), keep_mask)
    line.mark(grad_second)
    for k in range(1, stages - 2):
        chain_b.step()
    chain_a.step()
    chain_b.step()
    chain_c = Gather(w_down)
    chain_a.finish()
    first = place(chain_a.pieces(0), first_shape)
    first = place(chain_a.pieces(1), first_shape, first)
    for k in range(1, stages - 2):
        chain_c.step()
    chain_b.step()
    w = {"qkv": first.reshape(n * r_in, qkv_cols)}
    g1, s1, bqkv, bo, g2, s2, bd, bu = unpack_vectors(
        (chain_a.held, chain_a.got, chain_a.early, chain_a.late),
        qkv_cols,
        inverse_row,
        sizes,
        [[0], [1], [2, None, 3], [4], [5], [6], [7], [8]],
    )
    def attend(qkv):
        chain_c.step()
        o, logs = attention(*line.after(qkv))
        line.mark(o)
        up = place(chain_b.pieces(0), mid_shape)
        chain_b.finish()
        chain_c.step()
        w["up"] = place(chain_b.pieces(1), mid_shape, up)
        return o, logs

    def feed(a2, x1):
        mover = Mover(chain_c.pieces(0), row, ff_shape)
        g, gp, down = feed_forward_in(*line.after(a2), w["up"], r_in, bu, mover)
        line.mark(g)
        chain_c.finish()
        w["down"] = place(chain_c.pieces(1), ff_shape, down)
        y = feed_forward_out(line.after(g)[0], w["down"], bd, x1)
        return g, gp, y

    def forward(x, gathering=False):
        a1, qkv = norm_project(
            *line.after(x), g1, s1, w["qkv"], bqkv, qkv_cols // 2, qkv_cols
        )
        line.mark(a1)
        o, logs = attend(qkv) if gathering else attention(*line.after(qkv))
        if not gathering:
            line.mark(o)
        x1, a2 = project_norm(*line.after(o), w["up"], r_in, out_at, bo, x, g2, s2)
        line.mark(a2)
        if gathering:
            g, gp, y = feed(a2, x1)
        else:
            g, gp, y = feed_forward(*line.after(a2), w["up"], w["down"], r_in, bu, bd, x1)
        line.mark(y)
        return y, (x, a1, qkv, logs, o, x1, a2, g, gp)

    first, saved_first = forward(tokens[0], True)
    second, saved_second = forward(first)

    pairs = width // (2 * HEAD_DIM)
    parts = 2

    def ff_back(dy, saved):
        x, a1, qkv, logs, o, x1, a2, g, gp = saved
        outs = feed_forward_back(
            *line.after(dy), gp, w["up"], w["down"], r_in, x1, g2, out_at
        )
        line.mark(outs[0])
        return outs

    def heads_back(saved, d_o, i, cover=True):
        outs = attention_back(
            saved[2], saved[3], *line.after(d_o), i * pairs // parts, pairs // parts, cover
        )
        line.mark(outs[0])
        return outs

    def qkv_back(heads, saved, dx1, extra, dtypes):
        outs = project_back(
            [line.after(h[0])[0] for h in heads], w["qkv"], saved[0], g1, dx1, extra, dtypes
        )
        line.mark(outs[0])
        return outs

    dm2, du2, dx2, da2, do2, cdm2, cdu2, cda2, cg22, cs22 = ff_back(grad_second, saved_second)
    heads2 = [heads_back(saved_second, do2, i) for i in range(parts)]
    grad_first, dm1, cg12, cs12 = qkv_back(
        heads2, saved_second, dx2, (cot_first[0], keep_mask), (jnp.float32, jnp.bfloat16)
    )

    core = (me // nfs) % 2
    evens = 2 * jnp.arange(ndp // 2, dtype=jnp.int32)
    lefts_at = jnp.concatenate([evens + (1 - core), evens + core])
    shards_at = lefts_at[:, None] * nfs + jnp.arange(nfs, dtype=jnp.int32)
    index = jnp.concatenate([lefts_at, inverse_row[shards_at.reshape(-1)] % half])
    index = index.astype(jnp.int32)

    def grads(r, *jobs, cover=False):
        jobs = [(line.after(*ls), rs) for ls, rs in jobs]
        sent, kept = weight_grad(jobs, index, (ndp, nfs, r), 512, cover)
        line.mark(sent)
        return Reduction(perms, kept, sent, 0)

    def grads_split(r, lefts, rights):
        lefts = line.after(*lefts)
        parts_at = index[:ndp].reshape(2, -1), index[ndp:].reshape(2, -1)
        made = []
        for k in range(2):
            at = jnp.concatenate([parts_at[0][k], parts_at[1][k]])
            made.append(weight_grad_half(line.after(*lefts), rights, at, (ndp, nfs, r)))
            line.mark(made[k])
        return Reduction(perms, made[1], made[0], 0)

    sg = list(zip(saved_first, saved_second))
    red_down = grads_split(r_ff, sg[7], (dm1, dm2))
    _, du1, dx1, da1, do1, cdm1, cdu1, cda1, cg21, cs21 = ff_back(grad_first, saved_first)
    red_down.step(line)
    red_up = grads(r_in, (sg[6], (du1, du2)))
    red_down.step(line)
    heads1 = [heads_back(saved_first, do1, 0)]
    rights = lambda i: (heads1[i][0], heads2[i][0])
    red_down.step(line)
    red_up.step(line)
    red_one = grads(r_in, (sg[4], (da1, da2)), (sg[1], rights(0)))
    heads1.append(heads_back(saved_first, do1, 1, False))
    red_up.step(line)
    red_down.step(line)
    red_two = grads(r_in, (sg[1], rights(1)), cover=True)
    red_one.step(line)
    red_up.step(line)
    red_two.step(line)
    grad_inputs, cg11, cs11 = qkv_back(heads1, saved_first, dx1, None, (jnp.bfloat16,))
    halves = lambda k: [[h[i][k] for h in (heads1, heads2)] for i in range(parts)]
    cg11 = line.after(cg11)[0]
    sums = pack_sums(
        [
            [[cg11, cg12]],
            [[cs11, cs12]],
            halves(1),
            halves(2),
            [[cda1, cda2]],
            [[cg21, cg22]],
            [[cs21, cs22]],
            [[cdm1, cdm2]],
            [[cdu1, cdu2]],
        ],
        inverse_row,
        n,
        len(vectors),
    )
    line.mark(sums)
    red_small = Reduction(perms, sums[:half], sums[half:], 0)
    red_one.step(line)
    red_up.step(line)
    todo = [red_two, red_one, red_up, red_down]
    while todo:
        for red in todo:
            red.step(line)
            if red_small.done is None and red not in (red_up, red_down):
                red_small.step(line, jnp.float32)
        todo = [red for red in todo if red.done is None]
    outs = [red_small.done[i, : sizes[i]] for i in range(len(vectors))]
    o_g1, o_s1, o_bq, o_bv, o_bo, o_g2, o_s2, o_bd, o_bu = outs
    one = red_one.done
    d_out = one[:, :width]
    third = width // parts
    blocks = []
    for kind in range(3):
        blocks.append(one[:, width + kind * third : width + (kind + 1) * third])
        blocks.append(red_two.done[:, kind * third : (kind + 1) * third])
    d_qkv = jnp.concatenate(blocks, axis=1)
    return (
        first[None],
        second[None],
        grad_inputs[None],
        o_g1,
        o_s1,
        d_qkv,
        o_bq,
        o_bv,
        d_out,
        o_bo,
        o_g2,
        o_s2,
        red_up.done,
        o_bu,
        red_down.done,
        o_bd,
    )


def solution(mesh):
    ndp, nfs = mesh.shape["dp"], mesh.shape["fsdp"]
    return jax.shard_map(
        partial(per_device, ndp, nfs),
        mesh=mesh,
        in_specs=(
            P(("dp", "fsdp"), None, None),
            P(("dp", "fsdp")),
            P(("dp", "fsdp")),
            P(("dp", "fsdp"), None),
            P(("dp", "fsdp")),
            P(("dp", "fsdp")),
            P(("dp", "fsdp"), None),
            P(("dp", "fsdp")),
            P(("dp", "fsdp")),
            P(("dp", "fsdp")),
            P(("dp", "fsdp"), None),
            P(("dp", "fsdp")),
            P(("dp", "fsdp"), None),
            P(("dp", "fsdp")),
            P(("dp", "fsdp"), None, None),
            P(("dp", "fsdp"), None, None),
            P(("dp", "fsdp"), None),
        ),
        out_specs=(
            P(("dp", "fsdp"), None, None),
            P(("dp", "fsdp"), None, None),
            P(("dp", "fsdp"), None, None),
            P(("dp", "fsdp")),
            P(("dp", "fsdp")),
            P(("dp", "fsdp"), None),
            P(("dp", "fsdp")),
            P(("dp", "fsdp")),
            P(("dp", "fsdp"), None),
            P(("dp", "fsdp")),
            P(("dp", "fsdp")),
            P(("dp", "fsdp")),
            P(("dp", "fsdp"), None),
            P(("dp", "fsdp")),
            P(("dp", "fsdp"), None),
            P(("dp", "fsdp")),
        ),
        check_vma=False,
    )
```
